512 devices in a mesh: shot: 128 (over y, z, x_hi), freq: 4 (over x_lo, core).
Axes of the slice: x: 4 (x_hi: 2, x_lo: 2; x = x_hi * 2 + x_lo), y: 8, z: 8, core: 2. Of those that a mesh axis runs over, the one named last changes fastest.
Arguments:
- blended: bfloat16 [2, 512, 512, 256], P(None, 'shot', 'freq'), may hold values from -6 to 6
- estimate: bfloat16 [2, 512, 512, 256], P(None, 'shot', 'freq'), may hold values from -5 to 5
- partner: int32 [512], P('shot'), may hold values from 0 to 511, as said below
- delays: int32 [512], replicated, may hold values from 0 to 256
- levels: int32 [128], replicated, may hold values from 1 to 4
Outputs:
- deblended: bfloat16 [2, 512, 512, 256], P(None, 'shot', 'freq')
The draws below stay inside these ranges and needn't reach their ends.
Inputs may be any that keep to these rules, and one draw needn't show every extreme that they name: Shot s of block b = s // 4 is paired with a shot of block (b + 64) modulo 512 / 4; the pairing is mutual, partner[partner[s]] = s.
All inputs are finite; a program needn't handle non-finite values.
Results may differ from the reference program's by a relative error of at most 0.005.
Values may be sent and summed in bfloat16 or wider, within the bound.
No kernel may reach another device: no remote copies, remote signals or barrier semaphores. Data moves between devices by JAX's collectives and lax.ppermute only.
A program may use at most 64 MiB of HBM per device.

```python
import math
import jax
import jax.numpy as jnp
from jax import lax

NR = 256
NF = 512
NT = 1024
SHOT_DEV = 4
SHOTS = 512
WINDOWS = 128
PASSES = 2


def draw_partner(key, part):
    blocks = SHOTS // SHOT_DEV
    half_blocks = blocks // 2
    pair_keys = jax.random.split(jax.random.fold_in(key, 17), half_blocks)
    shuffles = jax.vmap(lambda one_key: jax.random.permutation(one_key, SHOT_DEV))(pair_keys)
    starts = jnp.arange(half_blocks, dtype=jnp.int32)[:, None] * SHOT_DEV
    lower_pairs = starts + half_blocks * SHOT_DEV + shuffles
    inverse = jnp.argsort(shuffles, axis=1)
    upper_pairs = starts + inverse
    return jnp.concatenate([lower_pairs.reshape(-1), upper_pairs.reshape(-1)]).astype(jnp.int32)


def set_ends(values, own_key, low, largest):
    dims = values.shape
    place = [jax.random.randint(jax.random.fold_in(own_key, axis), (), 0, dims[axis]) for axis in range(len(dims))]
    values = values.at[tuple(place)].set(low)
    longest = dims.index(max(dims))
    place[longest] = (place[longest] + 1) % dims[longest]
    return values.at[tuple(place)].set(largest)


def level_of(key, extent, cuts, smallest, high):
    loudness = 1.0
    for position, parts in cuts:
        draws = jax.random.uniform(jax.random.fold_in(jax.random.fold_in(key, 6), position), (parts,), jnp.float32, smallest / len(cuts), high / len(cuts))
        loudness = loudness * jnp.repeat(jnp.exp(draws), extent[position] // parts).reshape((-1,) + (1,) * (len(extent) - 1 - position))
    return loudness


def scatter_about(stream_key, dims, width, reach, cuts=(), kind=jnp.bfloat16):
    gain = level_of(stream_key, dims, cuts, -0.22, 0.18) if cuts else 1.0
    entries = jax.random.normal(stream_key, dims, jnp.float32) * width * gain
    return jnp.minimum(jnp.maximum(entries, -reach), reach).astype(kind)


def setup_inputs(seed: int = 0) -> dict:
    keys = jax.random.split(jax.random.key(seed), 6)
    blended = scatter_about(keys[0], (2, SHOTS, NF, NR), 1.0, 6.0, ((1, 128), (2, 4)))
    estimate = scatter_about(keys[1], (2, SHOTS, NF, NR), 0.7, 5.0, ((1, 128), (2, 4)))
    partner = draw_partner(jax.random.fold_in(keys[5], 71), 0)
    delays = set_ends(jax.random.randint(keys[3], (SHOTS,), 0, NT // 4 + 1), jax.random.fold_in(keys[3], 1), 0, (NT // 4 + 1) - 1).astype(jnp.int32)
    levels = set_ends(jax.random.randint(keys[4], (WINDOWS,), 1, 5), jax.random.fold_in(keys[4], 1), 1, 4).astype(jnp.int32)
    return dict(blended=blended, estimate=estimate, partner=partner, delays=delays, levels=levels)


relaxation = 0.5
level_scale = 0.25

def tables(length):
    indices = jnp.arange(length, dtype=jnp.int32)
    products = jnp.mod(indices[:, None] * indices[None, :], length)
    angles = 2.0 * math.pi / length * products.astype(jnp.float32)
    return (jnp.cos(angles), jnp.sin(angles))

def spectrum(real_part, imag_part, direction_sign, shot_cos, shot_sin, recv_cos, recv_sin):
    highest = lax.Precision.HIGHEST

    def receivers(values, table):
        return jnp.einsum('...n,nk->...k', values, table, precision=highest)

    def shots(values, table):
        return jnp.einsum('tk,...tfn->...kfn', table, values, precision=highest)
    first_real = receivers(real_part, recv_cos) + direction_sign * receivers(imag_part, recv_sin)
    first_imag = receivers(imag_part, recv_cos) - direction_sign * receivers(real_part, recv_sin)
    out_real = shots(first_real, shot_cos) + direction_sign * shots(first_imag, shot_sin)
    out_imag = shots(first_imag, shot_cos) - direction_sign * shots(first_real, shot_sin)
    scale = 1.0 / math.sqrt(shot_cos.shape[0] * recv_cos.shape[0])
    return (out_real * scale, out_imag * scale)

def shrink(real_part, imag_part, threshold):
    modulus = jnp.sqrt(real_part * real_part + imag_part * imag_part)
    factor = jnp.maximum(modulus - threshold, 0.0) / jnp.maximum(modulus, threshold)
    return (real_part * factor, imag_part * factor)

def one_pass(current, blended, partner, delays, levels):
    block = SHOT_DEV
    span = 2 * block
    current_f = current.astype(jnp.float32)
    partner_recs = current_f[:, partner]
    offsets = delays[partner] - delays
    frequency = jnp.arange(NF, dtype=jnp.int32)
    phase_index = jnp.mod(frequency[None, :] * offsets[:, None], NT)
    angles = 2.0 * math.pi / NT * phase_index.astype(jnp.float32)
    phase_cos = jnp.cos(angles)[:, :, None]
    phase_sin = jnp.sin(angles)[:, :, None]
    shifted_real = partner_recs[0] * phase_cos + partner_recs[1] * phase_sin
    shifted_imag = partner_recs[1] * phase_cos - partner_recs[0] * phase_sin
    shifted = jnp.stack([shifted_real, shifted_imag])
    updated = current_f + relaxation * (blended.astype(jnp.float32) - current_f - shifted)
    padded = jnp.concatenate([updated, jnp.zeros((2, block, NF, NR), jnp.float32)], axis=1)
    steps_t = jnp.arange(span, dtype=jnp.float32)
    taper = jnp.sin(math.pi * (steps_t + 0.5) / span) ** 2
    shot_cos, shot_sin = tables(span)
    recv_cos, recv_sin = tables(NR)

    def window(window_index):
        segment = lax.dynamic_slice_in_dim(padded, window_index * block, span, axis=1)
        segment = segment * taper[None, :, None, None]
        coef_real, coef_imag = spectrum(segment[0], segment[1], 1.0, shot_cos, shot_sin, recv_cos, recv_sin)
        modulus = jnp.sqrt(coef_real * coef_real + coef_imag * coef_imag)
        mean_mod = jnp.sum(modulus) / (span * NF * NR)
        threshold = level_scale * levels[window_index].astype(jnp.float32) * mean_mod
        kept_real, kept_imag = shrink(coef_real, coef_imag, threshold)
        back_real, back_imag = spectrum(kept_real, kept_imag, -1.0, shot_cos, shot_sin, recv_cos, recv_sin)
        result = jnp.stack([back_real, back_imag])
        return (result[:, :block], result[:, block:])
    firsts, seconds = lax.map(window, jnp.arange(WINDOWS, dtype=jnp.int32))
    firsts = jnp.transpose(firsts, (1, 0, 2, 3, 4)).reshape(2, SHOTS, NF, NR)
    seconds = jnp.transpose(seconds, (1, 0, 2, 3, 4)).reshape(2, SHOTS, NF, NR)
    seconds = jnp.concatenate([jnp.zeros((2, block, NF, NR), jnp.float32), seconds[:, :SHOTS - block]], axis=1)
    return (firsts + seconds).astype(jnp.bfloat16)

def reference(blended, estimate, partner, delays, levels):
    current = estimate
    for pass_index in range(PASSES):
        current = one_pass(current, blended, partner, delays, levels)
    return current
```

```python
import functools
import math

import jax
import jax.numpy as jnp
import numpy as np
from jax import lax
from jax.experimental import pallas as pl
from jax.experimental.pallas import tpu as pltpu
from jax.sharding import Mesh
from jax.sharding import PartitionSpec as P

NT = 1024
PASSES = 2
SHOTS_DEV = 4
ROLES = 4
RELAX = 0.5
LEVEL_SCALE = 0.25
TINY = 1e-37
ROOT8 = 1.0 / math.sqrt(8.0)
HALF_ROOT = math.sqrt(0.5)
TAPER = [math.sin(math.pi * (t + 0.5) / 8) ** 2 * ROOT8 for t in range(8)]
GROUP = ("yh", "h")
SUM_GROUP = ("yh", "h", "f")

f32 = jnp.float32
bf16 = jnp.bfloat16
VMEM = pl.BlockSpec(memory_space=pltpu.VMEM)
SMEM = pl.BlockSpec(memory_space=pltpu.SMEM)


def receiver_tables(length, sign):
    k = np.arange(length)
    angle = 2.0 * np.pi / length * ((k[:, None] * k[None, :]) % length)
    c, s = np.cos(angle) / math.sqrt(length), sign * np.sin(angle) / math.sqrt(length)
    full = np.block([[c, -s], [s, c]]).astype(np.float32)
    high = full.astype(jnp.bfloat16)
    low = (full - high.astype(np.float32)).astype(jnp.bfloat16)
    return np.stack([high, low])


def add(a, b):
    return (a[0] + b[0], a[1] + b[1])


def sub(a, b):
    return (a[0] - b[0], a[1] - b[1])


def turn(a, sign):
    return (a[1], -a[0]) if sign > 0 else (-a[1], a[0])


def twist(a, power, sign):
    if power == 0:
        return a
    if power == 2:
        return turn(a, sign)
    re, im = a
    if sign > 0:
        one = ((re + im) * HALF_ROOT, (im - re) * HALF_ROOT)
    else:
        one = ((re - im) * HALF_ROOT, (im + re) * HALF_ROOT)
    return one if power == 1 else turn(one, sign)


def dft4(a, b, c, d, sign):
    s0, s1, s2, s3 = add(a, c), sub(a, c), add(b, d), turn(sub(b, d), sign)
    return [add(s0, s2), add(s1, s3), sub(s0, s2), sub(s1, s3)]


def dft8(x, sign, part="both"):
    even = dft4(x[0], x[2], x[4], x[6], sign)
    odd = dft4(x[1], x[3], x[5], x[7], sign)
    odd = [twist(odd[k], k, sign) for k in range(4)]
    first = [add(even[k], odd[k]) for k in range(4)] if part != "second" else []
    second = [sub(even[k], odd[k]) for k in range(4)] if part != "first" else []
    return first + second


def windowed(first, second):
    both = first + second
    return [(both[t][0] * TAPER[t], both[t][1] * TAPER[t]) for t in range(8)]


def load(ref, ab, block, rows, half, q):
    lo, hi = half * 128, q + half * 128
    out = []
    for t in range(SHOTS_DEV):
        at = (ab, block, t) if block is not None else (ab, t)
        out.append((ref[(*at, rows, slice(lo, lo + 128))], ref[(*at, rows, slice(hi, hi + 128))]))
    return out


def place(n):
    g = lax.axis_index("g")
    first, last = g == 0, g == n - 1
    return g, first, last


def fetch_halo(n, up_ref, down_ref, halo_ref):
    _, first, last = place(n)
    for ab in range(2):
        source = jnp.where(first, 0, ab)
        halo_ref[0, ab] = up_ref[source].astype(f32)
        source = jnp.where(last, 1, ab)
        scale = jnp.where(last, 0.0, 1.0) if ab == 1 else 1.0
        halo_ref[1, ab] = down_ref[source].astype(f32) * scale


def spectra(z_ref, halo_ref, ab, rows, half, q):
    prev = load(halo_ref, 0, ab, rows, half, q)
    even = load(z_ref, ab, 0, rows, half, q)
    odd = load(z_ref, ab, 1, rows, half, q)
    after = load(halo_ref, 1, ab, rows, half, q)
    for pair in ((prev, even), (even, odd), (odd, after)):
        yield dft8(windowed(*pair), 1)


def pack_kernel(nf, e_ref, b_ref, partner_ref, delays_ref, out_ref):
    q = e_ref.shape[3]
    fl = e_ref.shape[2] // ROLES
    block = (lax.axis_index("yh") * lax.axis_size("g") + lax.axis_index("g")) * 2 + lax.axis_index("h")
    row = lax.broadcasted_iota(jnp.int32, (16, 2 * q), 0)
    meta = jnp.zeros((16, 2 * q), f32)
    for t in range(SHOTS_DEV):
        other = partner_ref[t]
        offset = (delays_ref[other] - delays_ref[block * SHOTS_DEV + t]) & (NT - 1)
        for i, value in enumerate((other & (SHOTS_DEV - 1), offset >> 5, offset & 31)):
            meta = jnp.where(row == 3 * t + i, value.astype(f32), meta)
    for role in range(ROLES):
        rows = slice(role * fl, (role + 1) * fl)
        for k, ref in enumerate((e_ref, b_ref)):
            for t in range(SHOTS_DEV):
                out_ref[role, k * SHOTS_DEV + t, :, :q] = ref[0, t, rows, :]
                out_ref[role, k * SHOTS_DEV + t, :, q:] = ref[1, t, rows, :]
        out_ref[role, 2 * SHOTS_DEV, :16, :] = meta.astype(bf16)
        out_ref[role, 2 * SHOTS_DEV, 16:, :] = jnp.zeros((fl - 16, 2 * q), bf16)


def phases(index):
    quadrant = (index + 128) >> 8
    x = (index - (quadrant << 8)).astype(f32) * (2.0 * math.pi / NT)
    x2 = x * x
    s = x * (1 + x2 * (-1 / 6 + x2 * (1 / 120 + x2 * (-1 / 5040 + x2 * (1 / 362880)))))
    c = 1 + x2 * (-1 / 2 + x2 * (1 / 24 + x2 * (-1 / 720 + x2 * (1 / 40320))))
    swap = (quadrant & 1) == 1
    cos, sin = jnp.where(swap, s, c), jnp.where(swap, c, s)
    cos = jnp.where(((quadrant + 1) & 2) == 2, -cos, cos)
    sin = jnp.where((quadrant & 2) == 2, -sin, sin)
    return cos, sin


def relax(e_ref, bh_ref, meta_ref, phase_ref, z_ref, down_ref, up_ref):
    fl, q = e_ref.shape[3], e_ref.shape[4] // 2

    def body(i, carry):
        rows = pl.ds(pl.multiple_of(i * 16, 16), 16)
        for ab in range(2):
            for p in range(2):
                for t in range(SHOTS_DEV):
                    slot = jnp.broadcast_to(meta_ref[2 * ab + p, 3 * t : 3 * t + 1, :128], (16, 128))
                    cos = phase_ref[ab, p, t, 0, rows, :] * RELAX
                    sin = phase_ref[ab, p, t, 1, rows, :] * RELAX
                    for half in range(q // 128):
                        spans = (slice(half * 128, half * 128 + 128), slice(q + half * 128, q + half * 128 + 128))
                        other = [e_ref[1 - ab, p, 0, rows, span] for span in spans]
                        for k in range(1, SHOTS_DEV):
                            other = [
                                jnp.where(slot == k, e_ref[1 - ab, p, k, rows, span], o)
                                for o, span in zip(other, spans)
                            ]
                        shifted = (other[0] * cos + other[1] * sin, other[1] * cos - other[0] * sin)
                        for span, shift in zip(spans, shifted):
                            mine = e_ref[ab, p, t, rows, span]
                            z = mine + RELAX * (bh_ref[ab, p, t, rows, span] - mine) - shift
                            z_ref[ab, p, t, rows, span] = z
                            side = down_ref if p == 0 else up_ref
                            side[ab, t, rows, span] = z.astype(bf16)
        return carry

    lax.fori_loop(0, fl // 16, body, 0)


def first_kernel(in_ref, table_ref, z_ref, bh_ref, meta_ref, phase_ref, down_ref, up_ref, e_ref):
    fl, q2 = in_ref.shape[2], in_ref.shape[3]
    high, low = table_ref[0], table_ref[1]
    for src in range(ROLES):
        ab, p = src // 2, src % 2
        data = in_ref[src, : 2 * SHOTS_DEV].reshape(2 * SHOTS_DEV * fl, q2)
        out = jnp.dot(data, high, preferred_element_type=f32) + jnp.dot(data, low, preferred_element_type=f32)
        out = out.reshape(2, SHOTS_DEV, fl, q2)
        e_ref[ab, p] = out[0]
        bh_ref[ab, p] = out[1]
        meta = in_ref[src, 2 * SHOTS_DEV, :16, :128].astype(f32)
        meta_ref[src] = meta
        whole = meta.astype(jnp.int32)
        freq = lax.axis_index("f") * (ROLES * fl) + (lax.axis_index("yh") * 2 + lax.axis_index("h")) * fl
        freq = freq + lax.broadcasted_iota(jnp.int32, (fl, 128), 0)
        for t in range(SHOTS_DEV):
            offset = whole[3 * t + 1 : 3 * t + 2, :] * 32 + whole[3 * t + 2 : 3 * t + 3, :]
            cos, sin = phases((freq * offset) & (NT - 1))
            phase_ref[ab, p, t, 0] = cos
            phase_ref[ab, p, t, 1] = sin
    relax(e_ref, bh_ref, meta_ref, phase_ref, z_ref, down_ref, up_ref)


def sums_kernel(n, z_ref, up_ref, down_ref, out_ref, halo_ref):
    fl, q = z_ref.shape[3], z_ref.shape[4] // 2
    fetch_halo(n, up_ref, down_ref, halo_ref)

    def body(i, totals):
        rows = pl.ds(pl.multiple_of(i * 8, 8), 8)
        totals = list(totals)
        for ab in range(2):
            for half in range(q // 128):
                for w, x in enumerate(spectra(z_ref, halo_ref, ab, rows, half, q)):
                    for re, im in x:
                        square = re * re + im * im
                        totals[ab * 3 + w] += square * lax.rsqrt(jnp.maximum(square, TINY))
        return tuple(totals)

    totals = lax.fori_loop(0, fl // 8, body, (jnp.zeros((8, 128), f32),) * 6)
    row = lax.broadcasted_iota(jnp.int32, (8, 128), 0)
    tile = jnp.zeros((8, 128), f32)
    for k, total in enumerate(totals):
        tile = jnp.where(row == k, jnp.sum(total, axis=0, keepdims=True), tile)
    for k in range(out_ref.shape[0]):
        out_ref[k] = tile


def shrink_windows(n, count, z_ref, up_ref, down_ref, parts_ref, levels_ref, e_ref, halo_ref):
    fl, q = z_ref.shape[3], z_ref.shape[4] // 2
    fetch_halo(n, up_ref, down_ref, halo_ref)
    g, first, _ = place(n)
    tile = parts_ref[0]
    for k in range(1, parts_ref.shape[0]):
        tile = tile + parts_ref[k]
    total = jnp.sum(tile, axis=1, keepdims=True)
    lams = []
    for ab in range(2):
        for w in range(3):
            window = jnp.maximum((ab * n + g) * 2 + w - 1, 0)
            scale = LEVEL_SCALE / count * levels_ref[window].astype(f32)
            lams.append(jnp.broadcast_to(total[3 * ab + w : 3 * ab + w + 1, :] * scale, (8, 128)))
    here = jnp.where(first, 0.0, ROOT8)

    def body(i, carry):
        rows = pl.ds(pl.multiple_of(i * 8, 8), 8)
        for ab in range(2):
            for half in range(q // 128):
                parts = []
                for w, x in enumerate(spectra(z_ref, halo_ref, ab, rows, half, q)):
                    lam = lams[3 * ab + w]
                    root = here if (ab == 0 and w == 0) else ROOT8
                    kept = []
                    for re, im in x:
                        inverse = lax.rsqrt(jnp.maximum(re * re + im * im, TINY))
                        factor = jnp.maximum(root - lam * inverse * root, 0.0)
                        kept.append((re * factor, im * factor))
                    parts.append(dft8(kept, -1, ("second", "both", "first")[w]))
                for p, (a, b) in enumerate(((parts[0], parts[1][:4]), (parts[1][4:], parts[2]))):
                    for t in range(SHOTS_DEV):
                        re, im = add(a[t], b[t])
                        e_ref[ab, p, t, rows, slice(half * 128, half * 128 + 128)] = re
                        e_ref[ab, p, t, rows, slice(q + half * 128, q + half * 128 + 128)] = im
        return carry

    lax.fori_loop(0, fl // 8, body, 0)


def middle_kernel(n, count, z_ref, up_ref, down_ref, parts_ref, levels_ref, bh_ref, meta_ref, phase_ref,
                  z_out, down_out, up_out, e_ref, halo_ref):
    shrink_windows(n, count, z_ref, up_ref, down_ref, parts_ref, levels_ref, e_ref, halo_ref)
    relax(e_ref, bh_ref, meta_ref, phase_ref, z_out, down_out, up_out)


def last_kernel(n, count, z_ref, up_ref, down_ref, parts_ref, levels_ref, table_ref, out_ref, e_ref, halo_ref):
    shrink_windows(n, count, z_ref, up_ref, down_ref, parts_ref, levels_ref, e_ref, halo_ref)
    fl, q2 = z_ref.shape[3], z_ref.shape[4]
    high, low = table_ref[0], table_ref[1]
    for src in range(ROLES):
        data = e_ref[src // 2, src % 2].reshape(SHOTS_DEV * fl, q2)
        top = data.astype(bf16)
        rest = (data - top.astype(f32)).astype(bf16)
        out = jnp.dot(top, high, preferred_element_type=f32)
        out = out + (jnp.dot(rest, high, preferred_element_type=f32) + jnp.dot(top, low, preferred_element_type=f32))
        out_ref[src] = out.reshape(SHOTS_DEV, fl, q2).astype(bf16)


def unpack_kernel(in_ref, out_ref):
    fl, q = in_ref.shape[2], in_ref.shape[3] // 2
    for role in range(ROLES):
        rows = slice(role * fl, (role + 1) * fl)
        for t in range(SHOTS_DEV):
            out_ref[0, t, rows, :] = in_ref[role, t, :, :q]
            out_ref[1, t, rows, :] = in_ref[role, t, :, q:]


def call(kernel, name, outs, in_specs, scratch=()):
    return pl.pallas_call(
        kernel,
        out_shape=outs,
        in_specs=in_specs,
        out_specs=jax.tree.map(lambda _: VMEM, outs),
        scratch_shapes=list(scratch),
        name=name,
        compiler_params=pltpu.CompilerParams(vmem_limit_bytes=24 * 1024 * 1024),
    )


def on_device(n, nf, blended, estimate, partner, delays, levels):
    q, fl = estimate.shape[3], estimate.shape[2] // ROLES
    shape = jax.ShapeDtypeStruct
    run = (2, 2, SHOTS_DEV, fl, 2 * q)
    side = shape((2, SHOTS_DEV, fl, 2 * q), bf16)
    e_scratch = pltpu.VMEM(run, f32)
    halo_scratch = pltpu.VMEM((2, 2, SHOTS_DEV, fl, 2 * q), f32)
    count = 8 * nf * ROLES * fl * q
    members = ROLES * nf
    forward, backward = receiver_tables(q, 1.0), receiver_tables(q, -1.0)

    packed = call(
        functools.partial(pack_kernel, nf),
        "pack",
        shape((ROLES, 2 * SHOTS_DEV + 1, fl, 2 * q), bf16),
        [VMEM, VMEM, SMEM, SMEM],
    )(estimate, blended, partner, delays)
    gathered = lax.all_to_all(packed, GROUP, 0, 0, tiled=True)
    z, bh, meta, phase, down, up = call(
        first_kernel,
        "first",
        (
            shape(run, f32),
            shape(run, f32),
            shape((ROLES, 16, 128), f32),
            shape((2, 2, SHOTS_DEV, 2, fl, 128), f32),
            side,
            side,
        ),
        [VMEM, VMEM],
        [e_scratch],
    )(gathered, jnp.asarray(forward))
    for index in range(PASSES):
        down = lax.ppermute(down, "g", [(i, (i - 1) % n) for i in range(n)])
        up = lax.ppermute(up, "g", [(i, (i + 1) % n) for i in range(n)])
        parts = call(
            functools.partial(sums_kernel, n),
            "sums",
            shape((members, 8, 128), f32),
            [VMEM] * 3,
            [halo_scratch],
        )(z, up, down)
        parts = lax.all_to_all(parts, SUM_GROUP, 0, 0, tiled=True)
        if index < PASSES - 1:
            z, down, up = call(
                functools.partial(middle_kernel, n, count),
                "middle",
                (shape(run, f32), side, side),
                [VMEM] * 4 + [SMEM] + [VMEM] * 3,
                [e_scratch, halo_scratch],
            )(z, up, down, parts, levels, bh, meta, phase)
    out = call(
        functools.partial(last_kernel, n, count),
        "last",
        shape((ROLES, SHOTS_DEV, fl, 2 * q), bf16),
        [VMEM] * 4 + [SMEM] + [VMEM],
        [e_scratch, halo_scratch],
    )(z, up, down, parts, levels, jnp.asarray(backward))
    out = lax.all_to_all(out, GROUP, 0, 0, tiled=True)
    return call(unpack_kernel, "unpack", shape(estimate.shape, bf16), [VMEM])(out)


def solution(mesh):
    shots, nf = mesh.shape["shot"], mesh.shape["freq"]
    n = shots // 4
    fine = Mesh(mesh.devices.reshape(2, n, 2, nf), ("yh", "g", "h", "f"))
    spec = P(None, ("yh", "g", "h"), "f", None)
    return jax.shard_map(
        functools.partial(on_device, n, nf),
        mesh=fine,
        in_specs=(spec, spec, P(("yh", "g", "h")), P(), P()),
        out_specs=spec,
        check_vma=False,
    )
```

```python
import functools
import math

import jax
import jax.numpy as jnp
import numpy as np
from jax import lax
from jax.experimental import pallas as pl
from jax.experimental.pallas import tpu as pltpu
from jax.sharding import Mesh
from jax.sharding import PartitionSpec as P

NT = 1024
PASSES = 2
SHOTS_DEV = 4
ROLES = 4
RELAX = 0.5
LEVEL_SCALE = 0.25
TINY = 1e-37
ROOT8 = 1.0 / math.sqrt(8.0)
HALF_ROOT = math.sqrt(0.5)
TAPER = [math.sin(math.pi * (t + 0.5) / 8) ** 2 * ROOT8 for t in range(8)]
GROUP = ("yh", "h")
SUM_GROUP = ("yh", "h", "f")

f32 = jnp.float32
bf16 = jnp.bfloat16
VMEM = pl.BlockSpec(memory_space=pltpu.VMEM)
SMEM = pl.BlockSpec(memory_space=pltpu.SMEM)
HBM = pl.BlockSpec(memory_space=pltpu.HBM)


def receiver_tables(length, sign):
    k = np.arange(length)
    angle = 2.0 * np.pi / length * ((k[:, None] * k[None, :]) % length)
    c, s = np.cos(angle) / math.sqrt(length), sign * np.sin(angle) / math.sqrt(length)
    full = np.block([[c, -s], [s, c]]).astype(np.float32)
    high = full.astype(jnp.bfloat16)
    low = (full - high.astype(np.float32)).astype(jnp.bfloat16)
    return np.stack([high, low])


def add(a, b):
    return (a[0] + b[0], a[1] + b[1])


def sub(a, b):
    return (a[0] - b[0], a[1] - b[1])


def turn(a, sign):
    return (a[1], -a[0]) if sign > 0 else (-a[1], a[0])


def twist(a, power, sign):
    if power == 0:
        return a
    if power == 2:
        return turn(a, sign)
    re, im = a
    if sign > 0:
        one = ((re + im) * HALF_ROOT, (im - re) * HALF_ROOT)
    else:
        one = ((re - im) * HALF_ROOT, (im + re) * HALF_ROOT)
    return one if power == 1 else turn(one, sign)


def dft4(a, b, c, d, sign):
    s0, s1, s2, s3 = add(a, c), sub(a, c), add(b, d), turn(sub(b, d), sign)
    return [add(s0, s2), add(s1, s3), sub(s0, s2), sub(s1, s3)]


def dft8(x, sign, part="both"):
    even = dft4(x[0], x[2], x[4], x[6], sign)
    odd = dft4(x[1], x[3], x[5], x[7], sign)
    odd = [twist(odd[k], k, sign) for k in range(4)]
    first = [add(even[k], odd[k]) for k in range(4)] if part != "second" else []
    second = [sub(even[k], odd[k]) for k in range(4)] if part != "first" else []
    return first + second


def windowed(first, second):
    both = first + second
    return [(both[t][0] * TAPER[t], both[t][1] * TAPER[t]) for t in range(8)]


def load(ref, ab, block, rows, half, q):
    lo, hi = half * 128, q + half * 128
    out = []
    for t in range(SHOTS_DEV):
        at = (ab, block, t) if block is not None else (ab, t)
        out.append((ref[(*at, rows, slice(lo, lo + 128))], ref[(*at, rows, slice(hi, hi + 128))]))
    return out


def place(n):
    g = lax.axis_index("g")
    first, last = g == 0, g == n - 1
    return g, first, last


def fetch_halo(n, up_ref, down_ref, halo_ref):
    _, first, last = place(n)
    for ab in range(2):
        source = jnp.where(first, 0, ab)
        halo_ref[0, ab] = up_ref[source].astype(f32)
        source = jnp.where(last, 1, ab)
        scale = jnp.where(last, 0.0, 1.0) if ab == 1 else 1.0
        halo_ref[1, ab] = down_ref[source].astype(f32) * scale


def spectra(z_ref, halo_ref, ab, rows, half, q):
    prev = load(halo_ref, 0, ab, rows, half, q)
    even = load(z_ref, ab, 0, rows, half, q)
    odd = load(z_ref, ab, 1, rows, half, q)
    after = load(halo_ref, 1, ab, rows, half, q)
    for pair in ((prev, even), (even, odd), (odd, after)):
        yield dft8(windowed(*pair), 1)


def pack_kernel(e_ref, b_ref, partner_ref, delays_ref, out_ref, partner_smem, delays_smem, sems, small_sems):
    fl = e_ref.shape[2] // ROLES
    columns = e_ref.shape[3] // 128
    small = [
        pltpu.make_async_copy(partner_ref, partner_smem, small_sems.at[0]),
        pltpu.make_async_copy(delays_ref, delays_smem, small_sems.at[1]),
    ]
    for copy in small:
        copy.start()
    copies = []
    for k, ref in enumerate((e_ref, b_ref)):
        for part in range(2):
            for half in range(columns):
                for role in range(ROLES):
                    source = ref.at[part, :, pl.ds(role * fl, fl), pl.ds(half * 128, 128)]
                    first = (part * columns + half) * 2 * SHOTS_DEV + k * SHOTS_DEV
                    target = out_ref.at[role, pl.ds(first, SHOTS_DEV)]
                    copies.append(pltpu.make_async_copy(source, target, sems.at[len(copies)]))
                    copies[-1].start()
    for copy in small:
        copy.wait()
    block = (lax.axis_index("yh") * lax.axis_size("g") + lax.axis_index("g")) * 2 + lax.axis_index("h")
    row = lax.broadcasted_iota(jnp.int32, (fl, 128), 0)
    meta = jnp.zeros((fl, 128), f32)
    for t in range(SHOTS_DEV):
        other = partner_smem[t]
        offset = (delays_smem[other] - delays_smem[block * SHOTS_DEV + t]) & (NT - 1)
        for i, value in enumerate((other & (SHOTS_DEV - 1), offset >> 5, offset & 31)):
            meta = jnp.where(row == 3 * t + i, value.astype(f32), meta)
    for role in range(ROLES):
        out_ref[role, 4 * SHOTS_DEV * columns] = meta.astype(bf16)
    for copy in copies:
        copy.wait()


def phases(index):
    quadrant = (index + 128) >> 8
    x = (index - (quadrant << 8)).astype(f32) * (2.0 * math.pi / NT)
    x2 = x * x
    s = x * (1 + x2 * (-1 / 6 + x2 * (1 / 120 + x2 * (-1 / 5040 + x2 * (1 / 362880)))))
    c = 1 + x2 * (-1 / 2 + x2 * (1 / 24 + x2 * (-1 / 720 + x2 * (1 / 40320))))
    swap = (quadrant & 1) == 1
    cos, sin = jnp.where(swap, s, c), jnp.where(swap, c, s)
    cos = jnp.where(((quadrant + 1) & 2) == 2, -cos, cos)
    sin = jnp.where((quadrant & 2) == 2, -sin, sin)
    return cos, sin


def relax(e_ref, bh_ref, meta_ref, phase_ref, z_ref, down_ref, up_ref):
    fl, q = e_ref.shape[3], e_ref.shape[4] // 2

    def body(i, carry):
        rows = pl.ds(pl.multiple_of(i * 16, 16), 16)
        for ab in range(2):
            for p in range(2):
                for t in range(SHOTS_DEV):
                    slot = jnp.broadcast_to(meta_ref[2 * ab + p, 3 * t : 3 * t + 1, :128], (16, 128))
                    cos = phase_ref[ab, p, t, 0, rows, :] * RELAX
                    sin = phase_ref[ab, p, t, 1, rows, :] * RELAX
                    for half in range(q // 128):
                        spans = (slice(half * 128, half * 128 + 128), slice(q + half * 128, q + half * 128 + 128))
                        other = [e_ref[1 - ab, p, 0, rows, span] for span in spans]
                        for k in range(1, SHOTS_DEV):
                            other = [
                                jnp.where(slot == k, e_ref[1 - ab, p, k, rows, span], o)
                                for o, span in zip(other, spans)
                            ]
                        shifted = (other[0] * cos + other[1] * sin, other[1] * cos - other[0] * sin)
                        for span, shift in zip(spans, shifted):
                            mine = e_ref[ab, p, t, rows, span]
                            z = mine + RELAX * (bh_ref[ab, p, t, rows, span] - mine) - shift
                            z_ref[ab, p, t, rows, span] = z
                            side = down_ref if p == 0 else up_ref
                            side[ab, t, rows, span] = z.astype(bf16)
        return carry

    lax.fori_loop(0, fl // 16, body, 0)


def first_kernel(in_ref, table_ref, z_ref, bh_ref, meta_ref, phase_ref, down_ref, up_ref, e_ref):
    fl, q2 = in_ref.shape[2], table_ref.shape[1]
    high, low = table_ref[0], table_ref[1]
    slabs = 2 * SHOTS_DEV
    for src in range(ROLES):
        ab, p = src // 2, src % 2
        data = [in_ref[src, c * slabs : (c + 1) * slabs].reshape(slabs * fl, 128) for c in range(q2 // 128)]
        data = jnp.concatenate(data, axis=1)
        out = jnp.dot(data, high, preferred_element_type=f32) + jnp.dot(data, low, preferred_element_type=f32)
        out = out.reshape(2, SHOTS_DEV, fl, q2)
        e_ref[ab, p] = out[0]
        bh_ref[ab, p] = out[1]
        meta = in_ref[src, slabs * (q2 // 128), :16, :].astype(f32)
        meta_ref[src] = meta
        whole = meta.astype(jnp.int32)
        freq = lax.axis_index("f") * (ROLES * fl) + (lax.axis_index("yh") * 2 + lax.axis_index("h")) * fl
        freq = freq + lax.broadcasted_iota(jnp.int32, (fl, 128), 0)
        for t in range(SHOTS_DEV):
            offset = whole[3 * t + 1 : 3 * t + 2, :] * 32 + whole[3 * t + 2 : 3 * t + 3, :]
            cos, sin = phases((freq * offset) & (NT - 1))
            phase_ref[ab, p, t, 0] = cos
            phase_ref[ab, p, t, 1] = sin
    relax(e_ref, bh_ref, meta_ref, phase_ref, z_ref, down_ref, up_ref)


def sums_kernel(n, z_ref, up_ref, down_ref, out_ref, halo_ref):
    fl, q = z_ref.shape[3], z_ref.shape[4] // 2
    fetch_halo(n, up_ref, down_ref, halo_ref)

    def body(i, totals):
        rows = pl.ds(pl.multiple_of(i * 8, 8), 8)
        totals = list(totals)
        for ab in range(2):
            for half in range(q // 128):
                for w, x in enumerate(spectra(z_ref, halo_ref, ab, rows, half, q)):
                    for re, im in x:
                        square = re * re + im * im
                        totals[ab * 3 + w] += square * lax.rsqrt(jnp.maximum(square, TINY))
        return tuple(totals)

    totals = lax.fori_loop(0, fl // 8, body, (jnp.zeros((8, 128), f32),) * 6)
    row = lax.broadcasted_iota(jnp.int32, (8, 128), 0)
    tile = jnp.zeros((8, 128), f32)
    for k, total in enumerate(totals):
        tile = jnp.where(row == k, jnp.sum(total, axis=0, keepdims=True), tile)
    for k in range(out_ref.shape[0]):
        out_ref[k] = tile


def shrink_windows(n, count, z_ref, up_ref, down_ref, parts_ref, levels_ref, e_ref, halo_ref):
    fl, q = z_ref.shape[3], z_ref.shape[4] // 2
    fetch_halo(n, up_ref, down_ref, halo_ref)
    g, first, _ = place(n)
    tile = parts_ref[0]
    for k in range(1, parts_ref.shape[0]):
        tile = tile + parts_ref[k]
    total = jnp.sum(tile, axis=1, keepdims=True)
    lams = []
    for ab in range(2):
        for w in range(3):
            window = jnp.maximum((ab * n + g) * 2 + w - 1, 0)
            scale = LEVEL_SCALE / count * levels_ref[window].astype(f32)
            lams.append(jnp.broadcast_to(total[3 * ab + w : 3 * ab + w + 1, :] * scale, (8, 128)))
    here = jnp.where(first, 0.0, ROOT8)

    def body(i, carry):
        rows = pl.ds(pl.multiple_of(i * 8, 8), 8)
        for ab in range(2):
            for half in range(q // 128):
                parts = []
                for w, x in enumerate(spectra(z_ref, halo_ref, ab, rows, half, q)):
                    lam = lams[3 * ab + w]
                    root = here if (ab == 0 and w == 0) else ROOT8
                    kept = []
                    for re, im in x:
                        inverse = lax.rsqrt(jnp.maximum(re * re + im * im, TINY))
                        factor = jnp.maximum(root - lam * inverse * root, 0.0)
                        kept.append((re * factor, im * factor))
                    parts.append(dft8(kept, -1, ("second", "both", "first")[w]))
                for p, (a, b) in enumerate(((parts[0], parts[1][:4]), (parts[1][4:], parts[2]))):
                    for t in range(SHOTS_DEV):
                        re, im = add(a[t], b[t])
                        e_ref[ab, p, t, rows, slice(half * 128, half * 128 + 128)] = re
                        e_ref[ab, p, t, rows, slice(q + half * 128, q + half * 128 + 128)] = im
        return carry

    lax.fori_loop(0, fl // 8, body, 0)


def middle_kernel(n, count, z_ref, up_ref, down_ref, parts_ref, levels_ref, bh_ref, meta_ref, phase_ref,
                  z_out, down_out, up_out, e_ref, halo_ref):
    shrink_windows(n, count, z_ref, up_ref, down_ref, parts_ref, levels_ref, e_ref, halo_ref)
    relax(e_ref, bh_ref, meta_ref, phase_ref, z_out, down_out, up_out)


def last_kernel(n, count, z_ref, up_ref, down_ref, parts_ref, levels_ref, table_ref, out_ref, e_ref, halo_ref):
    shrink_windows(n, count, z_ref, up_ref, down_ref, parts_ref, levels_ref, e_ref, halo_ref)
    fl, q2 = z_ref.shape[3], z_ref.shape[4]
    high, low = table_ref[0], table_ref[1]
    data = e_ref[...].reshape(ROLES * SHOTS_DEV * fl, q2)
    top = data.astype(bf16)
    rest = (data - top.astype(f32)).astype(bf16)
    out = jnp.dot(top, high, preferred_element_type=f32)
    out = out + (jnp.dot(rest, high, preferred_element_type=f32) + jnp.dot(top, low, preferred_element_type=f32))
    out_ref[...] = out.reshape(ROLES, SHOTS_DEV, fl, q2).astype(bf16)


def unpack_kernel(in_ref, out_ref):
    fl, q = in_ref.shape[2], in_ref.shape[3] // 2
    for role in range(ROLES):
        rows = slice(role * fl, (role + 1) * fl)
        for t in range(SHOTS_DEV):
            out_ref[0, t, rows, :] = in_ref[role, t, :, :q]
            out_ref[1, t, rows, :] = in_ref[role, t, :, q:]


def call(kernel, name, outs, in_specs, scratch=()):
    return pl.pallas_call(
        kernel,
        out_shape=outs,
        in_specs=in_specs,
        out_specs=jax.tree.map(lambda _: VMEM, outs),
        scratch_shapes=list(scratch),
        name=name,
        compiler_params=pltpu.CompilerParams(vmem_limit_bytes=24 * 1024 * 1024),
    )


def on_device(n, nf, blended, estimate, partner, delays, levels):
    q, fl = estimate.shape[3], estimate.shape[2] // ROLES
    shape = jax.ShapeDtypeStruct
    run = (2, 2, SHOTS_DEV, fl, 2 * q)
    side = shape((2, SHOTS_DEV, fl, 2 * q), bf16)
    e_scratch = pltpu.VMEM(run, f32)
    halo_scratch = pltpu.VMEM((2, 2, SHOTS_DEV, fl, 2 * q), f32)
    count = 8 * nf * ROLES * fl * q
    members = ROLES * nf
    forward, backward = receiver_tables(q, 1.0), receiver_tables(q, -1.0)

    slabs = 2 * SHOTS_DEV * (2 * q // 128)
    packed = call(
        pack_kernel,
        "pack",
        shape((ROLES, slabs + 1, fl, 128), bf16),
        [HBM] * 4,
        [
            pltpu.SMEM(partner.shape, jnp.int32),
            pltpu.SMEM(delays.shape, jnp.int32),
            pltpu.SemaphoreType.DMA((4 * ROLES * (q // 128),)),
            pltpu.SemaphoreType.DMA((2,)),
        ],
    )(estimate, blended, partner, delays)
    gathered = lax.all_to_all(packed, GROUP, 0, 0, tiled=True)
    z, bh, meta, phase, down, up = call(
        first_kernel,
        "first",
        (
            shape(run, f32),
            shape(run, f32),
            shape((ROLES, 16, 128), f32),
            shape((2, 2, SHOTS_DEV, 2, fl, 128), f32),
            side,
            side,
        ),
        [VMEM, VMEM],
        [e_scratch],
    )(gathered, jnp.asarray(forward))
    for index in range(PASSES):
        down = lax.ppermute(down, "g", [(i, (i - 1) % n) for i in range(n)])
        up = lax.ppermute(up, "g", [(i, (i + 1) % n) for i in range(n)])
        parts = call(
            functools.partial(sums_kernel, n),
            "sums",
            shape((members, 8, 128), f32),
            [VMEM] * 3,
            [halo_scratch],
        )(z, up, down)
        parts = lax.all_to_all(parts, SUM_GROUP, 0, 0, tiled=True)
        if index < PASSES - 1:
            z, down, up = call(
                functools.partial(middle_kernel, n, count),
                "middle",
                (shape(run, f32), side, side),
                [VMEM] * 4 + [SMEM] + [VMEM] * 3,
                [e_scratch, halo_scratch],
            )(z, up, down, parts, levels, bh, meta, phase)
    out = call(
        functools.partial(last_kernel, n, count),
        "last",
        shape((ROLES, SHOTS_DEV, fl, 2 * q), bf16),
        [VMEM] * 4 + [SMEM] + [VMEM],
        [e_scratch, halo_scratch],
    )(z, up, down, parts, levels, jnp.asarray(backward))
    out = lax.all_to_all(out, GROUP, 0, 0, tiled=True)
    return call(unpack_kernel, "unpack", shape(estimate.shape, bf16), [VMEM])(out)


def solution(mesh):
    shots, nf = mesh.shape["shot"], mesh.shape["freq"]
    n = shots // 4
    fine = Mesh(mesh.devices.reshape(2, n, 2, nf), ("yh", "g", "h", "f"))
    spec = P(None, ("yh", "g", "h"), "f", None)
    return jax.shard_map(
        functools.partial(on_device, n, nf),
        mesh=fine,
        in_specs=(spec, spec, P(("yh", "g", "h")), P(), P()),
        out_specs=spec,
        check_vma=False,
    )
```

```python
import functools
import math

import jax
import jax.numpy as jnp
import numpy as np
from jax import lax
from jax.experimental import pallas as pl
from jax.experimental.pallas import tpu as pltpu
from jax.sharding import Mesh
from jax.sharding import PartitionSpec as P

NT = 1024
SHOTS_DEV = 4
ROLES = 4
RELAX = 0.5
LEVEL_SCALE = 0.25
TINY = 1e-37
PACK_GRANT = 65_900_000
ROOT8 = 1.0 / math.sqrt(8.0)
HALF_ROOT = math.sqrt(0.5)
TAPER = [math.sin(math.pi * (t + 0.5) / 8) ** 2 * ROOT8 for t in range(8)]
GROUP = ("yh", "h")
SUM_GROUP = ("yh", "h", "f")

f32 = jnp.float32
bf16 = jnp.bfloat16
VMEM = pl.BlockSpec(memory_space=pltpu.VMEM)
SMEM = pl.BlockSpec(memory_space=pltpu.SMEM)
HBM = pl.BlockSpec(memory_space=pltpu.HBM)


def receiver_tables(length, sign):
    k = np.arange(length)
    angle = 2.0 * np.pi / length * ((k[:, None] * k[None, :]) % length)
    c, s = np.cos(angle) / math.sqrt(length), sign * np.sin(angle) / math.sqrt(length)
    full = np.block([[c, -s], [s, c]]).astype(np.float32)
    high = full.astype(jnp.bfloat16)
    low = (full - high.astype(np.float32)).astype(jnp.bfloat16)
    return np.stack([high, low])


def add(a, b):
    return (a[0] + b[0], a[1] + b[1])


def sub(a, b):
    return (a[0] - b[0], a[1] - b[1])


def turn(a, sign):
    return (a[1], -a[0]) if sign > 0 else (-a[1], a[0])


def twist(a, power, sign):
    if power == 0:
        return a
    if power == 2:
        return turn(a, sign)
    re, im = a
    if sign > 0:
        one = ((re + im) * HALF_ROOT, (im - re) * HALF_ROOT)
    else:
        one = ((re - im) * HALF_ROOT, (im + re) * HALF_ROOT)
    return one if power == 1 else turn(one, sign)


def dft4(a, b, c, d, sign):
    s0, s1, s2, s3 = add(a, c), sub(a, c), add(b, d), turn(sub(b, d), sign)
    return [add(s0, s2), add(s1, s3), sub(s0, s2), sub(s1, s3)]


def dft8(x, sign, part="both"):
    even = dft4(x[0], x[2], x[4], x[6], sign)
    odd = dft4(x[1], x[3], x[5], x[7], sign)
    odd = [twist(odd[k], k, sign) for k in range(4)]
    first = [add(even[k], odd[k]) for k in range(4)] if part != "second" else []
    second = [sub(even[k], odd[k]) for k in range(4)] if part != "first" else []
    return first + second


def windowed(first, second, scale):
    out = [(re * TAPER[t], im * TAPER[t]) for t, (re, im) in enumerate(first)]
    for t, (re, im) in enumerate(second):
        weight = TAPER[SHOTS_DEV + t] if scale is None else TAPER[SHOTS_DEV + t] * scale
        out.append((re * weight, im * weight))
    return out


def load(ref, at, rows, half, q):
    lo, hi = half * 128, q + half * 128
    return [(ref[(*at, t, rows, slice(lo, lo + 128))], ref[(*at, t, rows, slice(hi, hi + 128))]) for t in range(SHOTS_DEV)]


def store(ref, at, rows, half, q, block):
    for t, (re, im) in enumerate(block):
        ref[(*at, t, rows, slice(half * 128, half * 128 + 128))] = re
        ref[(*at, t, rows, slice(q + half * 128, q + half * 128 + 128))] = im


def seams(n):
    g = lax.axis_index("g")
    return jnp.where(g == 0, 0.0, 1.0), jnp.where(g == n - 1, 0.0, 1.0)


def seam_scale(marks, ab, w, wide):
    before, after = (1, 3) if wide else (0, 2)
    return marks[0] if (ab == 0 and w == before) else marks[1] if (ab == 1 and w == after) else None


def blocks_of(z_ref, halo_ref, ab, rows, half, q, wide):
    before = [load(halo_ref, (0, ab, k), rows, half, q) for k in range(2 if wide else 1)]
    own = [load(z_ref, (ab, k), rows, half, q) for k in range(2)]
    after = [load(halo_ref, (1, ab, k), rows, half, q) for k in range(2 if wide else 1)]
    return before + own + after


def add_sums(n, z_ref, halo_ref, out_ref, wide):
    fl, q = z_ref.shape[3], z_ref.shape[4] // 2
    marks = seams(n)
    count = 5 if wide else 3

    def body(i, totals):
        rows = pl.ds(pl.multiple_of(i * 8, 8), 8)
        totals = list(totals)
        for ab in range(2):
            for half in range(q // 128):
                blocks = blocks_of(z_ref, halo_ref, ab, rows, half, q, wide)
                for w in range(count):
                    for re, im in dft8(windowed(blocks[w], blocks[w + 1], seam_scale(marks, ab, w, wide)), 1):
                        square = re * re + im * im
                        totals[ab * count + w] += square * lax.rsqrt(jnp.maximum(square, TINY))
        return tuple(totals)

    totals = lax.fori_loop(0, fl // 8, body, (jnp.zeros((8, 128), f32),) * (2 * count))
    row = lax.broadcasted_iota(jnp.int32, (16, 128), 0)
    tile = jnp.zeros((16, 128), f32)
    for k, total in enumerate(totals):
        tile = jnp.where(row == k, jnp.sum(total, axis=0, keepdims=True), tile)
    for k in range(out_ref.shape[0]):
        out_ref[k] = tile


def shrink_windows(n, size, z_ref, halo_ref, parts_ref, levels_ref, e_ref, wide):
    fl, q = z_ref.shape[3], z_ref.shape[4] // 2
    count = 5 if wide else 3
    marks = seams(n)
    tile = parts_ref[0]
    for k in range(1, parts_ref.shape[0]):
        tile = tile + parts_ref[k]
    total = jnp.sum(tile, axis=1, keepdims=True)
    lams = []
    for ab in range(2):
        for w in range(count):
            window = (2 * (ab * n + lax.axis_index("g")) + w - count // 2 + 4 * n) & (4 * n - 1)
            scale = LEVEL_SCALE / size * ROOT8 * levels_ref[window].astype(f32)
            lams.append(jnp.broadcast_to(total[count * ab + w : count * ab + w + 1, :] * scale, (8, 128)))

    def body(i, carry):
        rows = pl.ds(pl.multiple_of(i * 8, 8), 8)
        for ab in range(2):
            for half in range(q // 128):
                blocks = blocks_of(z_ref, halo_ref, ab, rows, half, q, wide)
                held = None
                for w in range(count):
                    scale = seam_scale(marks, ab, w, wide)
                    kept = []
                    for re, im in dft8(windowed(blocks[w], blocks[w + 1], scale), 1):
                        inverse = lax.rsqrt(jnp.maximum(re * re + im * im, TINY))
                        factor = jnp.maximum(ROOT8 - lams[count * ab + w] * inverse, 0.0)
                        kept.append((re * factor, im * factor))
                    y = dft8(kept, -1, "second" if w == 0 else "first" if w == count - 1 else "both")
                    if w > 0:
                        store(e_ref, (ab, w - 1), rows, half, q, [add(c, d) for c, d in zip(held, y[:4])])
                        y = y[4:]
                    held = y if scale is None else [(re * scale, im * scale) for re, im in y]
        return carry

    lax.fori_loop(0, fl // 8, body, 0)


def pack_kernel(e_ref, b_ref, partner_ref, delays_ref, out_ref, partner_smem, delays_smem, sems, small_sems):
    fl = e_ref.shape[2] // ROLES
    columns = e_ref.shape[3] // 128
    small = [
        pltpu.make_async_copy(partner_ref, partner_smem, small_sems.at[0]),
        pltpu.make_async_copy(delays_ref, delays_smem, small_sems.at[1]),
    ]
    for copy in small:
        copy.start()
    copies = []
    for k, ref in enumerate((e_ref, b_ref)):
        for part in range(2):
            for half in range(columns):
                for role in range(ROLES):
                    source = ref.at[part, :, pl.ds(role * fl, fl), pl.ds(half * 128, 128)]
                    first = (part * columns + half) * 2 * SHOTS_DEV + k * SHOTS_DEV
                    target = out_ref.at[role, pl.ds(first, SHOTS_DEV)]
                    copies.append(pltpu.make_async_copy(source, target, sems.at[len(copies)]))
                    copies[-1].start()
    for copy in small:
        copy.wait()
    block = (lax.axis_index("yh") * lax.axis_size("g") + lax.axis_index("g")) * 2 + lax.axis_index("h")
    row = lax.broadcasted_iota(jnp.int32, (fl, 128), 0)
    meta = jnp.zeros((fl, 128), f32)
    for t in range(SHOTS_DEV):
        other = partner_smem[t]
        offset = (delays_smem[other] - delays_smem[block * SHOTS_DEV + t]) & (NT - 1)
        for i, value in enumerate((other & (SHOTS_DEV - 1), offset >> 5, offset & 31)):
            meta = jnp.where(row == 3 * t + i, value.astype(f32), meta)
    for role in range(ROLES):
        out_ref[role, 4 * SHOTS_DEV * columns] = meta.astype(bf16)
    for copy in copies:
        copy.wait()


def phases(index):
    quadrant = (index + 128) >> 8
    x = (index - (quadrant << 8)).astype(f32) * (2.0 * math.pi / NT)
    x2 = x * x
    s = x * (1 + x2 * (-1 / 6 + x2 * (1 / 120 + x2 * (-1 / 5040 + x2 * (1 / 362880)))))
    c = 1 + x2 * (-1 / 2 + x2 * (1 / 24 + x2 * (-1 / 720 + x2 * (1 / 40320))))
    swap = (quadrant & 1) == 1
    cos, sin = jnp.where(swap, s, c), jnp.where(swap, c, s)
    cos = jnp.where(((quadrant + 1) & 2) == 2, -cos, cos)
    sin = jnp.where((quadrant & 2) == 2, -sin, sin)
    return cos, sin


def relax(e_ref, ab, k, rows, b_of, meta_of, phase_of, emit):
    q = e_ref.shape[4] // 2
    for t in range(SHOTS_DEV):
        slot = jnp.broadcast_to(meta_of(t), (16, 128))
        cos, sin = phase_of(t)
        for half in range(q // 128):
            spans = (slice(half * 128, half * 128 + 128), slice(q + half * 128, q + half * 128 + 128))
            other = [e_ref[1 - ab, k, 0, rows, span] for span in spans]
            for j in range(1, SHOTS_DEV):
                other = [jnp.where(slot == j, e_ref[1 - ab, k, j, rows, span], o) for o, span in zip(other, spans)]
            shifted = (other[0] * cos + other[1] * sin, other[1] * cos - other[0] * sin)
            for span, shift in zip(spans, shifted):
                emit(t, span, RELAX * ((e_ref[ab, k, t, rows, span] + b_of(t, span)) - shift))


def relax_own(e_ref, offset, b_of, meta_ref, phase_ref, emit):
    fl = e_ref.shape[3]

    def body(i, carry):
        rows = pl.ds(pl.multiple_of(i * 16, 16), 16)
        for ab in range(2):
            for p in range(2):
                relax(
                    e_ref,
                    ab,
                    p + offset,
                    rows,
                    lambda t, span: b_of(ab, p, t, rows, span),
                    lambda t: meta_ref[2 * ab + p, 3 * t : 3 * t + 1, :],
                    lambda t: (phase_ref[ab, p, t, 0, rows, :], phase_ref[ab, p, t, 1, rows, :]),
                    lambda t, span, z: emit(ab, p, t, rows, span, z),
                )
        return carry

    lax.fori_loop(0, fl // 16, body, 0)


def fill_phases(meta, fl, phase_ref, at):
    whole = meta.astype(jnp.int32)
    freq = lax.axis_index("f") * (ROLES * fl) + (lax.axis_index("yh") * 2 + lax.axis_index("h")) * fl
    freq = freq + lax.broadcasted_iota(jnp.int32, (fl, 128), 0)
    for t in range(SHOTS_DEV):
        offset = whole[3 * t + 1 : 3 * t + 2, :] * 32 + whole[3 * t + 2 : 3 * t + 3, :]
        cos, sin = phases((freq * offset) & (NT - 1))
        phase_ref[(*at, t, 0)] = cos
        phase_ref[(*at, t, 1)] = sin


def first_kernel(in_ref, table_ref, z_ref, meta_ref, phase_ref, zs_ref, b_even_ref, b_odd_ref, e_ref, bh_ref):
    fl, q2 = in_ref.shape[2], table_ref.shape[1]
    high, low = table_ref[0], table_ref[1]
    slabs = 2 * SHOTS_DEV
    for src in range(ROLES):
        ab, p = src // 2, src % 2
        data = [in_ref[src, c * slabs : (c + 1) * slabs].reshape(slabs * fl, 128) for c in range(q2 // 128)]
        data = jnp.concatenate(data, axis=1)
        out = jnp.dot(data, high, preferred_element_type=f32) + jnp.dot(data, low, preferred_element_type=f32)
        out = out.reshape(2, SHOTS_DEV, fl, q2)
        e_ref[ab, p] = out[0]
        bh_ref[ab, p] = out[1]
        raw = in_ref[src, slabs * (q2 // 128), :16, :]
        side = b_odd_ref if p else b_even_ref
        side[ab, : SHOTS_DEV * fl, :] = out[1].reshape(SHOTS_DEV * fl, q2).astype(bf16)
        side[ab, SHOTS_DEV * fl :, :] = jnp.concatenate([raw] * (q2 // 128), axis=1)
        meta_ref[src] = raw.astype(f32)
        fill_phases(raw.astype(f32), fl, phase_ref, (ab, p))

    def emit(ab, p, t, rows, span, z):
        z_ref[ab, p, t, rows, span] = z
        zs_ref[ab, p, t, rows, span] = z.astype(bf16)

    def b_of(ab, p, t, rows, span):
        return bh_ref[ab, p, t, rows, span]

    relax_own(e_ref, 0, b_of, meta_ref, phase_ref, emit)


def fetch_halo(n, up_ref, down_ref, halo_ref):
    g = lax.axis_index("g")
    for ab in range(2):
        halo_ref[0, ab] = up_ref[jnp.where(g == 0, 1 - ab, ab)].astype(f32)
        halo_ref[1, ab] = down_ref[jnp.where(g == n - 1, 1 - ab, ab)].astype(f32)


def wide_sums_kernel(n, z_ref, up_ref, down_ref, out_ref, halo_ref):
    fetch_halo(n, up_ref, down_ref, halo_ref)
    add_sums(n, z_ref, halo_ref, out_ref, True)


def sums_kernel(n, z_ref, halo_ref, out_ref):
    add_sums(n, z_ref, halo_ref, out_ref, False)


def middle_kernel(n, size, z_ref, up_ref, down_ref, parts_ref, levels_ref, b_even_ref, b_odd_ref, meta_ref, phase_ref,
                  b_up_ref, b_down_ref, z_out, halo_out, e_ref, far_ref, halo_ref):
    fl = z_ref.shape[3]
    g = lax.axis_index("g")
    fetch_halo(n, up_ref, down_ref, halo_ref)
    shrink_windows(n, size, z_ref, halo_ref, parts_ref, levels_ref, e_ref, True)

    def emit(ab, p, t, rows, span, z):
        z_out[ab, p, t, rows, span] = z

    def b_of(ab, p, t, rows, span):
        at = pl.ds(pl.multiple_of(rows.start + t * fl, 16), 16)
        return (b_odd_ref if p else b_even_ref)[ab, at, span].astype(f32)

    relax_own(e_ref, 1, b_of, meta_ref, phase_ref, emit)
    sides = []
    for side, ref in enumerate((b_up_ref, b_down_ref)):
        for ab in range(2):
            lane = jnp.where(g == (n - 1 if side else 0), 1 - ab, ab)
            meta = ref[lane, SHOTS_DEV * fl :, :128].astype(f32)
            fill_phases(meta, fl, far_ref, (side, ab))
            sides.append((side, ab, lane, ref, meta))

    for i in range(fl // 16):
        rows = slice(i * 16, i * 16 + 16)
        for side, ab, lane, ref, meta in sides:

            def emit_halo(t, span, z, side=side, ab=ab, rows=rows):
                halo_out[side, ab, 0, t, rows, span] = z

            relax(
                e_ref,
                ab,
                3 * side,
                rows,
                lambda t, span: ref[lane, t * fl + i * 16 : t * fl + i * 16 + 16, span].astype(f32),
                lambda t: meta[3 * t : 3 * t + 1, :],
                lambda t: (far_ref[side, ab, t, 0, rows, :], far_ref[side, ab, t, 1, rows, :]),
                emit_halo,
            )


def last_kernel(n, size, z_ref, halo_ref, parts_ref, levels_ref, table_ref, out_ref, e_ref):
    shrink_windows(n, size, z_ref, halo_ref, parts_ref, levels_ref, e_ref, False)
    fl, q2 = z_ref.shape[3], z_ref.shape[4]
    high, low = table_ref[0], table_ref[1]
    data = e_ref[...].reshape(ROLES * SHOTS_DEV * fl, q2)
    top = data.astype(bf16)
    rest = (data - top.astype(f32)).astype(bf16)
    out = jnp.dot(top, high, preferred_element_type=f32)
    out = out + (jnp.dot(rest, high, preferred_element_type=f32) + jnp.dot(top, low, preferred_element_type=f32))
    out_ref[...] = out.reshape(ROLES, SHOTS_DEV, fl, q2).astype(bf16)


def unpack_kernel(in_ref, out_ref):
    fl, q = in_ref.shape[2], in_ref.shape[3] // 2
    for role in range(ROLES):
        rows = slice(role * fl, (role + 1) * fl)
        for t in range(SHOTS_DEV):
            out_ref[0, t, rows, :] = in_ref[role, t, :, :q]
            out_ref[1, t, rows, :] = in_ref[role, t, :, q:]


def call(kernel, name, outs, in_specs, scratch=(), grant=24 * 1024 * 1024):
    return pl.pallas_call(
        kernel,
        out_shape=outs,
        in_specs=in_specs,
        out_specs=jax.tree.map(lambda _: VMEM, outs),
        scratch_shapes=list(scratch),
        name=name,
        compiler_params=pltpu.CompilerParams(vmem_limit_bytes=grant),
    )


def on_device(n, nf, blended, estimate, partner, delays, levels):
    q, fl = estimate.shape[3], estimate.shape[2] // ROLES
    shape = jax.ShapeDtypeStruct
    block = (SHOTS_DEV, fl, 2 * q)
    side = shape((2, SHOTS_DEV * fl + 16, 2 * q), bf16)
    size = 8 * nf * ROLES * fl * q
    parts_shape = shape((ROLES * nf, 16, 128), f32)
    forward, backward = receiver_tables(q, 1.0), receiver_tables(q, -1.0)
    before = [(i, (i - 1) % n) for i in range(n)]
    after = [(i, (i + 1) % n) for i in range(n)]

    slabs = 2 * SHOTS_DEV * (2 * q // 128)
    packed = call(
        pack_kernel,
        "pack",
        shape((ROLES, slabs + 1, fl, 128), bf16),
        [HBM] * 4,
        [
            pltpu.SMEM(partner.shape, jnp.int32),
            pltpu.SMEM(delays.shape, jnp.int32),
            pltpu.SemaphoreType.DMA((4 * ROLES * (q // 128),)),
            pltpu.SemaphoreType.DMA((2,)),
        ],
        PACK_GRANT,
    )(estimate, blended, partner, delays)
    gathered = lax.all_to_all(packed, GROUP, 0, 0, tiled=True)
    z, meta, phase, zs, b_even, b_odd = call(
        first_kernel,
        "first",
        (
            shape((2, 2, *block), f32),
            shape((ROLES, 16, 128), f32),
            shape((2, 2, SHOTS_DEV, 2, fl, 128), f32),
            shape((2, 2, *block), bf16),
            side,
            side,
        ),
        [VMEM, VMEM],
        [pltpu.VMEM((2, 2, *block), f32)] * 2,
    )(gathered, jnp.asarray(forward))
    down = lax.ppermute(zs, "g", before)
    up = lax.ppermute(zs, "g", after)
    b_down = lax.ppermute(b_even, "g", before)
    b_up = lax.ppermute(b_odd, "g", after)
    far = pltpu.VMEM((2, 2, 2, *block), f32)
    parts = call(functools.partial(wide_sums_kernel, n), "wide_sums", parts_shape, [VMEM] * 3, [far])(z, up, down)
    parts = lax.all_to_all(parts, SUM_GROUP, 0, 0, tiled=True)
    z, halo = call(
        functools.partial(middle_kernel, n, size),
        "middle",
        (shape((2, 2, *block), f32), shape((2, 2, 1, *block), f32)),
        [VMEM] * 4 + [SMEM] + [VMEM] * 6,
        [pltpu.VMEM((2, 4, *block), f32), pltpu.VMEM((2, 2, SHOTS_DEV, 2, fl, 128), f32), far],
    )(z, up, down, parts, levels, b_even, b_odd, meta, phase, b_up, b_down)
    parts = call(functools.partial(sums_kernel, n), "sums", parts_shape, [VMEM] * 2)(z, halo)
    parts = lax.all_to_all(parts, SUM_GROUP, 0, 0, tiled=True)
    out = call(
        functools.partial(last_kernel, n, size),
        "last",
        shape((ROLES, *block), bf16),
        [VMEM] * 3 + [SMEM] + [VMEM],
        [pltpu.VMEM((2, 2, *block), f32)],
    )(z, halo, parts, levels, jnp.asarray(backward))
    out = lax.all_to_all(out, GROUP, 0, 0, tiled=True)
    return call(unpack_kernel, "unpack", shape(estimate.shape, bf16), [VMEM])(out)


def solution(mesh):
    shots, nf = mesh.shape["shot"], mesh.shape["freq"]
    n = shots // 4
    fine = Mesh(mesh.devices.reshape(2, n, 2, nf), ("yh", "g", "h", "f"))
    spec = P(None, ("yh", "g", "h"), "f", None)
    return jax.shard_map(
        functools.partial(on_device, n, nf),
        mesh=fine,
        in_specs=(spec, spec, P(("yh", "g", "h")), P(), P()),
        out_specs=spec,
        check_vma=False,
    )
```

```python
import functools
import math

import jax
import jax.numpy as jnp
import numpy as np
from jax import lax
from jax.experimental import pallas as pl
from jax.experimental.pallas import tpu as pltpu
from jax.sharding import Mesh
from jax.sharding import PartitionSpec as P

NT = 1024
SHOTS_DEV = 4
ROLES = 4
RELAX = 0.5
LEVEL_SCALE = 0.25
TINY = 1e-37
ROOT8 = 1.0 / math.sqrt(8.0)
HALF_ROOT = math.sqrt(0.5)
TAPER = [math.sin(math.pi * (t + 0.5) / 8) ** 2 * ROOT8 for t in range(8)]
GROUP = ("yh", "h")
SUM_GROUP = ("yh", "h", "f")

f32 = jnp.float32
bf16 = jnp.bfloat16
VMEM = pl.BlockSpec(memory_space=pltpu.VMEM)
SMEM = pl.BlockSpec(memory_space=pltpu.SMEM)
HBM = pl.BlockSpec(memory_space=pltpu.HBM)


def receiver_tables(length, sign):
    k = np.arange(length)
    angle = 2.0 * np.pi / length * ((k[:, None] * k[None, :]) % length)
    c, s = np.cos(angle) / math.sqrt(length), sign * np.sin(angle) / math.sqrt(length)
    full = np.block([[c, -s], [s, c]]).astype(np.float32)
    high = full.astype(jnp.bfloat16)
    low = (full - high.astype(np.float32)).astype(jnp.bfloat16)
    return np.stack([high, low])


def add(a, b):
    return (a[0] + b[0], a[1] + b[1])


def sub(a, b):
    return (a[0] - b[0], a[1] - b[1])


def turn(a, sign):
    return (a[1], -a[0]) if sign > 0 else (-a[1], a[0])


def twist(a, power, sign):
    if power == 0:
        return a
    if power == 2:
        return turn(a, sign)
    re, im = a
    if sign > 0:
        one = ((re + im) * HALF_ROOT, (im - re) * HALF_ROOT)
    else:
        one = ((re - im) * HALF_ROOT, (im + re) * HALF_ROOT)
    return one if power == 1 else turn(one, sign)


def dft4(a, b, c, d, sign):
    s0, s1, s2, s3 = add(a, c), sub(a, c), add(b, d), turn(sub(b, d), sign)
    return [add(s0, s2), add(s1, s3), sub(s0, s2), sub(s1, s3)]


def dft8(x, sign, part="both"):
    even = dft4(x[0], x[2], x[4], x[6], sign)
    odd = dft4(x[1], x[3], x[5], x[7], sign)
    odd = [twist(odd[k], k, sign) for k in range(4)]
    first = [add(even[k], odd[k]) for k in range(4)] if part != "second" else []
    second = [sub(even[k], odd[k]) for k in range(4)] if part != "first" else []
    return first + second


def windowed(first, second, scale):
    out = [(re * TAPER[t], im * TAPER[t]) for t, (re, im) in enumerate(first)]
    for t, (re, im) in enumerate(second):
        weight = TAPER[SHOTS_DEV + t] if scale is None else TAPER[SHOTS_DEV + t] * scale
        out.append((re * weight, im * weight))
    return out


def load(ref, at, rows, half, q, count=SHOTS_DEV):
    lo, hi = half * 128, q + half * 128
    return [(ref[(*at, t, rows, slice(lo, lo + 128))], ref[(*at, t, rows, slice(hi, hi + 128))]) for t in range(count)]


def store(ref, at, rows, half, q, block):
    for t, (re, im) in enumerate(block):
        ref[(*at, t, rows, slice(half * 128, half * 128 + 128))] = re
        ref[(*at, t, rows, slice(q + half * 128, q + half * 128 + 128))] = im


def seams(n):
    g = lax.axis_index("g")
    return jnp.where(g == 0, 0.0, 1.0), jnp.where(g == n - 1, 0.0, 1.0)


def seam_scale(marks, ab, w, wide):
    before, after = (1, 3) if wide else (0, 2)
    return marks[0] if (ab == 0 and w == before) else marks[1] if (ab == 1 and w == after) else None


def blocks_of(z_ref, halo_ref, ab, rows, half, q, wide):
    before = [load(halo_ref, (0, ab, k), rows, half, q) for k in range(2 if wide else 1)]
    own = [load(z_ref, (ab, k), rows, half, q) for k in range(2)]
    after = [load(halo_ref, (1, ab, k), rows, half, q) for k in range(2 if wide else 1)]
    return before + own + after


def add_sums(n, z_ref, halo_ref, out_ref, wide, x_ref=None):
    fl, q = z_ref.shape[3], z_ref.shape[4] // 2
    marks = seams(n)
    count = 5 if wide else 3

    def body(i, totals):
        rows = pl.ds(pl.multiple_of(i * 8, 8), 8)
        totals = list(totals)
        for ab in range(2):
            for half in range(q // 128):
                blocks = blocks_of(z_ref, halo_ref, ab, rows, half, q, wide)
                for w in range(count):
                    x = dft8(windowed(blocks[w], blocks[w + 1], seam_scale(marks, ab, w, wide)), 1)
                    if x_ref is not None:
                        store(x_ref, (ab, w), rows, half, q, x)
                    for re, im in x:
                        square = re * re + im * im
                        totals[ab * count + w] += square * lax.rsqrt(jnp.maximum(square, TINY))
        return tuple(totals)

    totals = lax.fori_loop(0, fl // 8, body, (jnp.zeros((8, 128), f32),) * (2 * count))
    row = lax.broadcasted_iota(jnp.int32, (16, 128), 0)
    tile = jnp.zeros((16, 128), f32)
    for k, total in enumerate(totals):
        tile = jnp.where(row == k, jnp.sum(total, axis=0, keepdims=True), tile)
    for k in range(out_ref.shape[0]):
        out_ref[k] = tile


def shrink_windows(n, size, spectra_of, parts_ref, levels_ref, e_ref, wide):
    fl, q = e_ref.shape[3], e_ref.shape[4] // 2
    count = 5 if wide else 3
    marks = seams(n)
    tile = parts_ref[0]
    for k in range(1, parts_ref.shape[0]):
        tile = tile + parts_ref[k]
    total = jnp.sum(tile, axis=1, keepdims=True)
    lams = []
    for ab in range(2):
        for w in range(count):
            window = (2 * (ab * n + lax.axis_index("g")) + w - count // 2 + 4 * n) & (4 * n - 1)
            scale = LEVEL_SCALE / size * ROOT8 * levels_ref[window].astype(f32)
            lams.append(jnp.broadcast_to(total[count * ab + w : count * ab + w + 1, :] * scale, (8, 128)))

    def body(i, carry):
        rows = pl.ds(pl.multiple_of(i * 8, 8), 8)
        for ab in range(2):
            for half in range(q // 128):
                held = None
                for w, x in enumerate(spectra_of(ab, rows, half)):
                    scale = seam_scale(marks, ab, w, wide)
                    kept = []
                    for re, im in x:
                        inverse = lax.rsqrt(jnp.maximum(re * re + im * im, TINY))
                        factor = jnp.maximum(ROOT8 - lams[count * ab + w] * inverse, 0.0)
                        kept.append((re * factor, im * factor))
                    y = dft8(kept, -1, "second" if w == 0 else "first" if w == count - 1 else "both")
                    if w > 0:
                        store(e_ref, (ab, w - 1), rows, half, q, [add(c, d) for c, d in zip(held, y[:4])])
                        y = y[4:]
                    held = y if scale is None else [(re * scale, im * scale) for re, im in y]
        return carry

    lax.fori_loop(0, fl // 8, body, 0)


def pack_kernel(e_ref, b_ref, partner_ref, delays_ref, out_ref, partner_smem, delays_smem, sems, small_sems):
    fl = e_ref.shape[2] // ROLES
    columns = e_ref.shape[3] // 128
    small = [
        pltpu.make_async_copy(partner_ref, partner_smem, small_sems.at[0]),
        pltpu.make_async_copy(delays_ref, delays_smem, small_sems.at[1]),
    ]
    for copy in small:
        copy.start()
    copies = []
    for k, ref in enumerate((e_ref, b_ref)):
        for part in range(2):
            for half in range(columns):
                for role in range(ROLES):
                    source = ref.at[part, :, pl.ds(role * fl, fl), pl.ds(half * 128, 128)]
                    first = (part * columns + half) * 2 * SHOTS_DEV + k * SHOTS_DEV
                    target = out_ref.at[role, pl.ds(first, SHOTS_DEV)]
                    copies.append(pltpu.make_async_copy(source, target, sems.at[len(copies)]))
                    copies[-1].start()
    for copy in small:
        copy.wait()
    block = (lax.axis_index("yh") * lax.axis_size("g") + lax.axis_index("g")) * 2 + lax.axis_index("h")
    row = lax.broadcasted_iota(jnp.int32, (fl, 128), 0)
    meta = jnp.zeros((fl, 128), f32)
    for t in range(SHOTS_DEV):
        other = partner_smem[t]
        offset = (delays_smem[other] - delays_smem[block * SHOTS_DEV + t]) & (NT - 1)
        for i, value in enumerate((other & (SHOTS_DEV - 1), offset >> 5, offset & 31)):
            meta = jnp.where(row == 3 * t + i, value.astype(f32), meta)
    for role in range(ROLES):
        out_ref[role, 4 * SHOTS_DEV * columns] = meta.astype(bf16)
    for copy in copies:
        copy.wait()


def phases(index):
    quadrant = (index + 128) >> 8
    x = (index - (quadrant << 8)).astype(f32) * (2.0 * math.pi / NT)
    x2 = x * x
    s = x * (1 + x2 * (-1 / 6 + x2 * (1 / 120 + x2 * (-1 / 5040 + x2 * (1 / 362880)))))
    c = 1 + x2 * (-1 / 2 + x2 * (1 / 24 + x2 * (-1 / 720 + x2 * (1 / 40320))))
    swap = (quadrant & 1) == 1
    cos, sin = jnp.where(swap, s, c), jnp.where(swap, c, s)
    cos = jnp.where(((quadrant + 1) & 2) == 2, -cos, cos)
    sin = jnp.where((quadrant & 2) == 2, -sin, sin)
    return cos, sin


def fill_phases(metas, fl, phase_ref):
    lane = lax.broadcasted_iota(jnp.int32, (1, 128), 1)
    offsets = jnp.zeros((1, 128), jnp.int32)
    for m, meta in enumerate(metas):
        whole = meta.astype(jnp.int32)
        for t in range(SHOTS_DEV):
            offset = whole[3 * t + 1 : 3 * t + 2, :] * 32 + whole[3 * t + 2 : 3 * t + 3, :]
            offsets = jnp.where(lane == SHOTS_DEV * m + t, offset, offsets)
    freq = lax.axis_index("f") * (ROLES * fl) + (lax.axis_index("yh") * 2 + lax.axis_index("h")) * fl
    freq = freq + lax.broadcasted_iota(jnp.int32, (fl, 128), 0)
    cos, sin = phases((freq * offsets) & (NT - 1))
    phase_ref[0] = cos
    phase_ref[1] = sin


def relax(e_ref, ab, k, rows, b_of, meta_of, phase, column, emit):
    q = e_ref.shape[4] // 2
    for t in range(SHOTS_DEV):
        slot = jnp.broadcast_to(meta_of(t), (16, 128))
        cos, sin = [jnp.broadcast_to(table[:, column + t : column + t + 1], (16, 128)) for table in phase]
        for half in range(q // 128):
            spans = (slice(half * 128, half * 128 + 128), slice(q + half * 128, q + half * 128 + 128))
            other = [e_ref[1 - ab, k, 0, rows, span] for span in spans]
            for j in range(1, SHOTS_DEV):
                other = [jnp.where(slot == j, e_ref[1 - ab, k, j, rows, span], o) for o, span in zip(other, spans)]
            shifted = (other[0] * cos + other[1] * sin, other[1] * cos - other[0] * sin)
            for span, shift in zip(spans, shifted):
                emit(t, span, RELAX * ((e_ref[ab, k, t, rows, span] + b_of(t, span)) - shift))


def first_kernel(in_ref, table_ref, z_ref, meta_ref, phase_ref, zs_ref, b_even_ref, b_odd_ref, e_ref, bh_ref):
    fl, q2 = in_ref.shape[2], table_ref.shape[1]
    high, low = table_ref[0], table_ref[1]
    slabs = 2 * SHOTS_DEV
    metas = []
    for src in range(ROLES):
        ab, p = src // 2, src % 2
        data = [in_ref[src, c * slabs : (c + 1) * slabs].reshape(slabs * fl, 128) for c in range(q2 // 128)]
        data = jnp.concatenate(data, axis=1)
        out = jnp.dot(data, high, preferred_element_type=f32) + jnp.dot(data, low, preferred_element_type=f32)
        out = out.reshape(2, SHOTS_DEV, fl, q2)
        e_ref[ab, p] = out[0]
        bh_ref[ab, p] = out[1]
        raw = in_ref[src, slabs * (q2 // 128), :16, :]
        side = b_odd_ref if p else b_even_ref
        side[ab, : SHOTS_DEV * fl, :] = out[1].reshape(SHOTS_DEV * fl, q2).astype(bf16)
        side[ab, SHOTS_DEV * fl :, :] = jnp.concatenate([raw] * (q2 // 128), axis=1)
        metas.append(raw.astype(f32))
        meta_ref[src] = metas[-1]
    fill_phases(metas, fl, phase_ref)

    def body(i, carry):
        rows = pl.ds(pl.multiple_of(i * 16, 16), 16)
        phase = (phase_ref[0, rows, :], phase_ref[1, rows, :])
        for ab in range(2):
            for p in range(2):

                def emit(t, span, z):
                    z_ref[ab, p, t, rows, span] = z
                    zs_ref[ab, p, t, rows, span] = z.astype(bf16)

                relax(
                    e_ref,
                    ab,
                    p,
                    rows,
                    lambda t, span: bh_ref[ab, p, t, rows, span],
                    lambda t: meta_ref[2 * ab + p, 3 * t : 3 * t + 1, :],
                    phase,
                    SHOTS_DEV * (2 * ab + p),
                    emit,
                )
        return carry

    lax.fori_loop(0, fl // 16, body, 0)


def wide_sums_kernel(n, z_ref, up_ref, down_ref, out_ref, halo_ref):
    g = lax.axis_index("g")
    for ab in range(2):
        halo_ref[0, ab] = up_ref[jnp.where(g == 0, 1 - ab, ab)].astype(f32)
        halo_ref[1, ab] = down_ref[jnp.where(g == n - 1, 1 - ab, ab)].astype(f32)
    add_sums(n, z_ref, halo_ref, out_ref, True)


def middle_kernel(n, size, z_ref, halo_ref, parts_ref, levels_ref, b_even_ref, b_odd_ref, meta_ref, phase_ref,
                  b_up_ref, b_down_ref, x_out, parts_out, e_ref, far_meta_ref, far_ref, z2_ref, halo2_ref):
    fl, q = z_ref.shape[3], z_ref.shape[4] // 2
    g = lax.axis_index("g")
    marks = seams(n)

    def spectra_of(ab, rows, half):
        blocks = blocks_of(z_ref, halo_ref, ab, rows, half, q, True)
        for w in range(5):
            yield dft8(windowed(blocks[w], blocks[w + 1], seam_scale(marks, ab, w, True)), 1)

    shrink_windows(n, size, spectra_of, parts_ref, levels_ref, e_ref, True)
    lanes = []
    for side, ref in enumerate((b_up_ref, b_down_ref)):
        for ab in range(2):
            lanes.append(jnp.where(g == (n - 1 if side else 0), 1 - ab, ab))
            far_meta_ref[2 * side + ab] = ref[lanes[-1], SHOTS_DEV * fl :, :128].astype(f32)
    fill_phases([far_meta_ref[m] for m in range(4)], fl, far_ref)

    def body(i, carry):
        rows = pl.ds(pl.multiple_of(i * 16, 16), 16)
        own = (phase_ref[0, rows, :], phase_ref[1, rows, :])
        far = (far_ref[0, rows, :], far_ref[1, rows, :])
        for ab in range(2):
            for k in range(4):
                side, p = k // 2, k - 1
                if k in (1, 2):
                    b_ref, lane, phase, m, metas = (b_odd_ref if p else b_even_ref), ab, own, 2 * ab + p, meta_ref
                else:
                    b_ref, lane, phase, m, metas = (b_down_ref if side else b_up_ref), lanes[2 * side + ab], far, 2 * side + ab, far_meta_ref

                def emit(t, span, z):
                    if k in (1, 2):
                        z2_ref[ab, p, t, rows, span] = z
                    else:
                        halo2_ref[side, ab, 0, t, rows, span] = z

                def b_of(t, span):
                    at = pl.ds(pl.multiple_of(i * 16 + t * fl, 16), 16)
                    return b_ref[lane, at, span].astype(f32)

                def meta_of(t):
                    return metas[m, 3 * t : 3 * t + 1, :]

                relax(e_ref, ab, k, rows, b_of, meta_of, phase, SHOTS_DEV * m, emit)
        return carry

    lax.fori_loop(0, fl // 16, body, 0)
    add_sums(n, z2_ref, halo2_ref, parts_out, False, x_out)


def last_kernel(n, size, x_ref, parts_ref, levels_ref, table_ref, out_ref, e_ref):
    fl, q2 = x_ref.shape[3], x_ref.shape[4]

    def spectra_of(ab, rows, half):
        for w in range(3):
            yield load(x_ref, (ab, w), rows, half, q2 // 2, 8)

    shrink_windows(n, size, spectra_of, parts_ref, levels_ref, e_ref, False)
    data = e_ref[...].reshape(ROLES * SHOTS_DEV * fl, q2).astype(bf16)
    out = jnp.dot(data, table_ref[0], preferred_element_type=f32)
    out_ref[...] = out.reshape(ROLES, SHOTS_DEV, fl, q2).astype(bf16)


def unpack_kernel(in_ref, out_ref, sems):
    fl, q = in_ref.shape[2], in_ref.shape[3] // 2
    copies = []
    for role in range(ROLES):
        for part in range(2):
            source = in_ref.at[role, :, :, pl.ds(part * q, q)]
            target = out_ref.at[part, :, pl.ds(role * fl, fl), :]
            copies.append(pltpu.make_async_copy(source, target, sems.at[len(copies)]))
            copies[-1].start()
    for copy in copies:
        copy.wait()


def call(kernel, name, outs, in_specs, scratch=(), out_specs=None):
    return pl.pallas_call(
        kernel,
        out_shape=outs,
        in_specs=in_specs,
        out_specs=jax.tree.map(lambda _: VMEM, outs) if out_specs is None else out_specs,
        scratch_shapes=list(scratch),
        name=name,
        compiler_params=pltpu.CompilerParams(vmem_limit_bytes=24 * 1024 * 1024),
    )


def on_device(n, nf, blended, estimate, partner, delays, levels):
    q, fl = estimate.shape[3], estimate.shape[2] // ROLES
    shape = jax.ShapeDtypeStruct
    block = (SHOTS_DEV, fl, 2 * q)
    side = shape((2, SHOTS_DEV * fl + 16, 2 * q), bf16)
    size = 8 * nf * ROLES * fl * q
    parts_shape = shape((ROLES * nf, 16, 128), f32)
    forward, backward = receiver_tables(q, 1.0), receiver_tables(q, -1.0)
    before = [(i, (i - 1) % n) for i in range(n)]
    after = [(i, (i + 1) % n) for i in range(n)]

    slabs = 2 * SHOTS_DEV * (2 * q // 128)
    packed = call(
        pack_kernel,
        "pack",
        shape((ROLES, slabs + 1, fl, 128), bf16),
        [HBM] * 4,
        [
            pltpu.SMEM(partner.shape, jnp.int32),
            pltpu.SMEM(delays.shape, jnp.int32),
            pltpu.SemaphoreType.DMA((4 * ROLES * (q // 128),)),
            pltpu.SemaphoreType.DMA((2,)),
        ],
    )(*[pltpu.with_memory_space_constraint(x, pltpu.HBM) for x in (estimate, blended, partner, delays)])
    gathered = lax.all_to_all(packed, GROUP, 0, 0, tiled=True)
    z, meta, phase, zs, b_even, b_odd = call(
        first_kernel,
        "first",
        (
            shape((2, 2, *block), f32),
            shape((ROLES, 16, 128), f32),
            shape((2, fl, 128), f32),
            shape((2, 2, *block), bf16),
            side,
            side,
        ),
        [VMEM, VMEM],
        [pltpu.VMEM((2, 2, *block), f32)] * 2,
    )(gathered, jnp.asarray(forward))
    down = lax.ppermute(zs, "g", before)
    up = lax.ppermute(zs, "g", after)
    b_down = lax.ppermute(b_even, "g", before)
    b_up = lax.ppermute(b_odd, "g", after)
    parts, halo = call(
        functools.partial(wide_sums_kernel, n),
        "wide_sums",
        (parts_shape, shape((2, 2, 2, *block), f32)),
        [VMEM] * 3,
    )(z, up, down)
    parts = lax.all_to_all(parts, SUM_GROUP, 0, 0, tiled=True)
    x, parts = call(
        functools.partial(middle_kernel, n, size),
        "middle",
        (shape((2, 3, 8, fl, 2 * q), f32), parts_shape),
        [VMEM] * 3 + [SMEM] + [VMEM] * 6,
        [
            pltpu.VMEM((2, 4, *block), f32),
            pltpu.VMEM((ROLES, 16, 128), f32),
            pltpu.VMEM((2, fl, 128), f32),
            pltpu.VMEM((2, 2, *block), f32),
            pltpu.VMEM((2, 2, 1, *block), f32),
        ],
    )(z, halo, parts, levels, b_even, b_odd, meta, phase, b_up, b_down)
    parts = lax.all_to_all(parts, SUM_GROUP, 0, 0, tiled=True)
    out = call(
        functools.partial(last_kernel, n, size),
        "last",
        shape((ROLES, *block), bf16),
        [VMEM] * 2 + [SMEM] + [VMEM],
        [pltpu.VMEM((2, 2, *block), f32)],
    )(x, parts, levels, jnp.asarray(backward[:1]))
    out = lax.all_to_all(out, GROUP, 0, 0, tiled=True)
    return call(
        unpack_kernel,
        "unpack",
        shape(estimate.shape, bf16),
        [VMEM],
        [pltpu.SemaphoreType.DMA((2 * ROLES,))],
        HBM,
    )(out)


def solution(mesh):
    shots, nf = mesh.shape["shot"], mesh.shape["freq"]
    n = shots // 4
    fine = Mesh(mesh.devices.reshape(2, n, 2, nf), ("yh", "g", "h", "f"))
    spec = P(None, ("yh", "g", "h"), "f", None)
    return jax.shard_map(
        functools.partial(on_device, n, nf),
        mesh=fine,
        in_specs=(spec, spec, P(("yh", "g", "h")), P(), P()),
        out_specs=spec,
        check_vma=False,
    )
```

```python
import functools
import math

import jax
import jax.numpy as jnp
import numpy as np
from jax import lax
from jax.experimental import pallas as pl
from jax.experimental.pallas import tpu as pltpu
from jax.sharding import Mesh
from jax.sharding import PartitionSpec as P

NT = 1024
SHOTS_DEV = 4
ROLES = 4
RELAX = 0.5
LEVEL_SCALE = 0.25
TINY = 1e-37
ROOT8 = 1.0 / math.sqrt(8.0)
HALF_ROOT = math.sqrt(0.5)
TAPER = [math.sin(math.pi * (t + 0.5) / 8) ** 2 * ROOT8 for t in range(8)]
GROUP = ("yh", "h")
SUM_GROUP = ("yh", "h", "f")

f32 = jnp.float32
bf16 = jnp.bfloat16
VMEM = pl.BlockSpec(memory_space=pltpu.VMEM)
SMEM = pl.BlockSpec(memory_space=pltpu.SMEM)
HBM = pl.BlockSpec(memory_space=pltpu.HBM)


def receiver_tables(length, sign):
    k = np.arange(length)
    angle = 2.0 * np.pi / length * ((k[:, None] * k[None, :]) % length)
    c, s = np.cos(angle) / math.sqrt(length), sign * np.sin(angle) / math.sqrt(length)
    full = np.block([[c, -s], [s, c]]).astype(np.float32)
    high = full.astype(jnp.bfloat16)
    low = (full - high.astype(np.float32)).astype(jnp.bfloat16)
    return np.stack([high, low])


def add(a, b):
    return (a[0] + b[0], a[1] + b[1])


def sub(a, b):
    return (a[0] - b[0], a[1] - b[1])


def add_turned(a, b, sign):
    return (a[0] + b[1], a[1] - b[0]) if sign > 0 else (a[0] - b[1], a[1] + b[0])


def eighth(a, sign):
    re, im = a
    if sign > 0:
        return ((re + im) * HALF_ROOT, (im - re) * HALF_ROOT)
    return ((re - im) * HALF_ROOT, (im + re) * HALF_ROOT)


def dft4(a, b, c, d, sign):
    s0, s1, s2, s3 = add(a, c), sub(a, c), add(b, d), sub(b, d)
    return [add(s0, s2), add_turned(s1, s3, sign), sub(s0, s2), add_turned(s1, s3, -sign)]


def dft8(x, sign, part="both"):
    even = dft4(x[0], x[2], x[4], x[6], sign)
    odd = dft4(x[1], x[3], x[5], x[7], sign)
    one, three = eighth(odd[1], sign), eighth(odd[3], sign)
    out = []
    if part != "second":
        out += [add(even[0], odd[0]), add(even[1], one), add_turned(even[2], odd[2], sign), add_turned(even[3], three, sign)]
    if part != "first":
        out += [sub(even[0], odd[0]), sub(even[1], one), add_turned(even[2], odd[2], -sign), add_turned(even[3], three, -sign)]
    return out


def windowed(first, second, scale):
    out = [(re * TAPER[t], im * TAPER[t]) for t, (re, im) in enumerate(first)]
    for t, (re, im) in enumerate(second):
        weight = TAPER[SHOTS_DEV + t] if scale is None else TAPER[SHOTS_DEV + t] * scale
        out.append((re * weight, im * weight))
    return out


def load(ref, at, rows, half, q, count=SHOTS_DEV):
    lo, hi = half * 128, q + half * 128
    return [(ref[(*at, t, rows, slice(lo, lo + 128))], ref[(*at, t, rows, slice(hi, hi + 128))]) for t in range(count)]


def store(ref, at, rows, half, q, block):
    for t, (re, im) in enumerate(block):
        ref[(*at, t, rows, slice(half * 128, half * 128 + 128))] = re
        ref[(*at, t, rows, slice(q + half * 128, q + half * 128 + 128))] = im


def seams(n):
    g = lax.axis_index("g")
    return jnp.where(g == 0, 0.0, 1.0), jnp.where(g == n - 1, 0.0, 1.0)


def seam_scale(marks, ab, w, wide):
    before, after = (1, 3) if wide else (0, 2)
    return marks[0] if (ab == 0 and w == before) else marks[1] if (ab == 1 and w == after) else None


def blocks_of(z_ref, halo_ref, ab, rows, half, q, wide):
    before = [load(halo_ref, (0, ab, k), rows, half, q) for k in range(2 if wide else 1)]
    own = [load(z_ref, (ab, k), rows, half, q) for k in range(2)]
    after = [load(halo_ref, (1, ab, k), rows, half, q) for k in range(2 if wide else 1)]
    return before + own + after


def add_sums(n, z_ref, halo_ref, out_ref, wide, x_ref=None):
    fl, q = z_ref.shape[3], z_ref.shape[4] // 2
    marks = seams(n)
    count = 5 if wide else 3

    def body(i, totals):
        rows = pl.ds(pl.multiple_of(i * 8, 8), 8)
        totals = list(totals)
        for ab in range(2):
            for half in range(q // 128):
                blocks = blocks_of(z_ref, halo_ref, ab, rows, half, q, wide)
                for w in range(count):
                    x = dft8(windowed(blocks[w], blocks[w + 1], seam_scale(marks, ab, w, wide)), 1)
                    if x_ref is not None:
                        store(x_ref, (ab, w), rows, half, q, x)
                    for re, im in x:
                        square = re * re + im * im
                        totals[ab * count + w] += square * lax.rsqrt(jnp.maximum(square, TINY))
        return tuple(totals)

    totals = lax.fori_loop(0, fl // 8, body, (jnp.zeros((8, 128), f32),) * (2 * count))
    row = lax.broadcasted_iota(jnp.int32, (16, 128), 0)
    tile = jnp.zeros((16, 128), f32)
    for k, total in enumerate(totals):
        tile = jnp.where(row == k, jnp.sum(total, axis=0, keepdims=True), tile)
    for k in range(out_ref.shape[0]):
        out_ref[k] = tile


def shrink_windows(n, size, spectra_of, parts_ref, levels_ref, e_ref, wide):
    fl, q = e_ref.shape[3], e_ref.shape[4] // 2
    count = 5 if wide else 3
    marks = seams(n)
    tile = parts_ref[0]
    for k in range(1, parts_ref.shape[0]):
        tile = tile + parts_ref[k]
    total = jnp.sum(tile, axis=1, keepdims=True)
    lams = []
    for ab in range(2):
        for w in range(count):
            window = (2 * (ab * n + lax.axis_index("g")) + w - count // 2 + 4 * n) & (4 * n - 1)
            scale = LEVEL_SCALE / size * ROOT8 * levels_ref[window].astype(f32)
            lams.append(jnp.broadcast_to(total[count * ab + w : count * ab + w + 1, :] * scale, (8, 128)))

    def body(i, carry):
        rows = pl.ds(pl.multiple_of(i * 8, 8), 8)
        for ab in range(2):
            for half in range(q // 128):
                held = None
                for w, x in enumerate(spectra_of(ab, rows, half)):
                    scale = seam_scale(marks, ab, w, wide)
                    kept = []
                    for re, im in x:
                        inverse = lax.rsqrt(jnp.maximum(re * re + im * im, TINY))
                        factor = jnp.maximum(ROOT8 - lams[count * ab + w] * inverse, 0.0)
                        kept.append((re * factor, im * factor))
                    y = dft8(kept, -1, "second" if w == 0 else "first" if w == count - 1 else "both")
                    if w > 0:
                        store(e_ref, (ab, w - 1), rows, half, q, [add(c, d) for c, d in zip(held, y[:4])])
                        y = y[4:]
                    held = y if scale is None else [(re * scale, im * scale) for re, im in y]
        return carry

    lax.fori_loop(0, fl // 8, body, 0)


def pack_kernel(e_ref, b_ref, partner_ref, delays_ref, out_ref, partner_smem, delays_smem, sems, small_sems):
    fl = e_ref.shape[2] // ROLES
    columns = e_ref.shape[3] // 128
    small = [
        pltpu.make_async_copy(partner_ref, partner_smem, small_sems.at[0]),
        pltpu.make_async_copy(delays_ref, delays_smem, small_sems.at[1]),
    ]
    for copy in small:
        copy.start()
    copies = []
    for k, ref in enumerate((e_ref, b_ref)):
        for part in range(2):
            for half in range(columns):
                for role in range(ROLES):
                    source = ref.at[part, :, pl.ds(role * fl, fl), pl.ds(half * 128, 128)]
                    first = (part * columns + half) * 2 * SHOTS_DEV + k * SHOTS_DEV
                    target = out_ref.at[role, pl.ds(first, SHOTS_DEV)]
                    copies.append(pltpu.make_async_copy(source, target, sems.at[len(copies)]))
                    copies[-1].start()
    for copy in small:
        copy.wait()
    block = (lax.axis_index("yh") * lax.axis_size("g") + lax.axis_index("g")) * 2 + lax.axis_index("h")
    row = lax.broadcasted_iota(jnp.int32, (fl, 128), 0)
    meta = jnp.zeros((fl, 128), f32)
    for t in range(SHOTS_DEV):
        other = partner_smem[t]
        offset = (delays_smem[other] - delays_smem[block * SHOTS_DEV + t]) & (NT - 1)
        for i, value in enumerate((other & (SHOTS_DEV - 1), offset >> 5, offset & 31)):
            meta = jnp.where(row == 3 * t + i, value.astype(f32), meta)
    for role in range(ROLES):
        out_ref[role, 4 * SHOTS_DEV * columns] = meta.astype(bf16)
    for copy in copies:
        copy.wait()


def phases(index):
    quadrant = (index + 128) >> 8
    x = (index - (quadrant << 8)).astype(f32) * (2.0 * math.pi / NT)
    x2 = x * x
    s = x * (1 + x2 * (-1 / 6 + x2 * (1 / 120 + x2 * (-1 / 5040 + x2 * (1 / 362880)))))
    c = 1 + x2 * (-1 / 2 + x2 * (1 / 24 + x2 * (-1 / 720 + x2 * (1 / 40320))))
    swap = (quadrant & 1) == 1
    cos, sin = jnp.where(swap, s, c), jnp.where(swap, c, s)
    cos = jnp.where(((quadrant + 1) & 2) == 2, -cos, cos)
    sin = jnp.where((quadrant & 2) == 2, -sin, sin)
    return cos, sin


def fill_phases(metas, fl, phase_ref):
    lane = lax.broadcasted_iota(jnp.int32, (1, 128), 1)
    offsets = jnp.zeros((1, 128), jnp.int32)
    for m, meta in enumerate(metas):
        whole = meta.astype(jnp.int32)
        for t in range(SHOTS_DEV):
            offset = whole[3 * t + 1 : 3 * t + 2, :] * 32 + whole[3 * t + 2 : 3 * t + 3, :]
            offsets = jnp.where(lane == SHOTS_DEV * m + t, offset, offsets)
    freq = lax.axis_index("f") * (ROLES * fl) + (lax.axis_index("yh") * 2 + lax.axis_index("h")) * fl
    freq = freq + lax.broadcasted_iota(jnp.int32, (fl, 128), 0)
    cos, sin = phases((freq * offsets) & (NT - 1))
    phase_ref[0] = cos
    phase_ref[1] = sin


def relax(e_ref, ab, k, rows, b_of, meta_of, phase, column, emit):
    q = e_ref.shape[4] // 2
    slots = [jnp.broadcast_to(meta_of(t), (16, 128)) for t in range(SHOTS_DEV)]
    turns = [[jnp.broadcast_to(table[:, column + t : column + t + 1], (16, 128)) for table in phase] for t in range(SHOTS_DEV)]
    for half in range(q // 128):
        spans = (slice(half * 128, half * 128 + 128), slice(q + half * 128, q + half * 128 + 128))
        others = [[e_ref[1 - ab, k, j, rows, span] for span in spans] for j in range(SHOTS_DEV)]
        for t in range(SHOTS_DEV):
            cos, sin = turns[t]
            other = others[0]
            for j in range(1, SHOTS_DEV):
                other = [jnp.where(slots[t] == j, new, old) for old, new in zip(other, others[j])]
            shifted = (other[0] * cos + other[1] * sin, other[1] * cos - other[0] * sin)
            for span, shift in zip(spans, shifted):
                emit(t, span, RELAX * ((e_ref[ab, k, t, rows, span] + b_of(t, span)) - shift))


def first_kernel(in_ref, table_ref, z_ref, meta_ref, phase_ref, zs_ref, b_even_ref, b_odd_ref, e_ref, bh_ref):
    fl, q2 = in_ref.shape[2], table_ref.shape[1]
    high, low = table_ref[0], table_ref[1]
    slabs = 2 * SHOTS_DEV
    metas = []
    data = [in_ref[:, c * slabs : (c + 1) * slabs].reshape(ROLES * slabs * fl, 128) for c in range(q2 // 128)]
    data = jnp.concatenate(data, axis=1)
    both = jnp.dot(data, high, preferred_element_type=f32) + jnp.dot(data, low, preferred_element_type=f32)
    both = both.reshape(ROLES, 2, SHOTS_DEV, fl, q2)
    for src in range(ROLES):
        ab, p = src // 2, src % 2
        out = both[src]
        e_ref[ab, p] = out[0]
        bh_ref[ab, p] = out[1]
        raw = in_ref[src, slabs * (q2 // 128), :16, :]
        side = b_odd_ref if p else b_even_ref
        side[ab, : SHOTS_DEV * fl, :] = out[1].reshape(SHOTS_DEV * fl, q2).astype(bf16)
        side[ab, SHOTS_DEV * fl :, :] = jnp.concatenate([raw] * (q2 // 128), axis=1)
        metas.append(raw.astype(f32))
        meta_ref[src] = metas[-1]
    fill_phases(metas, fl, phase_ref)

    def body(i, carry):
        rows = pl.ds(pl.multiple_of(i * 16, 16), 16)
        phase = (phase_ref[0, rows, :], phase_ref[1, rows, :])
        for ab in range(2):
            for p in range(2):

                def emit(t, span, z):
                    z_ref[ab, p, t, rows, span] = z
                    zs_ref[ab, p, t, rows, span] = z.astype(bf16)

                relax(
                    e_ref,
                    ab,
                    p,
                    rows,
                    lambda t, span: bh_ref[ab, p, t, rows, span],
                    lambda t: meta_ref[2 * ab + p, 3 * t : 3 * t + 1, :],
                    phase,
                    SHOTS_DEV * (2 * ab + p),
                    emit,
                )
        return carry

    lax.fori_loop(0, fl // 16, body, 0)


def fetch_halo(n, up_ref, down_ref, halo_ref):
    g = lax.axis_index("g")
    for ab in range(2):
        halo_ref[0, ab] = up_ref[jnp.where(g == 0, 1 - ab, ab)].astype(f32)
        halo_ref[1, ab] = down_ref[jnp.where(g == n - 1, 1 - ab, ab)].astype(f32)


def wide_sums_kernel(n, z_ref, up_ref, down_ref, out_ref, halo_ref):
    fetch_halo(n, up_ref, down_ref, halo_ref)
    add_sums(n, z_ref, halo_ref, out_ref, True)


def middle_kernel(n, size, z_ref, up_ref, down_ref, parts_ref, levels_ref, b_even_ref, b_odd_ref, meta_ref, phase_ref,
                  b_up_ref, b_down_ref, x_out, parts_out, e_ref, far_meta_ref, far_ref, z2_ref, halo2_ref, halo_ref):
    fl, q = z_ref.shape[3], z_ref.shape[4] // 2
    fetch_halo(n, up_ref, down_ref, halo_ref)
    g = lax.axis_index("g")
    marks = seams(n)

    def spectra_of(ab, rows, half):
        blocks = blocks_of(z_ref, halo_ref, ab, rows, half, q, True)
        for w in range(5):
            yield dft8(windowed(blocks[w], blocks[w + 1], seam_scale(marks, ab, w, True)), 1)

    shrink_windows(n, size, spectra_of, parts_ref, levels_ref, e_ref, True)
    lanes = []
    for side, ref in enumerate((b_up_ref, b_down_ref)):
        for ab in range(2):
            lanes.append(jnp.where(g == (n - 1 if side else 0), 1 - ab, ab))
            far_meta_ref[2 * side + ab] = ref[lanes[-1], SHOTS_DEV * fl :, :128].astype(f32)
    fill_phases([far_meta_ref[m] for m in range(4)], fl, far_ref)

    def body(i, carry):
        rows = pl.ds(pl.multiple_of(i * 16, 16), 16)
        own = (phase_ref[0, rows, :], phase_ref[1, rows, :])
        far = (far_ref[0, rows, :], far_ref[1, rows, :])
        for ab in range(2):
            for k in range(4):
                side, p = k // 2, k - 1
                if k in (1, 2):
                    b_ref, lane, phase, m, metas = (b_odd_ref if p else b_even_ref), ab, own, 2 * ab + p, meta_ref
                else:
                    b_ref, lane, phase, m, metas = (b_down_ref if side else b_up_ref), lanes[2 * side + ab], far, 2 * side + ab, far_meta_ref

                def emit(t, span, z):
                    if k in (1, 2):
                        z2_ref[ab, p, t, rows, span] = z
                    else:
                        halo2_ref[side, ab, 0, t, rows, span] = z

                def b_of(t, span):
                    at = pl.ds(pl.multiple_of(i * 16 + t * fl, 16), 16)
                    return b_ref[lane, at, span].astype(f32)

                def meta_of(t):
                    return metas[m, 3 * t : 3 * t + 1, :]

                relax(e_ref, ab, k, rows, b_of, meta_of, phase, SHOTS_DEV * m, emit)
        return carry

    lax.fori_loop(0, fl // 16, body, 0)
    add_sums(n, z2_ref, halo2_ref, parts_out, False, x_out)


def last_kernel(n, size, x_ref, parts_ref, levels_ref, table_ref, out_ref, e_ref):
    fl, q2 = x_ref.shape[3], x_ref.shape[4]

    def spectra_of(ab, rows, half):
        for w in range(3):
            yield load(x_ref, (ab, w), rows, half, q2 // 2, 8)

    shrink_windows(n, size, spectra_of, parts_ref, levels_ref, e_ref, False)
    data = e_ref[...].reshape(ROLES * SHOTS_DEV * fl, q2).astype(bf16)
    out = jnp.dot(data, table_ref[0], preferred_element_type=f32)
    out_ref[...] = out.reshape(ROLES, SHOTS_DEV, fl, q2).astype(bf16)


def unpack_kernel(in_ref, out_ref, sems):
    fl, q = in_ref.shape[2], in_ref.shape[3] // 2
    copies = []
    for role in range(ROLES):
        for part in range(2):
            source = in_ref.at[role, :, :, pl.ds(part * q, q)]
            target = out_ref.at[part, :, pl.ds(role * fl, fl), :]
            copies.append(pltpu.make_async_copy(source, target, sems.at[len(copies)]))
            copies[-1].start()
    for copy in copies:
        copy.wait()


def call(kernel, name, outs, in_specs, scratch=(), out_specs=None):
    return pl.pallas_call(
        kernel,
        out_shape=outs,
        in_specs=in_specs,
        out_specs=jax.tree.map(lambda _: VMEM, outs) if out_specs is None else out_specs,
        scratch_shapes=list(scratch),
        name=name,
        compiler_params=pltpu.CompilerParams(vmem_limit_bytes=24 * 1024 * 1024),
    )


def on_device(n, nf, blended, estimate, partner, delays, levels):
    q, fl = estimate.shape[3], estimate.shape[2] // ROLES
    shape = jax.ShapeDtypeStruct
    block = (SHOTS_DEV, fl, 2 * q)
    side = shape((2, SHOTS_DEV * fl + 16, 2 * q), bf16)
    size = 8 * nf * ROLES * fl * q
    parts_shape = shape((ROLES * nf, 16, 128), f32)
    forward, backward = receiver_tables(q, 1.0), receiver_tables(q, -1.0)
    before = [(i, (i - 1) % n) for i in range(n)]
    after = [(i, (i + 1) % n) for i in range(n)]

    slabs = 2 * SHOTS_DEV * (2 * q // 128)
    packed = call(
        pack_kernel,
        "pack",
        shape((ROLES, slabs + 1, fl, 128), bf16),
        [HBM] * 4,
        [
            pltpu.SMEM(partner.shape, jnp.int32),
            pltpu.SMEM(delays.shape, jnp.int32),
            pltpu.SemaphoreType.DMA((4 * ROLES * (q // 128),)),
            pltpu.SemaphoreType.DMA((2,)),
        ],
    )(*[pltpu.with_memory_space_constraint(x, pltpu.HBM) for x in (estimate, blended, partner, delays)])
    gathered = lax.all_to_all(packed, GROUP, 0, 0, tiled=True)
    z, meta, phase, zs, b_even, b_odd = call(
        first_kernel,
        "first",
        (
            shape((2, 2, *block), f32),
            shape((ROLES, 16, 128), f32),
            shape((2, fl, 128), f32),
            shape((2, 2, *block), bf16),
            side,
            side,
        ),
        [VMEM, VMEM],
        [pltpu.VMEM((2, 2, *block), f32)] * 2,
    )(gathered, jnp.asarray(forward))
    down = lax.ppermute(zs, "g", before)
    up = lax.ppermute(zs, "g", after)
    b_down = lax.ppermute(b_even, "g", before)
    b_up = lax.ppermute(b_odd, "g", after)
    far = pltpu.VMEM((2, 2, 2, *block), f32)
    parts = call(functools.partial(wide_sums_kernel, n), "wide_sums", parts_shape, [VMEM] * 3, [far])(z, up, down)
    parts = lax.all_to_all(parts, SUM_GROUP, 0, 0, tiled=True)
    x, parts = call(
        functools.partial(middle_kernel, n, size),
        "middle",
        (shape((2, 3, 8, fl, 2 * q), f32), parts_shape),
        [VMEM] * 4 + [SMEM] + [VMEM] * 6,
        [
            pltpu.VMEM((2, 4, *block), f32),
            pltpu.VMEM((ROLES, 16, 128), f32),
            pltpu.VMEM((2, fl, 128), f32),
            pltpu.VMEM((2, 2, *block), f32),
            pltpu.VMEM((2, 2, 1, *block), f32),
            far,
        ],
    )(z, up, down, parts, levels, b_even, b_odd, meta, phase, b_up, b_down)
    parts = lax.all_to_all(parts, SUM_GROUP, 0, 0, tiled=True)
    out = call(
        functools.partial(last_kernel, n, size),
        "last",
        shape((ROLES, *block), bf16),
        [VMEM] * 2 + [SMEM] + [VMEM],
        [pltpu.VMEM((2, 2, *block), f32)],
    )(x, parts, levels, jnp.asarray(backward[:1]))
    out = lax.all_to_all(out, GROUP, 0, 0, tiled=True)
    return call(
        unpack_kernel,
        "unpack",
        shape(estimate.shape, bf16),
        [VMEM],
        [pltpu.SemaphoreType.DMA((2 * ROLES,))],
        HBM,
    )(out)


def solution(mesh):
    shots, nf = mesh.shape["shot"], mesh.shape["freq"]
    n = shots // 4
    fine = Mesh(mesh.devices.reshape(2, n, 2, nf), ("yh", "g", "h", "f"))
    spec = P(None, ("yh", "g", "h"), "f", None)
    return jax.shard_map(
        functools.partial(on_device, n, nf),
        mesh=fine,
        in_specs=(spec, spec, P(("yh", "g", "h")), P(), P()),
        out_specs=spec,
        check_vma=False,
    )
```

```python
import functools
import math

import jax
import jax.numpy as jnp
import numpy as np
from jax import lax
from jax.experimental import pallas as pl
from jax.experimental.pallas import tpu as pltpu
from jax.sharding import Mesh
from jax.sharding import PartitionSpec as P

NT = 1024
SHOTS_DEV = 4
ROLES = 4
RELAX = 0.5
LEVEL_SCALE = 0.25
TINY = 1e-37
ROOT8 = 1.0 / math.sqrt(8.0)
HALF_ROOT = math.sqrt(0.5)
TAPER = [math.sin(math.pi * (t + 0.5) / 8) ** 2 * ROOT8 for t in range(8)]
STEPS = (0, 2, 3, 1)
GROUP = ("yh", "h")
SUM_GROUP = ("yh", "h", "f")

f32 = jnp.float32
bf16 = jnp.bfloat16
VMEM = pl.BlockSpec(memory_space=pltpu.VMEM)
SMEM = pl.BlockSpec(memory_space=pltpu.SMEM)
HBM = pl.BlockSpec(memory_space=pltpu.HBM)


def receiver_tables(length, sign):
    k = np.arange(length)
    angle = 2.0 * np.pi / length * ((k[:, None] * k[None, :]) % length)
    c, s = np.cos(angle) / math.sqrt(length), sign * np.sin(angle) / math.sqrt(length)
    full = np.block([[c, -s], [s, c]]).astype(np.float32)
    high = full.astype(jnp.bfloat16)
    low = (full - high.astype(np.float32)).astype(jnp.bfloat16)
    return np.stack([high, low])


def add(a, b):
    return (a[0] + b[0], a[1] + b[1])


def sub(a, b):
    return (a[0] - b[0], a[1] - b[1])


def add_turned(a, b, sign):
    return (a[0] + b[1], a[1] - b[0]) if sign > 0 else (a[0] - b[1], a[1] + b[0])


def eighth(a, sign):
    re, im = a
    if sign > 0:
        return ((re + im) * HALF_ROOT, (im - re) * HALF_ROOT)
    return ((re - im) * HALF_ROOT, (im + re) * HALF_ROOT)


def dft4(a, b, c, d, sign):
    s0, s1, s2, s3 = add(a, c), sub(a, c), add(b, d), sub(b, d)
    return [add(s0, s2), add_turned(s1, s3, sign), sub(s0, s2), add_turned(s1, s3, -sign)]


def dft8(x, sign, part="both"):
    even = dft4(x[0], x[2], x[4], x[6], sign)
    odd = dft4(x[1], x[3], x[5], x[7], sign)
    one, three = eighth(odd[1], sign), eighth(odd[3], sign)
    out = []
    if part != "second":
        out += [add(even[0], odd[0]), add(even[1], one), add_turned(even[2], odd[2], sign), add_turned(even[3], three, sign)]
    if part != "first":
        out += [sub(even[0], odd[0]), sub(even[1], one), add_turned(even[2], odd[2], -sign), add_turned(even[3], three, -sign)]
    return out


def windowed(first, second, scale):
    out = [(re * TAPER[t], im * TAPER[t]) for t, (re, im) in enumerate(first)]
    for t, (re, im) in enumerate(second):
        weight = TAPER[SHOTS_DEV + t] if scale is None else TAPER[SHOTS_DEV + t] * scale
        out.append((re * weight, im * weight))
    return out


def load(ref, at, rows, half, q, count=SHOTS_DEV):
    lo, hi = half * 128, q + half * 128
    return [(ref[(*at, t, rows, slice(lo, lo + 128))], ref[(*at, t, rows, slice(hi, hi + 128))]) for t in range(count)]


def store(ref, at, rows, half, q, block):
    for t, (re, im) in enumerate(block):
        ref[(*at, t, rows, slice(half * 128, half * 128 + 128))] = re
        ref[(*at, t, rows, slice(q + half * 128, q + half * 128 + 128))] = im


def seams(n):
    g = lax.axis_index("g")
    return jnp.where(g == 0, 0.0, 1.0), jnp.where(g == n - 1, 0.0, 1.0)


def seam_scale(marks, ab, w, wide):
    before, after = (1, 3) if wide else (0, 2)
    return marks[0] if (ab == 0 and w == before) else marks[1] if (ab == 1 and w == after) else None


def blocks_of(z_ref, halo_ref, ab, rows, half, q, wide):
    before = [load(halo_ref, (0, ab, k), rows, half, q) for k in range(2 if wide else 1)]
    own = [load(z_ref, (ab, k), rows, half, q) for k in range(2)]
    after = [load(halo_ref, (1, ab, k), rows, half, q) for k in range(2 if wide else 1)]
    return before + own + after


def add_sums(n, z_ref, halo_ref, out_ref, wide, x_ref=None):
    fl, q = z_ref.shape[3], z_ref.shape[4] // 2
    marks = seams(n)
    count = 5 if wide else 3

    def body(i, totals):
        rows = pl.ds(pl.multiple_of(i * 8, 8), 8)
        totals = list(totals)
        for ab in range(2):
            for half in range(q // 128):
                blocks = blocks_of(z_ref, halo_ref, ab, rows, half, q, wide)
                for w in range(count):
                    x = dft8(windowed(blocks[w], blocks[w + 1], seam_scale(marks, ab, w, wide)), 1)
                    if x_ref is not None:
                        store(x_ref, (ab, w), rows, half, q, x)
                    for re, im in x:
                        square = re * re + im * im
                        totals[ab * count + w] += square * lax.rsqrt(jnp.maximum(square, TINY))
        return tuple(totals)

    totals = lax.fori_loop(0, fl // 8, body, (jnp.zeros((8, 128), f32),) * (2 * count))
    row = lax.broadcasted_iota(jnp.int32, (16, 128), 0)
    tile = jnp.zeros((16, 128), f32)
    for k, total in enumerate(totals):
        tile = jnp.where(row == k, jnp.sum(total, axis=0, keepdims=True), tile)
    for k in range(out_ref.shape[0]):
        out_ref[k] = tile


def shrink_windows(n, size, spectra_of, parts_ref, levels_ref, e_ref, wide):
    fl, q = e_ref.shape[3], e_ref.shape[4] // 2
    count = 5 if wide else 3
    marks = seams(n)
    tile = parts_ref[0]
    for k in range(1, parts_ref.shape[0]):
        tile = tile + parts_ref[k]
    total = jnp.sum(tile, axis=1, keepdims=True)
    lams = []
    for ab in range(2):
        for w in range(count):
            window = (2 * (ab * n + lax.axis_index("g")) + w - count // 2 + 4 * n) & (4 * n - 1)
            scale = LEVEL_SCALE / size * ROOT8 * levels_ref[window].astype(f32)
            lams.append(jnp.broadcast_to(total[count * ab + w : count * ab + w + 1, :] * scale, (8, 128)))

    def body(i, carry):
        rows = pl.ds(pl.multiple_of(i * 8, 8), 8)
        for ab in range(2):
            for half in range(q // 128):
                held = None
                for w, x in enumerate(spectra_of(ab, rows, half)):
                    scale = seam_scale(marks, ab, w, wide)
                    kept = []
                    for re, im in x:
                        inverse = lax.rsqrt(jnp.maximum(re * re + im * im, TINY))
                        factor = jnp.maximum(ROOT8 - lams[count * ab + w] * inverse, 0.0)
                        kept.append((re * factor, im * factor))
                    y = dft8(kept, -1, "second" if w == 0 else "first" if w == count - 1 else "both")
                    if w > 0:
                        store(e_ref, (ab, w - 1), rows, half, q, [add(c, d) for c, d in zip(held, y[:4])])
                        y = y[4:]
                    held = y if scale is None else [(re * scale, im * scale) for re, im in y]
        return carry

    lax.fori_loop(0, fl // 8, body, 0)


def place():
    return lax.axis_index("yh") * 2 + lax.axis_index("h")


def pack_kernel(e_ref, b_ref, partner_ref, delays_ref, *refs):
    outs, (partner_smem, delays_smem, sems, small_sems) = refs[:ROLES], refs[ROLES:]
    fl = e_ref.shape[2] // ROLES
    columns = e_ref.shape[3] // 128
    small = [
        pltpu.make_async_copy(partner_ref, partner_smem, small_sems.at[0]),
        pltpu.make_async_copy(delays_ref, delays_smem, small_sems.at[1]),
    ]
    for copy in small:
        copy.start()
    copies = []
    for k, ref in enumerate((e_ref, b_ref)):
        for part in range(2):
            for half in range(columns):
                for step in range(ROLES):
                    rows = pl.ds(pl.multiple_of((place() ^ step) * fl, fl), fl)
                    source = ref.at[part, :, rows, pl.ds(half * 128, 128)]
                    first = (part * columns + half) * 2 * SHOTS_DEV + k * SHOTS_DEV
                    target = outs[step].at[pl.ds(first, SHOTS_DEV)]
                    copies.append(pltpu.make_async_copy(source, target, sems.at[len(copies)]))
                    copies[-1].start()
    for copy in small:
        copy.wait()
    block = (lax.axis_index("yh") * lax.axis_size("g") + lax.axis_index("g")) * 2 + lax.axis_index("h")
    row = lax.broadcasted_iota(jnp.int32, (fl, 128), 0)
    meta = jnp.zeros((fl, 128), f32)
    for t in range(SHOTS_DEV):
        other = partner_smem[t]
        offset = (delays_smem[other] - delays_smem[block * SHOTS_DEV + t]) & (NT - 1)
        for i, value in enumerate((other & (SHOTS_DEV - 1), offset >> 5, offset & 31)):
            meta = jnp.where(row == 3 * t + i, value.astype(f32), meta)
    for out_ref in outs:
        out_ref[4 * SHOTS_DEV * columns] = meta.astype(bf16)
    for copy in copies:
        copy.wait()


def phases(index):
    quadrant = (index + 128) >> 8
    x = (index - (quadrant << 8)).astype(f32) * (2.0 * math.pi / NT)
    x2 = x * x
    s = x * (1 + x2 * (-1 / 6 + x2 * (1 / 120 + x2 * (-1 / 5040 + x2 * (1 / 362880)))))
    c = 1 + x2 * (-1 / 2 + x2 * (1 / 24 + x2 * (-1 / 720 + x2 * (1 / 40320))))
    swap = (quadrant & 1) == 1
    cos, sin = jnp.where(swap, s, c), jnp.where(swap, c, s)
    cos = jnp.where(((quadrant + 1) & 2) == 2, -cos, cos)
    sin = jnp.where((quadrant & 2) == 2, -sin, sin)
    return cos, sin


def fill_phases(metas, fl, phase_ref):
    lane = lax.broadcasted_iota(jnp.int32, (1, 128), 1)
    offsets = jnp.zeros((1, 128), jnp.int32)
    for m, meta in enumerate(metas):
        whole = meta.astype(jnp.int32)
        for t in range(SHOTS_DEV):
            offset = whole[3 * t + 1 : 3 * t + 2, :] * 32 + whole[3 * t + 2 : 3 * t + 3, :]
            offsets = jnp.where(lane == SHOTS_DEV * m + t, offset, offsets)
    freq = lax.axis_index("f") * (ROLES * fl) + (lax.axis_index("yh") * 2 + lax.axis_index("h")) * fl
    freq = freq + lax.broadcasted_iota(jnp.int32, (fl, 128), 0)
    cos, sin = phases((freq * offsets) & (NT - 1))
    phase_ref[0] = cos
    phase_ref[1] = sin


def relax(e_ref, ab, k, rows, b_of, meta_of, phase, column, emit):
    q = e_ref.shape[4] // 2
    slots = [jnp.broadcast_to(meta_of(t), (16, 128)) for t in range(SHOTS_DEV)]
    turns = [[jnp.broadcast_to(table[:, column + t : column + t + 1], (16, 128)) for table in phase] for t in range(SHOTS_DEV)]
    for half in range(q // 128):
        spans = (slice(half * 128, half * 128 + 128), slice(q + half * 128, q + half * 128 + 128))
        others = [[e_ref[1 - ab, k, j, rows, span] for span in spans] for j in range(SHOTS_DEV)]
        for t in range(SHOTS_DEV):
            cos, sin = turns[t]
            other = others[0]
            for j in range(1, SHOTS_DEV):
                other = [jnp.where(slots[t] == j, new, old) for old, new in zip(other, others[j])]
            shifted = (other[0] * cos + other[1] * sin, other[1] * cos - other[0] * sin)
            for span, shift in zip(spans, shifted):
                emit(t, span, RELAX * ((e_ref[ab, k, t, rows, span] + b_of(t, span)) - shift))


def first_kernel(own_ref, y_ref, yh_ref, h_ref, table_hbm, z_ref, meta_ref, phase_ref, zs_ref, b_even_ref, b_odd_ref,
                 e_ref, bh_ref, in_ref, table_ref, table_sem):
    tables = pltpu.make_async_copy(table_hbm, table_ref, table_sem)
    tables.start()
    for step, ref in zip(STEPS, (own_ref, y_ref, yh_ref, h_ref)):
        in_ref[place() ^ step] = ref[...]
    tables.wait()
    fl, q2 = in_ref.shape[2], table_ref.shape[1]
    high, low = table_ref[0], table_ref[1]
    slabs = 2 * SHOTS_DEV
    metas = []
    data = [in_ref[:, c * slabs : (c + 1) * slabs].reshape(ROLES * slabs * fl, 128) for c in range(q2 // 128)]
    data = jnp.concatenate(data, axis=1)
    both = jnp.dot(data, high, preferred_element_type=f32) + jnp.dot(data, low, preferred_element_type=f32)
    both = both.reshape(ROLES, 2, SHOTS_DEV, fl, q2)
    for src in range(ROLES):
        ab, p = src // 2, src % 2
        out = both[src]
        e_ref[ab, p] = out[0]
        bh_ref[ab, p] = out[1]
        raw = in_ref[src, slabs * (q2 // 128), :16, :]
        side = b_odd_ref if p else b_even_ref
        side[ab, : SHOTS_DEV * fl, :] = out[1].reshape(SHOTS_DEV * fl, q2).astype(bf16)
        side[ab, SHOTS_DEV * fl :, :] = jnp.concatenate([raw] * (q2 // 128), axis=1)
        metas.append(raw.astype(f32))
        meta_ref[src] = metas[-1]
    fill_phases(metas, fl, phase_ref)

    def body(i, carry):
        rows = pl.ds(pl.multiple_of(i * 16, 16), 16)
        phase = (phase_ref[0, rows, :], phase_ref[1, rows, :])
        for ab in range(2):
            for p in range(2):

                def emit(t, span, z):
                    z_ref[ab, p, t, rows, span] = z
                    zs_ref[ab, p, t, rows, span] = z.astype(bf16)

                relax(
                    e_ref,
                    ab,
                    p,
                    rows,
                    lambda t, span: bh_ref[ab, p, t, rows, span],
                    lambda t: meta_ref[2 * ab + p, 3 * t : 3 * t + 1, :],
                    phase,
                    SHOTS_DEV * (2 * ab + p),
                    emit,
                )
        return carry

    lax.fori_loop(0, fl // 16, body, 0)


def fetch_halo(n, up_ref, down_ref, halo_ref):
    g = lax.axis_index("g")
    for ab in range(2):
        halo_ref[0, ab] = up_ref[jnp.where(g == 0, 1 - ab, ab)].astype(f32)
        halo_ref[1, ab] = down_ref[jnp.where(g == n - 1, 1 - ab, ab)].astype(f32)


def wide_sums_kernel(n, z_ref, up_ref, down_ref, out_ref, halo_ref):
    fetch_halo(n, up_ref, down_ref, halo_ref)
    add_sums(n, z_ref, halo_ref, out_ref, True)


def middle_kernel(n, size, z_ref, up_ref, down_ref, parts_ref, levels_ref, b_even_ref, b_odd_ref, meta_ref, phase_ref,
                  b_up_ref, b_down_ref, x_out, parts_out, e_ref, far_meta_ref, far_ref, z2_ref, halo2_ref, halo_ref):
    fl, q = z_ref.shape[3], z_ref.shape[4] // 2
    fetch_halo(n, up_ref, down_ref, halo_ref)
    g = lax.axis_index("g")
    marks = seams(n)

    def spectra_of(ab, rows, half):
        blocks = blocks_of(z_ref, halo_ref, ab, rows, half, q, True)
        for w in range(5):
            yield dft8(windowed(blocks[w], blocks[w + 1], seam_scale(marks, ab, w, True)), 1)

    shrink_windows(n, size, spectra_of, parts_ref, levels_ref, e_ref, True)
    lanes = []
    for side, ref in enumerate((b_up_ref, b_down_ref)):
        for ab in range(2):
            lanes.append(jnp.where(g == (n - 1 if side else 0), 1 - ab, ab))
            far_meta_ref[2 * side + ab] = ref[lanes[-1], SHOTS_DEV * fl :, :128].astype(f32)
    fill_phases([far_meta_ref[m] for m in range(4)], fl, far_ref)

    def body(i, carry):
        rows = pl.ds(pl.multiple_of(i * 16, 16), 16)
        own = (phase_ref[0, rows, :], phase_ref[1, rows, :])
        far = (far_ref[0, rows, :], far_ref[1, rows, :])
        for ab in range(2):
            for k in range(4):
                side, p = k // 2, k - 1
                if k in (1, 2):
                    b_ref, lane, phase, m, metas = (b_odd_ref if p else b_even_ref), ab, own, 2 * ab + p, meta_ref
                else:
                    b_ref, lane, phase, m, metas = (b_down_ref if side else b_up_ref), lanes[2 * side + ab], far, 2 * side + ab, far_meta_ref

                def emit(t, span, z):
                    if k in (1, 2):
                        z2_ref[ab, p, t, rows, span] = z
                    else:
                        halo2_ref[side, ab, 0, t, rows, span] = z

                def b_of(t, span):
                    at = pl.ds(pl.multiple_of(i * 16 + t * fl, 16), 16)
                    return b_ref[lane, at, span].astype(f32)

                def meta_of(t):
                    return metas[m, 3 * t : 3 * t + 1, :]

                relax(e_ref, ab, k, rows, b_of, meta_of, phase, SHOTS_DEV * m, emit)
        return carry

    lax.fori_loop(0, fl // 16, body, 0)
    add_sums(n, z2_ref, halo2_ref, parts_out, False, x_out)


def last_kernel(n, size, x_ref, parts_ref, levels_ref, table_ref, out_ref, e_ref):
    fl, q2 = x_ref.shape[3], x_ref.shape[4]

    def spectra_of(ab, rows, half):
        for w in range(3):
            yield load(x_ref, (ab, w), rows, half, q2 // 2, 8)

    shrink_windows(n, size, spectra_of, parts_ref, levels_ref, e_ref, False)
    data = e_ref[...].reshape(ROLES * SHOTS_DEV * fl, q2).astype(bf16)
    out = jnp.dot(data, table_ref[0], preferred_element_type=f32)
    out_ref[...] = out.reshape(ROLES, SHOTS_DEV, fl, q2).astype(bf16)


def unpack_kernel(in_ref, out_ref, sems):
    fl, q = in_ref.shape[2], in_ref.shape[3] // 2
    copies = []
    for role in range(ROLES):
        for part in range(2):
            source = in_ref.at[role, :, :, pl.ds(part * q, q)]
            target = out_ref.at[part, :, pl.ds(role * fl, fl), :]
            copies.append(pltpu.make_async_copy(source, target, sems.at[len(copies)]))
            copies[-1].start()
    for copy in copies:
        copy.wait()


def call(kernel, name, outs, in_specs, scratch=(), out_specs=None):
    return pl.pallas_call(
        kernel,
        out_shape=outs,
        in_specs=in_specs,
        out_specs=jax.tree.map(lambda _: VMEM, outs) if out_specs is None else out_specs,
        scratch_shapes=list(scratch),
        name=name,
        compiler_params=pltpu.CompilerParams(vmem_limit_bytes=24 * 1024 * 1024),
    )


def on_device(n, nf, blended, estimate, partner, delays, levels):
    q, fl = estimate.shape[3], estimate.shape[2] // ROLES
    shape = jax.ShapeDtypeStruct
    block = (SHOTS_DEV, fl, 2 * q)
    side = shape((2, SHOTS_DEV * fl + 16, 2 * q), bf16)
    size = 8 * nf * ROLES * fl * q
    parts_shape = shape((ROLES * nf, 16, 128), f32)
    forward, backward = receiver_tables(q, 1.0), receiver_tables(q, -1.0)
    before = [(i, (i - 1) % n) for i in range(n)]
    after = [(i, (i + 1) % n) for i in range(n)]

    slabs = 2 * SHOTS_DEV * (2 * q // 128)
    packed = call(
        pack_kernel,
        "pack",
        (shape((slabs + 1, fl, 128), bf16),) * ROLES,
        [HBM] * 4,
        [
            pltpu.SMEM(partner.shape, jnp.int32),
            pltpu.SMEM(delays.shape, jnp.int32),
            pltpu.SemaphoreType.DMA((4 * ROLES * (q // 128),)),
            pltpu.SemaphoreType.DMA((2,)),
        ],
    )(*[pltpu.with_memory_space_constraint(x, pltpu.HBM) for x in (estimate, blended, partner, delays)])
    gathered = {0: packed[0]}
    for step in STEPS[1:]:
        gathered[step] = lax.ppermute(packed[step], GROUP, [(i, i ^ step) for i in range(ROLES)])
    z, meta, phase, zs, b_even, b_odd = call(
        first_kernel,
        "first",
        (
            shape((2, 2, *block), f32),
            shape((ROLES, 16, 128), f32),
            shape((2, fl, 128), f32),
            shape((2, 2, *block), bf16),
            side,
            side,
        ),
        [VMEM] * 4 + [HBM],
        [
            pltpu.VMEM((2, 2, *block), f32),
            pltpu.VMEM((2, 2, *block), f32),
            pltpu.VMEM((ROLES, slabs + 1, fl, 128), bf16),
            pltpu.VMEM(forward.shape, bf16),
            pltpu.SemaphoreType.DMA,
        ],
    )(*gathered.values(), pltpu.with_memory_space_constraint(jnp.asarray(forward), pltpu.HBM))
    down = lax.ppermute(zs, "g", before)
    up = lax.ppermute(zs, "g", after)
    b_down = lax.ppermute(b_even, "g", before)
    b_up = lax.ppermute(b_odd, "g", after)
    far = pltpu.VMEM((2, 2, 2, *block), f32)
    parts = call(functools.partial(wide_sums_kernel, n), "wide_sums", parts_shape, [VMEM] * 3, [far])(z, up, down)
    parts = lax.all_to_all(parts, SUM_GROUP, 0, 0, tiled=True)
    x, parts = call(
        functools.partial(middle_kernel, n, size),
        "middle",
        (shape((2, 3, 8, fl, 2 * q), f32), parts_shape),
        [VMEM] * 4 + [SMEM] + [VMEM] * 6,
        [
            pltpu.VMEM((2, 4, *block), f32),
            pltpu.VMEM((ROLES, 16, 128), f32),
            pltpu.VMEM((2, fl, 128), f32),
            pltpu.VMEM((2, 2, *block), f32),
            pltpu.VMEM((2, 2, 1, *block), f32),
            far,
        ],
    )(z, up, down, parts, levels, b_even, b_odd, meta, phase, b_up, b_down)
    parts = lax.all_to_all(parts, SUM_GROUP, 0, 0, tiled=True)
    out = call(
        functools.partial(last_kernel, n, size),
        "last",
        shape((ROLES, *block), bf16),
        [VMEM] * 2 + [SMEM] + [VMEM],
        [pltpu.VMEM((2, 2, *block), f32)],
    )(x, parts, levels, jnp.asarray(backward[:1]))
    out = lax.all_to_all(out, GROUP, 0, 0, tiled=True)
    return call(
        unpack_kernel,
        "unpack",
        shape(estimate.shape, bf16),
        [VMEM],
        [pltpu.SemaphoreType.DMA((2 * ROLES,))],
        HBM,
    )(out)


def solution(mesh):
    shots, nf = mesh.shape["shot"], mesh.shape["freq"]
    n = shots // 4
    fine = Mesh(mesh.devices.reshape(2, n, 2, nf), ("yh", "g", "h", "f"))
    spec = P(None, ("yh", "g", "h"), "f", None)
    return jax.shard_map(
        functools.partial(on_device, n, nf),
        mesh=fine,
        in_specs=(spec, spec, P(("yh", "g", "h")), P(), P()),
        out_specs=spec,
        check_vma=False,
    )
```

```python
import functools
import math

import jax
import jax.numpy as jnp
import numpy as np
from jax import lax
from jax.experimental import pallas as pl
from jax.experimental.pallas import tpu as pltpu
from jax.sharding import Mesh
from jax.sharding import PartitionSpec as P

NT = 1024
SHOTS_DEV = 4
ROLES = 4
RELAX = 0.5
LEVEL_SCALE = 0.25
TINY = 1e-37
ROOT8 = 1.0 / math.sqrt(8.0)
HALF_ROOT = math.sqrt(0.5)
TAPER = [math.sin(math.pi * (t + 0.5) / 8) ** 2 * ROOT8 for t in range(8)]
GROUP = ("yh", "h")
SUM_GROUP = ("yh", "h", "f")

f32 = jnp.float32
bf16 = jnp.bfloat16
VMEM = pl.BlockSpec(memory_space=pltpu.VMEM)
SMEM = pl.BlockSpec(memory_space=pltpu.SMEM)
HBM = pl.BlockSpec(memory_space=pltpu.HBM)


def receiver_tables(length, sign):
    k = np.arange(length)
    angle = 2.0 * np.pi / length * ((k[:, None] * k[None, :]) % length)
    c, s = np.cos(angle) / math.sqrt(length), sign * np.sin(angle) / math.sqrt(length)
    full = np.block([[c, -s], [s, c]]).astype(np.float32)
    high = full.astype(jnp.bfloat16)
    low = (full - high.astype(np.float32)).astype(jnp.bfloat16)
    return np.stack([high, low])


def add(a, b):
    return (a[0] + b[0], a[1] + b[1])


def sub(a, b):
    return (a[0] - b[0], a[1] - b[1])


def add_turned(a, b, sign):
    return (a[0] + b[1], a[1] - b[0]) if sign > 0 else (a[0] - b[1], a[1] + b[0])


def eighth(a, sign):
    re, im = a
    if sign > 0:
        return ((re + im) * HALF_ROOT, (im - re) * HALF_ROOT)
    return ((re - im) * HALF_ROOT, (im + re) * HALF_ROOT)


def dft4(a, b, c, d, sign):
    s0, s1, s2, s3 = add(a, c), sub(a, c), add(b, d), sub(b, d)
    return [add(s0, s2), add_turned(s1, s3, sign), sub(s0, s2), add_turned(s1, s3, -sign)]


def dft8(x, sign, part="both"):
    even = dft4(x[0], x[2], x[4], x[6], sign)
    odd = dft4(x[1], x[3], x[5], x[7], sign)
    one, three = eighth(odd[1], sign), eighth(odd[3], sign)
    out = []
    if part != "second":
        out += [add(even[0], odd[0]), add(even[1], one), add_turned(even[2], odd[2], sign), add_turned(even[3], three, sign)]
    if part != "first":
        out += [sub(even[0], odd[0]), sub(even[1], one), add_turned(even[2], odd[2], -sign), add_turned(even[3], three, -sign)]
    return out


def windowed(first, second, scale):
    out = [(re * TAPER[t], im * TAPER[t]) for t, (re, im) in enumerate(first)]
    for t, (re, im) in enumerate(second):
        weight = TAPER[SHOTS_DEV + t] if scale is None else TAPER[SHOTS_DEV + t] * scale
        out.append((re * weight, im * weight))
    return out


def load(ref, at, rows, half, q, count=SHOTS_DEV):
    lo, hi = half * 128, q + half * 128
    return [(ref[(*at, t, rows, slice(lo, lo + 128))], ref[(*at, t, rows, slice(hi, hi + 128))]) for t in range(count)]


def store(ref, at, rows, half, q, block):
    for t, (re, im) in enumerate(block):
        ref[(*at, t, rows, slice(half * 128, half * 128 + 128))] = re
        ref[(*at, t, rows, slice(q + half * 128, q + half * 128 + 128))] = im


def seams(n):
    g = lax.axis_index("g")
    return jnp.where(g == 0, 0.0, 1.0), jnp.where(g == n - 1, 0.0, 1.0)


def seam_scale(marks, ab, w, wide):
    before, after = (1, 3) if wide else (0, 2)
    return marks[0] if (ab == 0 and w == before) else marks[1] if (ab == 1 and w == after) else None


def blocks_of(z_ref, halo_ref, ab, rows, half, q, wide):
    before = [load(halo_ref, (0, ab, k), rows, half, q) for k in range(2 if wide else 1)]
    own = [load(z_ref, (ab, k), rows, half, q) for k in range(2)]
    after = [load(halo_ref, (1, ab, k), rows, half, q) for k in range(2 if wide else 1)]
    return before + own + after


def add_sums(n, z_ref, halo_ref, out_ref, wide, x_ref=None):
    fl, q = z_ref.shape[3], z_ref.shape[4] // 2
    marks = seams(n)
    count = 5 if wide else 3

    def body(i, totals):
        rows = pl.ds(pl.multiple_of(i * 8, 8), 8)
        totals = list(totals)
        for ab in range(2):
            for half in range(q // 128):
                blocks = blocks_of(z_ref, halo_ref, ab, rows, half, q, wide)
                for w in range(count):
                    x = dft8(windowed(blocks[w], blocks[w + 1], seam_scale(marks, ab, w, wide)), 1)
                    if x_ref is not None:
                        store(x_ref, (ab, w), rows, half, q, x)
                    for re, im in x:
                        square = re * re + im * im
                        totals[ab * count + w] += square * lax.rsqrt(jnp.maximum(square, TINY))
        return tuple(totals)

    totals = lax.fori_loop(0, fl // 8, body, (jnp.zeros((8, 128), f32),) * (2 * count))
    row = lax.broadcasted_iota(jnp.int32, (16, 128), 0)
    tile = jnp.zeros((16, 128), f32)
    for k, total in enumerate(totals):
        tile = jnp.where(row == k, jnp.sum(total, axis=0, keepdims=True), tile)
    for k in range(out_ref.shape[0]):
        out_ref[k] = tile


def shrink_windows(n, size, spectra_of, parts_ref, levels_ref, e_ref, wide):
    fl, q = e_ref.shape[3], e_ref.shape[4] // 2
    count = 5 if wide else 3
    marks = seams(n)
    tile = parts_ref[0]
    for k in range(1, parts_ref.shape[0]):
        tile = tile + parts_ref[k]
    total = jnp.sum(tile, axis=1, keepdims=True)
    lams = []
    for ab in range(2):
        for w in range(count):
            window = (2 * (ab * n + lax.axis_index("g")) + w - count // 2 + 4 * n) & (4 * n - 1)
            scale = LEVEL_SCALE / size * ROOT8 * levels_ref[window].astype(f32)
            lams.append(jnp.broadcast_to(total[count * ab + w : count * ab + w + 1, :] * scale, (8, 128)))

    def body(i, carry):
        rows = pl.ds(pl.multiple_of(i * 8, 8), 8)
        for ab in range(2):
            for half in range(q // 128):
                held = None
                for w, x in enumerate(spectra_of(ab, rows, half)):
                    scale = seam_scale(marks, ab, w, wide)
                    kept = []
                    for re, im in x:
                        inverse = lax.rsqrt(jnp.maximum(re * re + im * im, TINY))
                        factor = jnp.maximum(ROOT8 - lams[count * ab + w] * inverse, 0.0)
                        kept.append((re * factor, im * factor))
                    y = dft8(kept, -1, "second" if w == 0 else "first" if w == count - 1 else "both")
                    if w > 0:
                        store(e_ref, (ab, w - 1), rows, half, q, [add(c, d) for c, d in zip(held, y[:4])])
                        y = y[4:]
                    held = y if scale is None else [(re * scale, im * scale) for re, im in y]
        return carry

    lax.fori_loop(0, fl // 8, body, 0)


def pack_kernel(e_ref, b_ref, partner_ref, delays_ref, out_ref, partner_smem, delays_smem, sems, small_sems):
    fl = e_ref.shape[2] // ROLES
    columns = e_ref.shape[3] // 128
    small = [
        pltpu.make_async_copy(partner_ref, partner_smem, small_sems.at[0]),
        pltpu.make_async_copy(delays_ref, delays_smem, small_sems.at[1]),
    ]
    for copy in small:
        copy.start()
    copies = []
    for k, ref in enumerate((e_ref, b_ref)):
        for part in range(2):
            for half in range(columns):
                for role in range(ROLES):
                    source = ref.at[part, :, pl.ds(role * fl, fl), pl.ds(half * 128, 128)]
                    first = (part * columns + half) * 2 * SHOTS_DEV + k * SHOTS_DEV
                    target = out_ref.at[role, pl.ds(first, SHOTS_DEV)]
                    copies.append(pltpu.make_async_copy(source, target, sems.at[len(copies)]))
                    copies[-1].start()
    for copy in small:
        copy.wait()
    block = (lax.axis_index("yh") * lax.axis_size("g") + lax.axis_index("g")) * 2 + lax.axis_index("h")
    row = lax.broadcasted_iota(jnp.int32, (fl, 128), 0)
    meta = jnp.zeros((fl, 128), f32)
    for t in range(SHOTS_DEV):
        other = partner_smem[t]
        offset = (delays_smem[other] - delays_smem[block * SHOTS_DEV + t]) & (NT - 1)
        for i, value in enumerate((other & (SHOTS_DEV - 1), offset >> 5, offset & 31)):
            meta = jnp.where(row == 3 * t + i, value.astype(f32), meta)
    for role in range(ROLES):
        out_ref[role, 4 * SHOTS_DEV * columns] = meta.astype(bf16)
    for copy in copies:
        copy.wait()


def phases(index):
    quadrant = (index + 128) >> 8
    x = (index - (quadrant << 8)).astype(f32) * (2.0 * math.pi / NT)
    x2 = x * x
    s = x * (1 + x2 * (-1 / 6 + x2 * (1 / 120 + x2 * (-1 / 5040 + x2 * (1 / 362880)))))
    c = 1 + x2 * (-1 / 2 + x2 * (1 / 24 + x2 * (-1 / 720 + x2 * (1 / 40320))))
    swap = (quadrant & 1) == 1
    cos, sin = jnp.where(swap, s, c), jnp.where(swap, c, s)
    cos = jnp.where(((quadrant + 1) & 2) == 2, -cos, cos)
    sin = jnp.where((quadrant & 2) == 2, -sin, sin)
    return cos, sin


def fill_phases(metas, fl, phase_ref):
    lane = lax.broadcasted_iota(jnp.int32, (1, 128), 1)
    offsets = jnp.zeros((1, 128), jnp.int32)
    for m, meta in enumerate(metas):
        whole = meta.astype(jnp.int32)
        for t in range(SHOTS_DEV):
            offset = whole[3 * t + 1 : 3 * t + 2, :] * 32 + whole[3 * t + 2 : 3 * t + 3, :]
            offsets = jnp.where(lane == SHOTS_DEV * m + t, offset, offsets)
    freq = lax.axis_index("f") * (ROLES * fl) + (lax.axis_index("yh") * 2 + lax.axis_index("h")) * fl
    freq = freq + lax.broadcasted_iota(jnp.int32, (fl, 128), 0)
    cos, sin = phases((freq * offsets) & (NT - 1))
    phase_ref[0] = cos
    phase_ref[1] = sin


def relax(e_ref, ab, k, rows, b_of, meta_of, phase, column, emit):
    q = e_ref.shape[4] // 2
    slots = [jnp.broadcast_to(meta_of(t), (16, 128)) for t in range(SHOTS_DEV)]
    turns = [[jnp.broadcast_to(table[:, column + t : column + t + 1], (16, 128)) for table in phase] for t in range(SHOTS_DEV)]
    for half in range(q // 128):
        spans = (slice(half * 128, half * 128 + 128), slice(q + half * 128, q + half * 128 + 128))
        others = [[e_ref[1 - ab, k, j, rows, span] for span in spans] for j in range(SHOTS_DEV)]
        for t in range(SHOTS_DEV):
            cos, sin = turns[t]
            other = others[0]
            for j in range(1, SHOTS_DEV):
                other = [jnp.where(slots[t] == j, new, old) for old, new in zip(other, others[j])]
            shifted = (other[0] * cos + other[1] * sin, other[1] * cos - other[0] * sin)
            for span, shift in zip(spans, shifted):
                emit(t, span, RELAX * ((e_ref[ab, k, t, rows, span] + b_of(t, span)) - shift))


def first_kernel(in_ref, table_ref, z_ref, meta_ref, phase_ref, zs_ref, b_even_ref, b_odd_ref, e_ref, bh_ref):
    fl, q2 = in_ref.shape[2], table_ref.shape[1]
    high, low = table_ref[0], table_ref[1]
    slabs = 2 * SHOTS_DEV
    metas = []
    data = [in_ref[:, c * slabs : (c + 1) * slabs].reshape(ROLES * slabs * fl, 128) for c in range(q2 // 128)]
    data = jnp.concatenate(data, axis=1)
    both = jnp.dot(data, high, preferred_element_type=f32) + jnp.dot(data, low, preferred_element_type=f32)
    both = both.reshape(ROLES, 2, SHOTS_DEV, fl, q2)
    for src in range(ROLES):
        ab, p = src // 2, src % 2
        out = both[src]
        e_ref[ab, p] = out[0]
        bh_ref[ab, p] = out[1]
        raw = in_ref[src, slabs * (q2 // 128), :16, :]
        side = b_odd_ref if p else b_even_ref
        side[ab, : SHOTS_DEV * fl, :] = out[1].reshape(SHOTS_DEV * fl, q2).astype(bf16)
        side[ab, SHOTS_DEV * fl :, :] = jnp.concatenate([raw] * (q2 // 128), axis=1)
        metas.append(raw.astype(f32))
        meta_ref[src] = metas[-1]
    fill_phases(metas, fl, phase_ref)

    def body(i, carry):
        rows = pl.ds(pl.multiple_of(i * 16, 16), 16)
        phase = (phase_ref[0, rows, :], phase_ref[1, rows, :])
        for ab in range(2):
            for p in range(2):

                def emit(t, span, z):
                    z_ref[ab, p, t, rows, span] = z
                    zs_ref[ab, p, t, rows, span] = z.astype(bf16)

                relax(
                    e_ref,
                    ab,
                    p,
                    rows,
                    lambda t, span: bh_ref[ab, p, t, rows, span],
                    lambda t: meta_ref[2 * ab + p, 3 * t : 3 * t + 1, :],
                    phase,
                    SHOTS_DEV * (2 * ab + p),
                    emit,
                )
        return carry

    lax.fori_loop(0, fl // 16, body, 0)


def fetch_halo(n, up_ref, down_ref, cross_ref, halo_ref):
    g = lax.axis_index("g")
    row = n // 4
    for side, ref, at_edge, swapped in (
        (0, up_ref, g % row == 0, g == 0),
        (1, down_ref, g % row == row - 1, g == n - 1),
    ):

        @pl.when(jnp.logical_not(at_edge))
        def _(side=side, ref=ref):
            for ab in range(2):
                halo_ref[side, ab] = ref[ab].astype(f32)

        @pl.when(at_edge)
        def _(side=side, swapped=swapped):
            for ab in range(2):
                halo_ref[side, ab] = cross_ref[jnp.where(swapped, 1 - ab, ab)].astype(f32)


def wide_sums_kernel(n, z_ref, cross_ref, up_ref, down_ref, out_ref, halo_ref):
    fetch_halo(n, up_ref, down_ref, cross_ref, halo_ref)
    add_sums(n, z_ref, halo_ref, out_ref, True)


def middle_kernel(n, size, z_ref, up_ref, down_ref, cross_ref, parts_ref, levels_ref, b_even_ref, b_odd_ref, meta_ref, phase_ref,
                  b_up_ref, b_down_ref, x_out, parts_out, e_ref, far_meta_ref, far_ref, z2_ref, halo2_ref, halo_ref):
    fl, q = z_ref.shape[3], z_ref.shape[4] // 2
    fetch_halo(n, up_ref, down_ref, cross_ref, halo_ref)
    g = lax.axis_index("g")
    marks = seams(n)

    def spectra_of(ab, rows, half):
        blocks = blocks_of(z_ref, halo_ref, ab, rows, half, q, True)
        for w in range(5):
            yield dft8(windowed(blocks[w], blocks[w + 1], seam_scale(marks, ab, w, True)), 1)

    shrink_windows(n, size, spectra_of, parts_ref, levels_ref, e_ref, True)
    lanes = []
    for side, ref in enumerate((b_up_ref, b_down_ref)):
        for ab in range(2):
            lanes.append(jnp.where(g == (n - 1 if side else 0), 1 - ab, ab))
            far_meta_ref[2 * side + ab] = ref[lanes[-1], SHOTS_DEV * fl :, :128].astype(f32)
    fill_phases([far_meta_ref[m] for m in range(4)], fl, far_ref)

    def body(i, carry):
        rows = pl.ds(pl.multiple_of(i * 16, 16), 16)
        own = (phase_ref[0, rows, :], phase_ref[1, rows, :])
        far = (far_ref[0, rows, :], far_ref[1, rows, :])
        for ab in range(2):
            for k in range(4):
                side, p = k // 2, k - 1
                if k in (1, 2):
                    b_ref, lane, phase, m, metas = (b_odd_ref if p else b_even_ref), ab, own, 2 * ab + p, meta_ref
                else:
                    b_ref, lane, phase, m, metas = (b_down_ref if side else b_up_ref), lanes[2 * side + ab], far, 2 * side + ab, far_meta_ref

                def emit(t, span, z):
                    if k in (1, 2):
                        z2_ref[ab, p, t, rows, span] = z
                    else:
                        halo2_ref[side, ab, 0, t, rows, span] = z

                def b_of(t, span):
                    at = pl.ds(pl.multiple_of(i * 16 + t * fl, 16), 16)
                    return b_ref[lane, at, span].astype(f32)

                def meta_of(t):
                    return metas[m, 3 * t : 3 * t + 1, :]

                relax(e_ref, ab, k, rows, b_of, meta_of, phase, SHOTS_DEV * m, emit)
        return carry

    lax.fori_loop(0, fl // 16, body, 0)
    add_sums(n, z2_ref, halo2_ref, parts_out, False, x_out)


def last_kernel(n, size, x_ref, parts_ref, levels_ref, table_ref, out_ref, e_ref):
    fl, q2 = x_ref.shape[3], x_ref.shape[4]

    def spectra_of(ab, rows, half):
        for w in range(3):
            yield load(x_ref, (ab, w), rows, half, q2 // 2, 8)

    shrink_windows(n, size, spectra_of, parts_ref, levels_ref, e_ref, False)
    data = e_ref[...].reshape(ROLES * SHOTS_DEV * fl, q2).astype(bf16)
    out = jnp.dot(data, table_ref[0], preferred_element_type=f32)
    out_ref[...] = out.reshape(ROLES, SHOTS_DEV, fl, q2).astype(bf16)


def unpack_kernel(in_ref, out_ref, sems):
    fl, q = in_ref.shape[2], in_ref.shape[3] // 2
    copies = []
    for role in range(ROLES):
        for part in range(2):
            source = in_ref.at[role, :, :, pl.ds(part * q, q)]
            target = out_ref.at[part, :, pl.ds(role * fl, fl), :]
            copies.append(pltpu.make_async_copy(source, target, sems.at[len(copies)]))
            copies[-1].start()
    for copy in copies:
        copy.wait()


def call(kernel, name, outs, in_specs, scratch=(), out_specs=None):
    return pl.pallas_call(
        kernel,
        out_shape=outs,
        in_specs=in_specs,
        out_specs=jax.tree.map(lambda _: VMEM, outs) if out_specs is None else out_specs,
        scratch_shapes=list(scratch),
        name=name,
        compiler_params=pltpu.CompilerParams(vmem_limit_bytes=24 * 1024 * 1024),
    )


def on_device(n, nf, blended, estimate, partner, delays, levels):
    q, fl = estimate.shape[3], estimate.shape[2] // ROLES
    shape = jax.ShapeDtypeStruct
    block = (SHOTS_DEV, fl, 2 * q)
    side = shape((2, SHOTS_DEV * fl + 16, 2 * q), bf16)
    size = 8 * nf * ROLES * fl * q
    parts_shape = shape((ROLES * nf, 16, 128), f32)
    forward, backward = receiver_tables(q, 1.0), receiver_tables(q, -1.0)
    before = [(i, (i - 1) % n) for i in range(n)]
    after = [(i, (i + 1) % n) for i in range(n)]

    slabs = 2 * SHOTS_DEV * (2 * q // 128)
    packed = call(
        pack_kernel,
        "pack",
        shape((ROLES, slabs + 1, fl, 128), bf16),
        [HBM] * 4,
        [
            pltpu.SMEM(partner.shape, jnp.int32),
            pltpu.SMEM(delays.shape, jnp.int32),
            pltpu.SemaphoreType.DMA((4 * ROLES * (q // 128),)),
            pltpu.SemaphoreType.DMA((2,)),
        ],
    )(*[pltpu.with_memory_space_constraint(x, pltpu.HBM) for x in (estimate, blended, partner, delays)])
    gathered = lax.all_to_all(packed, GROUP, 0, 0, tiled=True)
    z, meta, phase, zs, b_even, b_odd = call(
        first_kernel,
        "first",
        (
            shape((2, 2, *block), f32),
            shape((ROLES, 16, 128), f32),
            shape((2, fl, 128), f32),
            shape((2, 2, *block), bf16),
            side,
            side,
        ),
        [VMEM, VMEM],
        [pltpu.VMEM((2, 2, *block), f32)] * 2,
    )(gathered, jnp.asarray(forward))
    row = n // 4
    down = lax.ppermute(zs, "g", [(i, j) for i, j in before if i % row > 0])
    up = lax.ppermute(zs, "g", [(i, j) for i, j in after if j % row > 0])
    cross = lax.ppermute(zs, "g", [(i, j) for i, j in before if i % row == 0] + [(i, j) for i, j in after if j % row == 0])
    b_down = lax.ppermute(b_even, "g", before)
    b_up = lax.ppermute(b_odd, "g", after)
    far = pltpu.VMEM((2, 2, 2, *block), f32)
    parts = call(functools.partial(wide_sums_kernel, n), "wide_sums", parts_shape, [VMEM] * 4, [far])(z, cross, up, down)
    parts = lax.all_to_all(parts, SUM_GROUP, 0, 0, tiled=True)
    x, parts = call(
        functools.partial(middle_kernel, n, size),
        "middle",
        (shape((2, 3, 8, fl, 2 * q), f32), parts_shape),
        [VMEM] * 5 + [SMEM] + [VMEM] * 6,
        [
            pltpu.VMEM((2, 4, *block), f32),
            pltpu.VMEM((ROLES, 16, 128), f32),
            pltpu.VMEM((2, fl, 128), f32),
            pltpu.VMEM((2, 2, *block), f32),
            pltpu.VMEM((2, 2, 1, *block), f32),
            far,
        ],
    )(z, up, down, cross, parts, levels, b_even, b_odd, meta, phase, b_up, b_down)
    parts = lax.all_to_all(parts, SUM_GROUP, 0, 0, tiled=True)
    out = call(
        functools.partial(last_kernel, n, size),
        "last",
        shape((ROLES, *block), bf16),
        [VMEM] * 2 + [SMEM] + [VMEM],
        [pltpu.VMEM((2, 2, *block), f32)],
    )(x, parts, levels, jnp.asarray(backward[:1]))
    out = lax.all_to_all(out, GROUP, 0, 0, tiled=True)
    return call(
        unpack_kernel,
        "unpack",
        shape(estimate.shape, bf16),
        [VMEM],
        [pltpu.SemaphoreType.DMA((2 * ROLES,))],
        HBM,
    )(out)


def solution(mesh):
    shots, nf = mesh.shape["shot"], mesh.shape["freq"]
    n = shots // 4
    fine = Mesh(mesh.devices.reshape(2, n, 2, nf), ("yh", "g", "h", "f"))
    spec = P(None, ("yh", "g", "h"), "f", None)
    return jax.shard_map(
        functools.partial(on_device, n, nf),
        mesh=fine,
        in_specs=(spec, spec, P(("yh", "g", "h")), P(), P()),
        out_specs=spec,
        check_vma=False,
    )
```

```python
import functools
import math

import jax
import jax.numpy as jnp
import numpy as np
from jax import lax
from jax.experimental import pallas as pl
from jax.experimental.pallas import tpu as pltpu
from jax.sharding import Mesh
from jax.sharding import PartitionSpec as P

NT = 1024
SHOTS_DEV = 4
ROLES = 4
RELAX = 0.5
LEVEL_SCALE = 0.25
TINY = 1e-37
ROOT8 = 1.0 / math.sqrt(8.0)
HALF_ROOT = math.sqrt(0.5)
TAPER = [math.sin(math.pi * (t + 0.5) / 8) ** 2 * ROOT8 for t in range(8)]
GROUP = ("yh", "h")
SUM_GROUP = ("yh", "h", "f")

f32 = jnp.float32
bf16 = jnp.bfloat16
VMEM = pl.BlockSpec(memory_space=pltpu.VMEM)
SMEM = pl.BlockSpec(memory_space=pltpu.SMEM)
HBM = pl.BlockSpec(memory_space=pltpu.HBM)


def receiver_tables(length, sign):
    k = np.arange(length)
    angle = 2.0 * np.pi / length * ((k[:, None] * k[None, :]) % length)
    c, s = np.cos(angle) / math.sqrt(length), sign * np.sin(angle) / math.sqrt(length)
    full = np.block([[c, -s], [s, c]]).astype(np.float32)
    high = full.astype(jnp.bfloat16)
    low = (full - high.astype(np.float32)).astype(jnp.bfloat16)
    return np.stack([high, low])


def add(a, b):
    return (a[0] + b[0], a[1] + b[1])


def sub(a, b):
    return (a[0] - b[0], a[1] - b[1])


def add_turned(a, b, sign):
    return (a[0] + b[1], a[1] - b[0]) if sign > 0 else (a[0] - b[1], a[1] + b[0])


def eighth(a, sign):
    re, im = a
    if sign > 0:
        return ((re + im) * HALF_ROOT, (im - re) * HALF_ROOT)
    return ((re - im) * HALF_ROOT, (im + re) * HALF_ROOT)


def dft4(a, b, c, d, sign):
    s0, s1, s2, s3 = add(a, c), sub(a, c), add(b, d), sub(b, d)
    return [add(s0, s2), add_turned(s1, s3, sign), sub(s0, s2), add_turned(s1, s3, -sign)]


def dft8(x, sign, part="both"):
    even = dft4(x[0], x[2], x[4], x[6], sign)
    odd = dft4(x[1], x[3], x[5], x[7], sign)
    one, three = eighth(odd[1], sign), eighth(odd[3], sign)
    out = []
    if part != "second":
        out += [add(even[0], odd[0]), add(even[1], one), add_turned(even[2], odd[2], sign), add_turned(even[3], three, sign)]
    if part != "first":
        out += [sub(even[0], odd[0]), sub(even[1], one), add_turned(even[2], odd[2], -sign), add_turned(even[3], three, -sign)]
    return out


def windowed(first, second, scale):
    out = [(re * TAPER[t], im * TAPER[t]) for t, (re, im) in enumerate(first)]
    for t, (re, im) in enumerate(second):
        weight = TAPER[SHOTS_DEV + t] if scale is None else TAPER[SHOTS_DEV + t] * scale
        out.append((re * weight, im * weight))
    return out


def load(ref, at, rows, half, q, count=SHOTS_DEV):
    lo, hi = half * 128, q + half * 128
    return [(ref[(*at, t, rows, slice(lo, lo + 128))], ref[(*at, t, rows, slice(hi, hi + 128))]) for t in range(count)]


def store(ref, at, rows, half, q, block):
    for t, (re, im) in enumerate(block):
        ref[(*at, t, rows, slice(half * 128, half * 128 + 128))] = re
        ref[(*at, t, rows, slice(q + half * 128, q + half * 128 + 128))] = im


def seams(n):
    g = lax.axis_index("g")
    return jnp.where(g == 0, 0.0, 1.0), jnp.where(g == n - 1, 0.0, 1.0)


def seam_scale(marks, ab, w, wide):
    before, after = (1, 3) if wide else (0, 2)
    return marks[0] if (ab == 0 and w == before) else marks[1] if (ab == 1 and w == after) else None


def blocks_of(z_ref, halo_ref, ab, rows, half, q, wide):
    before = [load(halo_ref, (0, ab, k), rows, half, q) for k in range(2 if wide else 1)]
    own = [load(z_ref, (ab, k), rows, half, q) for k in range(2)]
    after = [load(halo_ref, (1, ab, k), rows, half, q) for k in range(2 if wide else 1)]
    return before + own + after


def add_sums(n, z_ref, halo_ref, out_ref, wide, x_ref=None):
    fl, q = z_ref.shape[3], z_ref.shape[4] // 2
    marks = seams(n)
    count = 5 if wide else 3

    def body(i, totals):
        rows = pl.ds(pl.multiple_of(i * 8, 8), 8)
        totals = list(totals)
        for ab in range(2):
            for half in range(q // 128):
                blocks = blocks_of(z_ref, halo_ref, ab, rows, half, q, wide)
                for w in range(count):
                    x = dft8(windowed(blocks[w], blocks[w + 1], seam_scale(marks, ab, w, wide)), 1)
                    if x_ref is not None:
                        store(x_ref, (ab, w), rows, half, q, x)
                    for re, im in x:
                        square = re * re + im * im
                        totals[ab * count + w] += square * lax.rsqrt(jnp.maximum(square, TINY))
        return tuple(totals)

    totals = lax.fori_loop(0, fl // 8, body, (jnp.zeros((8, 128), f32),) * (2 * count))
    row = lax.broadcasted_iota(jnp.int32, (16, 128), 0)
    tile = jnp.zeros((16, 128), f32)
    for k, total in enumerate(totals):
        tile = jnp.where(row == k, jnp.sum(total, axis=0, keepdims=True), tile)
    for k in range(out_ref.shape[0]):
        out_ref[k] = tile


def shrink_windows(n, size, spectra_of, parts_ref, levels_ref, e_ref, wide):
    fl, q = e_ref.shape[3], e_ref.shape[4] // 2
    count = 5 if wide else 3
    marks = seams(n)
    tile = parts_ref[0]
    for k in range(1, parts_ref.shape[0]):
        tile = tile + parts_ref[k]
    total = jnp.sum(tile, axis=1, keepdims=True)
    lams = []
    for ab in range(2):
        for w in range(count):
            window = (2 * (ab * n + lax.axis_index("g")) + w - count // 2 + 4 * n) & (4 * n - 1)
            scale = LEVEL_SCALE / size * ROOT8 * levels_ref[window].astype(f32)
            lams.append(jnp.broadcast_to(total[count * ab + w : count * ab + w + 1, :] * scale, (8, 128)))

    def body(i, carry):
        rows = pl.ds(pl.multiple_of(i * 8, 8), 8)
        for ab in range(2):
            for half in range(q // 128):
                held = None
                for w, x in enumerate(spectra_of(ab, rows, half)):
                    scale = seam_scale(marks, ab, w, wide)
                    kept = []
                    for re, im in x:
                        inverse = lax.rsqrt(jnp.maximum(re * re + im * im, TINY))
                        factor = jnp.maximum(ROOT8 - lams[count * ab + w] * inverse, 0.0)
                        kept.append((re * factor, im * factor))
                    y = dft8(kept, -1, "second" if w == 0 else "first" if w == count - 1 else "both")
                    if w > 0:
                        store(e_ref, (ab, w - 1), rows, half, q, [add(c, d) for c, d in zip(held, y[:4])])
                        y = y[4:]
                    held = y if scale is None else [(re * scale, im * scale) for re, im in y]
        return carry

    lax.fori_loop(0, fl // 8, body, 0)


def pack_kernel(e_ref, b_ref, partner_ref, delays_ref, out_ref, partner_smem, delays_smem, sems, small_sems):
    fl = e_ref.shape[2] // ROLES
    columns = e_ref.shape[3] // 128
    small = [
        pltpu.make_async_copy(partner_ref, partner_smem, small_sems.at[0]),
        pltpu.make_async_copy(delays_ref, delays_smem, small_sems.at[1]),
    ]
    for copy in small:
        copy.start()
    copies = []
    for k, ref in enumerate((e_ref, b_ref)):
        for part in range(2):
            for half in range(columns):
                for role in range(ROLES):
                    source = ref.at[part, :, pl.ds(role * fl, fl), pl.ds(half * 128, 128)]
                    first = (part * columns + half) * 2 * SHOTS_DEV + k * SHOTS_DEV
                    target = out_ref.at[role, pl.ds(first, SHOTS_DEV)]
                    copies.append(pltpu.make_async_copy(source, target, sems.at[len(copies)]))
                    copies[-1].start()
    for copy in small:
        copy.wait()
    block = (lax.axis_index("yh") * lax.axis_size("g") + lax.axis_index("g")) * 2 + lax.axis_index("h")
    row = lax.broadcasted_iota(jnp.int32, (fl, 128), 0)
    meta = jnp.zeros((fl, 128), f32)
    for t in range(SHOTS_DEV):
        other = partner_smem[t]
        offset = (delays_smem[other] - delays_smem[block * SHOTS_DEV + t]) & (NT - 1)
        for i, value in enumerate((other & (SHOTS_DEV - 1), offset >> 5, offset & 31)):
            meta = jnp.where(row == 3 * t + i, value.astype(f32), meta)
    for role in range(ROLES):
        out_ref[role, 4 * SHOTS_DEV * columns] = meta.astype(bf16)
    for copy in copies:
        copy.wait()


def phases(index):
    quadrant = (index + 128) >> 8
    x = (index - (quadrant << 8)).astype(f32) * (2.0 * math.pi / NT)
    x2 = x * x
    s = x * (1 + x2 * (-1 / 6 + x2 * (1 / 120 + x2 * (-1 / 5040 + x2 * (1 / 362880)))))
    c = 1 + x2 * (-1 / 2 + x2 * (1 / 24 + x2 * (-1 / 720 + x2 * (1 / 40320))))
    swap = (quadrant & 1) == 1
    cos, sin = jnp.where(swap, s, c), jnp.where(swap, c, s)
    cos = jnp.where(((quadrant + 1) & 2) == 2, -cos, cos)
    sin = jnp.where((quadrant & 2) == 2, -sin, sin)
    return cos, sin


def fill_phases(metas, fl, phase_ref):
    lane = lax.broadcasted_iota(jnp.int32, (1, 128), 1)
    offsets = jnp.zeros((1, 128), jnp.int32)
    for m, meta in enumerate(metas):
        whole = meta.astype(jnp.int32)
        for t in range(SHOTS_DEV):
            offset = whole[3 * t + 1 : 3 * t + 2, :] * 32 + whole[3 * t + 2 : 3 * t + 3, :]
            offsets = jnp.where(lane == SHOTS_DEV * m + t, offset, offsets)
    freq = lax.axis_index("f") * (ROLES * fl) + (lax.axis_index("yh") * 2 + lax.axis_index("h")) * fl
    freq = freq + lax.broadcasted_iota(jnp.int32, (fl, 128), 0)
    cos, sin = phases((freq * offsets) & (NT - 1))
    phase_ref[0] = cos
    phase_ref[1] = sin


def relax(e_ref, ab, k, rows, b_of, meta_of, phase, column, emit):
    q = e_ref.shape[4] // 2
    slots = [jnp.broadcast_to(meta_of(t), (16, 128)) for t in range(SHOTS_DEV)]
    turns = [[jnp.broadcast_to(table[:, column + t : column + t + 1], (16, 128)) for table in phase] for t in range(SHOTS_DEV)]
    for half in range(q // 128):
        spans = (slice(half * 128, half * 128 + 128), slice(q + half * 128, q + half * 128 + 128))
        others = [[e_ref[1 - ab, k, j, rows, span] for span in spans] for j in range(SHOTS_DEV)]
        for t in range(SHOTS_DEV):
            cos, sin = turns[t]
            other = others[0]
            for j in range(1, SHOTS_DEV):
                other = [jnp.where(slots[t] == j, new, old) for old, new in zip(other, others[j])]
            shifted = (other[0] * cos + other[1] * sin, other[1] * cos - other[0] * sin)
            for span, shift in zip(spans, shifted):
                emit(t, span, RELAX * ((e_ref[ab, k, t, rows, span] + b_of(t, span)) - shift))


def first_kernel(in_ref, table_ref, z_ref, meta_ref, phase_ref, zs_ref, b_even_ref, b_odd_ref, e_ref, bh_ref):
    fl, q2 = in_ref.shape[2], table_ref.shape[1]
    high, low = table_ref[0], table_ref[1]
    slabs = 2 * SHOTS_DEV
    metas = []
    data = [in_ref[:, c * slabs : (c + 1) * slabs].reshape(ROLES * slabs * fl, 128) for c in range(q2 // 128)]
    data = jnp.concatenate(data, axis=1)
    both = jnp.dot(data, high, preferred_element_type=f32) + jnp.dot(data, low, preferred_element_type=f32)
    both = both.reshape(ROLES, 2, SHOTS_DEV, fl, q2)
    for src in range(ROLES):
        ab, p = src // 2, src % 2
        out = both[src]
        e_ref[ab, p] = out[0]
        bh_ref[ab, p] = out[1]
        raw = in_ref[src, slabs * (q2 // 128), :16, :]
        side = b_odd_ref if p else b_even_ref
        side[ab, : SHOTS_DEV * fl, :] = out[1].reshape(SHOTS_DEV * fl, q2).astype(bf16)
        side[ab, SHOTS_DEV * fl :, :] = jnp.concatenate([raw] * (q2 // 128), axis=1)
        metas.append(raw.astype(f32))
        meta_ref[src] = metas[-1]
    fill_phases(metas, fl, phase_ref)

    def body(i, carry):
        rows = pl.ds(pl.multiple_of(i * 16, 16), 16)
        phase = (phase_ref[0, rows, :], phase_ref[1, rows, :])
        for ab in range(2):
            for p in range(2):

                def emit(t, span, z):
                    z_ref[ab, p, t, rows, span] = z
                    zs_ref[ab, p, t, rows, span] = z.astype(bf16)

                relax(
                    e_ref,
                    ab,
                    p,
                    rows,
                    lambda t, span: bh_ref[ab, p, t, rows, span],
                    lambda t: meta_ref[2 * ab + p, 3 * t : 3 * t + 1, :],
                    phase,
                    SHOTS_DEV * (2 * ab + p),
                    emit,
                )
        return carry

    lax.fori_loop(0, fl // 16, body, 0)


def fetch_halo(n, up_ref, down_ref, cross_ref, halo_ref):
    g = lax.axis_index("g")
    row = n // 4
    for side, ref, at_edge, swapped in (
        (0, up_ref, g % row == 0, g == 0),
        (1, down_ref, g % row == row - 1, g == n - 1),
    ):

        @pl.when(jnp.logical_not(at_edge))
        def _(side=side, ref=ref):
            for ab in range(2):
                halo_ref[side, ab] = ref[ab].astype(f32)

        @pl.when(at_edge)
        def _(side=side, swapped=swapped):
            for ab in range(2):
                halo_ref[side, ab] = cross_ref[jnp.where(swapped, 1 - ab, ab)].astype(f32)


def wide_sums_kernel(n, z_ref, cross_ref, up_ref, down_ref, out_ref, halo_ref):
    fetch_halo(n, up_ref, down_ref, cross_ref, halo_ref)
    add_sums(n, z_ref, halo_ref, out_ref, True)


def middle_kernel(n, size, z_ref, up_ref, down_ref, cross_ref, parts_ref, levels_ref, b_even_ref, b_odd_ref, meta_ref, phase_ref,
                  b_up_ref, b_down_ref, x_out, parts_out, e_ref, far_meta_ref, far_ref, z2_ref, halo2_ref, halo_ref):
    fl, q = z_ref.shape[3], z_ref.shape[4] // 2
    fetch_halo(n, up_ref, down_ref, cross_ref, halo_ref)
    g = lax.axis_index("g")
    marks = seams(n)

    def spectra_of(ab, rows, half):
        blocks = blocks_of(z_ref, halo_ref, ab, rows, half, q, True)
        for w in range(5):
            yield dft8(windowed(blocks[w], blocks[w + 1], seam_scale(marks, ab, w, True)), 1)

    shrink_windows(n, size, spectra_of, parts_ref, levels_ref, e_ref, True)
    lanes = []
    for side, ref in enumerate((b_up_ref, b_down_ref)):
        for ab in range(2):
            lanes.append(jnp.where(g == (n - 1 if side else 0), 1 - ab, ab))
            far_meta_ref[2 * side + ab] = ref[lanes[-1], SHOTS_DEV * fl :, :128].astype(f32)
    fill_phases([far_meta_ref[m] for m in range(4)], fl, far_ref)

    def body(i, carry):
        rows = pl.ds(pl.multiple_of(i * 16, 16), 16)
        own = (phase_ref[0, rows, :], phase_ref[1, rows, :])
        far = (far_ref[0, rows, :], far_ref[1, rows, :])
        for ab in range(2):
            for k in range(4):
                side, p = k // 2, k - 1
                if k in (1, 2):
                    b_ref, lane, phase, m, metas = (b_odd_ref if p else b_even_ref), ab, own, 2 * ab + p, meta_ref
                else:
                    b_ref, lane, phase, m, metas = (b_down_ref if side else b_up_ref), lanes[2 * side + ab], far, 2 * side + ab, far_meta_ref

                def emit(t, span, z):
                    if k in (1, 2):
                        z2_ref[ab, p, t, rows, span] = z
                    else:
                        halo2_ref[side, ab, 0, t, rows, span] = z

                def b_of(t, span):
                    at = pl.ds(pl.multiple_of(i * 16 + t * fl, 16), 16)
                    return b_ref[lane, at, span].astype(f32)

                def meta_of(t):
                    return metas[m, 3 * t : 3 * t + 1, :]

                relax(e_ref, ab, k, rows, b_of, meta_of, phase, SHOTS_DEV * m, emit)
        return carry

    lax.fori_loop(0, fl // 16, body, 0)
    add_sums(n, z2_ref, halo2_ref, parts_out, False, x_out)


def last_kernel(n, size, x_ref, parts_ref, levels_ref, table_ref, out_ref, e_ref):
    fl, q2 = x_ref.shape[3], x_ref.shape[4]

    def spectra_of(ab, rows, half):
        for w in range(3):
            yield load(x_ref, (ab, w), rows, half, q2 // 2, 8)

    shrink_windows(n, size, spectra_of, parts_ref, levels_ref, e_ref, False)
    data = e_ref[...].reshape(ROLES * SHOTS_DEV * fl, q2).astype(bf16)
    out = jnp.dot(data, table_ref[0], preferred_element_type=f32)
    out_ref[...] = out.reshape(ROLES, SHOTS_DEV, fl, q2).astype(bf16)


def unpack_kernel(in_ref, out_ref, sems):
    fl, q = in_ref.shape[2], in_ref.shape[3] // 2
    copies = []
    for role in range(ROLES):
        for part in range(2):
            source = in_ref.at[role, :, :, pl.ds(part * q, q)]
            target = out_ref.at[part, :, pl.ds(role * fl, fl), :]
            copies.append(pltpu.make_async_copy(source, target, sems.at[len(copies)]))
            copies[-1].start()
    for copy in copies:
        copy.wait()


def call(kernel, outs, in_specs, scratch=(), out_specs=None):
    return pl.pallas_call(
        kernel,
        out_shape=outs,
        in_specs=in_specs,
        out_specs=jax.tree.map(lambda _: VMEM, outs) if out_specs is None else out_specs,
        scratch_shapes=list(scratch),
        compiler_params=pltpu.CompilerParams(vmem_limit_bytes=24 * 1024 * 1024),
    )


def on_device(n, nf, blended, estimate, partner, delays, levels):
    q, fl = estimate.shape[3], estimate.shape[2] // ROLES
    shape = jax.ShapeDtypeStruct
    block = (SHOTS_DEV, fl, 2 * q)
    side = shape((2, SHOTS_DEV * fl + 16, 2 * q), bf16)
    size = 8 * nf * ROLES * fl * q
    parts_shape = shape((ROLES * nf, 16, 128), f32)
    forward, backward = receiver_tables(q, 1.0), receiver_tables(q, -1.0)
    before = [(i, (i - 1) % n) for i in range(n)]
    after = [(i, (i + 1) % n) for i in range(n)]

    slabs = 2 * SHOTS_DEV * (2 * q // 128)
    packed = call(
        pack_kernel,
        shape((ROLES, slabs + 1, fl, 128), bf16),
        [HBM] * 4,
        [
            pltpu.SMEM(partner.shape, jnp.int32),
            pltpu.SMEM(delays.shape, jnp.int32),
            pltpu.SemaphoreType.DMA((4 * ROLES * (q // 128),)),
            pltpu.SemaphoreType.DMA((2,)),
        ],
    )(*[pltpu.with_memory_space_constraint(x, pltpu.HBM) for x in (estimate, blended, partner, delays)])
    gathered = lax.all_to_all(packed, GROUP, 0, 0, tiled=True)
    z, meta, phase, zs, b_even, b_odd = call(
        first_kernel,
        (
            shape((2, 2, *block), f32),
            shape((ROLES, 16, 128), f32),
            shape((2, fl, 128), f32),
            shape((2, 2, *block), bf16),
            side,
            side,
        ),
        [VMEM, VMEM],
        [pltpu.VMEM((2, 2, *block), f32)] * 2,
    )(gathered, jnp.asarray(forward))
    row = n // 4
    down = lax.ppermute(zs, "g", [(i, j) for i, j in before if i % row > 0])
    up = lax.ppermute(zs, "g", [(i, j) for i, j in after if j % row > 0])
    ends = [(i, j) for i, j in before if i % row == 0] + [(i, j) for i, j in after if j % row == 0]
    cross = lax.ppermute(zs, "g", ends)
    b_down = lax.ppermute(b_even, "g", before)
    b_up = lax.ppermute(b_odd, "g", after)
    far = pltpu.VMEM((2, 2, 2, *block), f32)
    parts = call(functools.partial(wide_sums_kernel, n), parts_shape, [VMEM] * 4, [far])(z, cross, up, down)
    parts = lax.all_to_all(parts, SUM_GROUP, 0, 0, tiled=True)
    x, parts = call(
        functools.partial(middle_kernel, n, size),
        (shape((2, 3, 8, fl, 2 * q), f32), parts_shape),
        [VMEM] * 5 + [SMEM] + [VMEM] * 6,
        [
            pltpu.VMEM((2, 4, *block), f32),
            pltpu.VMEM((ROLES, 16, 128), f32),
            pltpu.VMEM((2, fl, 128), f32),
            pltpu.VMEM((2, 2, *block), f32),
            pltpu.VMEM((2, 2, 1, *block), f32),
            far,
        ],
    )(z, up, down, cross, parts, levels, b_even, b_odd, meta, phase, b_up, b_down)
    parts = lax.all_to_all(parts, SUM_GROUP, 0, 0, tiled=True)
    out = call(
        functools.partial(last_kernel, n, size),
        shape((ROLES, *block), bf16),
        [VMEM] * 2 + [SMEM] + [VMEM],
        [pltpu.VMEM((2, 2, *block), f32)],
    )(x, parts, levels, jnp.asarray(backward[:1]))
    out = lax.all_to_all(out, GROUP, 0, 0, tiled=True)
    return call(unpack_kernel, shape(estimate.shape, bf16), [VMEM], [pltpu.SemaphoreType.DMA((2 * ROLES,))], HBM)(out)


def solution(mesh):
    shots, nf = mesh.shape["shot"], mesh.shape["freq"]
    n = shots // 4
    fine = Mesh(mesh.devices.reshape(2, n, 2, nf), ("yh", "g", "h", "f"))
    spec = P(None, ("yh", "g", "h"), "f", None)
    return jax.shard_map(
        functools.partial(on_device, n, nf),
        mesh=fine,
        in_specs=(spec, spec, P(("yh", "g", "h")), P(), P()),
        out_specs=spec,
        check_vma=False,
    )
```

```python
import functools
import math

import jax
import jax.numpy as jnp
import numpy as np
from jax import lax
from jax.experimental import pallas as pl
from jax.experimental.pallas import tpu as pltpu
from jax.sharding import Mesh
from jax.sharding import PartitionSpec as P

NT = 1024
SHOTS_DEV = 4
ROLES = 4
RELAX = 0.5
LEVEL_SCALE = 0.25
TINY = 1e-37
ROOT8 = 1.0 / math.sqrt(8.0)
HALF_ROOT = math.sqrt(0.5)
TAPER = [math.sin(math.pi * (t + 0.5) / 8) ** 2 * ROOT8 for t in range(8)]
GROUP = ("yh", "h")
SUM_GROUP = ("yh", "h", "f")

f32 = jnp.float32
bf16 = jnp.bfloat16
VMEM = pl.BlockSpec(memory_space=pltpu.VMEM)
SMEM = pl.BlockSpec(memory_space=pltpu.SMEM)
HBM = pl.BlockSpec(memory_space=pltpu.HBM)


def receiver_tables(length, sign, gain):
    k = np.arange(length)
    angle = 2.0 * np.pi / length * ((k[:, None] * k[None, :]) % length)
    c, s = np.cos(angle) / math.sqrt(length), sign * np.sin(angle) / math.sqrt(length)
    full = (gain * np.block([[c, -s], [s, c]])).astype(np.float32)
    high = full.astype(jnp.bfloat16)
    low = (full - high.astype(np.float32)).astype(jnp.bfloat16)
    return np.stack([high, low])


def add(a, b):
    return (a[0] + b[0], a[1] + b[1])


def sub(a, b):
    return (a[0] - b[0], a[1] - b[1])


def add_turned(a, b, sign):
    return (a[0] + b[1], a[1] - b[0]) if sign > 0 else (a[0] - b[1], a[1] + b[0])


def eighth(a, sign):
    re, im = a
    if sign > 0:
        return ((re + im) * HALF_ROOT, (im - re) * HALF_ROOT)
    return ((re - im) * HALF_ROOT, (im + re) * HALF_ROOT)


def dft4(a, b, c, d, sign):
    s0, s1, s2, s3 = add(a, c), sub(a, c), add(b, d), sub(b, d)
    return [add(s0, s2), add_turned(s1, s3, sign), sub(s0, s2), add_turned(s1, s3, -sign)]


def dft8(x, sign, part="both"):
    even = dft4(x[0], x[2], x[4], x[6], sign)
    odd = dft4(x[1], x[3], x[5], x[7], sign)
    one, three = eighth(odd[1], sign), eighth(odd[3], sign)
    out = []
    if part != "second":
        out += [add(even[0], odd[0]), add(even[1], one), add_turned(even[2], odd[2], sign), add_turned(even[3], three, sign)]
    if part != "first":
        out += [sub(even[0], odd[0]), sub(even[1], one), add_turned(even[2], odd[2], -sign), add_turned(even[3], three, -sign)]
    return out


def windowed(first, second, scale):
    out = [(re * TAPER[t], im * TAPER[t]) for t, (re, im) in enumerate(first)]
    for t, (re, im) in enumerate(second):
        weight = TAPER[SHOTS_DEV + t] if scale is None else TAPER[SHOTS_DEV + t] * scale
        out.append((re * weight, im * weight))
    return out


def load(ref, at, rows, half, q, count=SHOTS_DEV):
    lo, hi = half * 128, q + half * 128
    return [(ref[(*at, t, rows, slice(lo, lo + 128))], ref[(*at, t, rows, slice(hi, hi + 128))]) for t in range(count)]


def store(ref, at, rows, half, q, block):
    for t, (re, im) in enumerate(block):
        ref[(*at, t, rows, slice(half * 128, half * 128 + 128))] = re
        ref[(*at, t, rows, slice(q + half * 128, q + half * 128 + 128))] = im


def seams(n):
    g = lax.axis_index("g")
    return jnp.where(g == 0, 0.0, 1.0), jnp.where(g == n - 1, 0.0, 1.0)


def seam_scale(marks, ab, w, wide):
    before, after = (1, 3) if wide else (0, 2)
    return marks[0] if (ab == 0 and w == before) else marks[1] if (ab == 1 and w == after) else None


def blocks_of(z_ref, halo_ref, ab, rows, half, q, wide):
    before = [load(halo_ref, (0, ab, k), rows, half, q) for k in range(2 if wide else 1)]
    own = [load(z_ref, (ab, k), rows, half, q) for k in range(2)]
    after = [load(halo_ref, (1, ab, k), rows, half, q) for k in range(2 if wide else 1)]
    return before + own + after


def add_sums(n, z_ref, halo_ref, out_ref, wide, x_ref=None):
    fl, q = z_ref.shape[3], z_ref.shape[4] // 2
    marks = seams(n)
    count = 5 if wide else 3

    def body(i, totals):
        rows = pl.ds(pl.multiple_of(i * 8, 8), 8)
        totals = list(totals)
        for ab in range(2):
            for half in range(q // 128):
                blocks = blocks_of(z_ref, halo_ref, ab, rows, half, q, wide)
                for w in range(count):
                    x = dft8(windowed(blocks[w], blocks[w + 1], seam_scale(marks, ab, w, wide)), 1)
                    if x_ref is not None:
                        store(x_ref, (ab, w), rows, half, q, x)
                    for re, im in x:
                        square = re * re + im * im
                        totals[ab * count + w] += square * lax.rsqrt(jnp.maximum(square, TINY))
        return tuple(totals)

    totals = lax.fori_loop(0, fl // 8, body, (jnp.zeros((8, 128), f32),) * (2 * count))
    row = lax.broadcasted_iota(jnp.int32, (16, 128), 0)
    tile = jnp.zeros((16, 128), f32)
    for k, total in enumerate(totals):
        tile = jnp.where(row == k, jnp.sum(total, axis=0, keepdims=True), tile)
    for k in range(out_ref.shape[0]):
        out_ref[k] = tile


def shrink_windows(n, size, spectra_of, parts_ref, levels_ref, e_ref, wide):
    fl, q = e_ref.shape[3], e_ref.shape[4] // 2
    count = 5 if wide else 3
    root = ROOT8 * RELAX if wide else ROOT8
    marks = seams(n)
    tile = parts_ref[0]
    for k in range(1, parts_ref.shape[0]):
        tile = tile + parts_ref[k]
    total = jnp.sum(tile, axis=1, keepdims=True)
    lams = []
    for ab in range(2):
        for w in range(count):
            window = (2 * (ab * n + lax.axis_index("g")) + w - count // 2 + 4 * n) & (4 * n - 1)
            scale = LEVEL_SCALE / size * root * levels_ref[window].astype(f32)
            lams.append(jnp.broadcast_to(total[count * ab + w : count * ab + w + 1, :] * scale, (8, 128)))

    def body(i, carry):
        rows = pl.ds(pl.multiple_of(i * 8, 8), 8)
        for ab in range(2):
            for half in range(q // 128):
                held = None
                for w, x in enumerate(spectra_of(ab, rows, half)):
                    scale = seam_scale(marks, ab, w, wide)
                    kept = []
                    for re, im in x:
                        inverse = lax.rsqrt(jnp.maximum(re * re + im * im, TINY))
                        factor = jnp.maximum(root - lams[count * ab + w] * inverse, 0.0)
                        kept.append((re * factor, im * factor))
                    y = dft8(kept, -1, "second" if w == 0 else "first" if w == count - 1 else "both")
                    if w > 0:
                        store(e_ref, (ab, w - 1), rows, half, q, [add(c, d) for c, d in zip(held, y[:4])])
                        y = y[4:]
                    held = y if scale is None else [(re * scale, im * scale) for re, im in y]
        return carry

    lax.fori_loop(0, fl // 8, body, 0)


def pack_kernel(e_ref, b_ref, partner_ref, delays_ref, out_ref, partner_smem, delays_smem, sems, small_sems):
    fl = e_ref.shape[2] // ROLES
    columns = e_ref.shape[3] // 128
    small = [
        pltpu.make_async_copy(partner_ref, partner_smem, small_sems.at[0]),
        pltpu.make_async_copy(delays_ref, delays_smem, small_sems.at[1]),
    ]
    for copy in small:
        copy.start()
    copies = []
    for k, ref in enumerate((e_ref, b_ref)):
        for part in range(2):
            for half in range(columns):
                for role in range(ROLES):
                    source = ref.at[part, :, pl.ds(role * fl, fl), pl.ds(half * 128, 128)]
                    first = (part * columns + half) * 2 * SHOTS_DEV + k * SHOTS_DEV
                    target = out_ref.at[role, pl.ds(first, SHOTS_DEV)]
                    copies.append(pltpu.make_async_copy(source, target, sems.at[len(copies)]))
                    copies[-1].start()
    for copy in small:
        copy.wait()
    block = (lax.axis_index("yh") * lax.axis_size("g") + lax.axis_index("g")) * 2 + lax.axis_index("h")
    row = lax.broadcasted_iota(jnp.int32, (fl, 128), 0)
    meta = jnp.zeros((fl, 128), f32)
    for t in range(SHOTS_DEV):
        other = partner_smem[t]
        offset = (delays_smem[other] - delays_smem[block * SHOTS_DEV + t]) & (NT - 1)
        for i, value in enumerate((other & (SHOTS_DEV - 1), offset >> 5, offset & 31)):
            meta = jnp.where(row == 3 * t + i, value.astype(f32), meta)
    for role in range(ROLES):
        out_ref[role, 4 * SHOTS_DEV * columns] = meta.astype(bf16)
    for copy in copies:
        copy.wait()


def phases(index):
    quadrant = (index + 128) >> 8
    x = (index - (quadrant << 8)).astype(f32) * (2.0 * math.pi / NT)
    x2 = x * x
    s = x * (1 + x2 * (-1 / 6 + x2 * (1 / 120 + x2 * (-1 / 5040 + x2 * (1 / 362880)))))
    c = 1 + x2 * (-1 / 2 + x2 * (1 / 24 + x2 * (-1 / 720 + x2 * (1 / 40320))))
    swap = (quadrant & 1) == 1
    cos, sin = jnp.where(swap, s, c), jnp.where(swap, c, s)
    cos = jnp.where(((quadrant + 1) & 2) == 2, -cos, cos)
    sin = jnp.where((quadrant & 2) == 2, -sin, sin)
    return cos, sin


def fill_phases(metas, fl, phase_ref):
    lane = lax.broadcasted_iota(jnp.int32, (1, 128), 1)
    offsets = jnp.zeros((1, 128), jnp.int32)
    for m, meta in enumerate(metas):
        whole = meta.astype(jnp.int32)
        for t in range(SHOTS_DEV):
            offset = whole[3 * t + 1 : 3 * t + 2, :] * 32 + whole[3 * t + 2 : 3 * t + 3, :]
            offsets = jnp.where(lane == SHOTS_DEV * m + t, offset, offsets)
    freq = lax.axis_index("f") * (ROLES * fl) + (lax.axis_index("yh") * 2 + lax.axis_index("h")) * fl
    freq = freq + lax.broadcasted_iota(jnp.int32, (fl, 128), 0)
    cos, sin = phases((freq * offsets) & (NT - 1))
    phase_ref[0] = cos
    phase_ref[1] = sin


def relax(e_ref, ab, k, rows, b_of, meta_of, phase, column, emit):
    q = e_ref.shape[4] // 2
    slots = [jnp.broadcast_to(meta_of(t), (16, 128)) for t in range(SHOTS_DEV)]
    turns = [[jnp.broadcast_to(table[:, column + t : column + t + 1], (16, 128)) for table in phase] for t in range(SHOTS_DEV)]
    for half in range(q // 128):
        spans = (slice(half * 128, half * 128 + 128), slice(q + half * 128, q + half * 128 + 128))
        others = [[e_ref[1 - ab, k, j, rows, span] for span in spans] for j in range(SHOTS_DEV)]
        for t in range(SHOTS_DEV):
            cos, sin = turns[t]
            other = others[0]
            for j in range(1, SHOTS_DEV):
                other = [jnp.where(slots[t] == j, new, old) for old, new in zip(other, others[j])]
            shifted = (other[0] * cos + other[1] * sin, other[1] * cos - other[0] * sin)
            for span, shift in zip(spans, shifted):
                emit(t, span, (e_ref[ab, k, t, rows, span] + b_of(t, span)) - shift)


def first_kernel(in_ref, table_ref, z_ref, meta_ref, phase_ref, zs_ref, b_even_ref, b_odd_ref, e_ref, bh_ref):
    fl, q2 = in_ref.shape[2], table_ref.shape[1]
    high, low = table_ref[0], table_ref[1]
    slabs = 2 * SHOTS_DEV
    metas = []
    data = [in_ref[:, c * slabs : (c + 1) * slabs].reshape(ROLES * slabs * fl, 128) for c in range(q2 // 128)]
    data = jnp.concatenate(data, axis=1)
    both = jnp.dot(data, high, preferred_element_type=f32) + jnp.dot(data, low, preferred_element_type=f32)
    both = both.reshape(ROLES, 2, SHOTS_DEV, fl, q2)
    for src in range(ROLES):
        ab, p = src // 2, src % 2
        out = both[src]
        e_ref[ab, p] = out[0]
        bh_ref[ab, p] = out[1]
        raw = in_ref[src, slabs * (q2 // 128), :16, :]
        side = b_odd_ref if p else b_even_ref
        side[ab, : SHOTS_DEV * fl, :] = out[1].reshape(SHOTS_DEV * fl, q2).astype(bf16)
        side[ab, SHOTS_DEV * fl :, :] = jnp.concatenate([raw] * (q2 // 128), axis=1)
        metas.append(raw.astype(f32))
        meta_ref[src] = metas[-1]
    fill_phases(metas, fl, phase_ref)

    def body(i, carry):
        rows = pl.ds(pl.multiple_of(i * 16, 16), 16)
        phase = (phase_ref[0, rows, :], phase_ref[1, rows, :])
        for ab in range(2):
            for p in range(2):

                def emit(t, span, z):
                    z_ref[ab, p, t, rows, span] = z
                    zs_ref[ab, p, t, rows, span] = z.astype(bf16)

                relax(
                    e_ref,
                    ab,
                    p,
                    rows,
                    lambda t, span: bh_ref[ab, p, t, rows, span],
                    lambda t: meta_ref[2 * ab + p, 3 * t : 3 * t + 1, :],
                    phase,
                    SHOTS_DEV * (2 * ab + p),
                    emit,
                )
        return carry

    lax.fori_loop(0, fl // 16, body, 0)


def wide_sums_kernel(n, z_ref, cross_ref, up_ref, down_ref, out_ref, near_ref, halo_ref):
    g = lax.axis_index("g")
    row = n // 4
    for side, ref, at_edge, swapped in (
        (0, up_ref, g % row == 0, g == 0),
        (1, down_ref, g % row == row - 1, g == n - 1),
    ):

        @pl.when(jnp.logical_not(at_edge))
        def _(side=side, ref=ref):
            for ab in range(2):
                near_ref[side, ab] = ref[ab]
                halo_ref[side, ab] = ref[ab].astype(f32)

        @pl.when(at_edge)
        def _(side=side, swapped=swapped):
            for ab in range(2):
                block = cross_ref[jnp.where(swapped, 1 - ab, ab)]
                near_ref[side, ab] = block
                halo_ref[side, ab] = block.astype(f32)

    add_sums(n, z_ref, halo_ref, out_ref, True)


def middle_kernel(n, size, z_ref, near_ref, parts_ref, levels_ref, b_even_ref, b_odd_ref, meta_ref, phase_ref,
                  b_up_ref, b_down_ref, x_out, parts_out, e_ref, far_meta_ref, far_ref, z2_ref, halo2_ref, halo_ref):
    fl, q = z_ref.shape[3], z_ref.shape[4] // 2
    halo_ref[...] = near_ref[...].astype(f32)
    g = lax.axis_index("g")
    marks = seams(n)

    def spectra_of(ab, rows, half):
        blocks = blocks_of(z_ref, halo_ref, ab, rows, half, q, True)
        for w in range(5):
            yield dft8(windowed(blocks[w], blocks[w + 1], seam_scale(marks, ab, w, True)), 1)

    shrink_windows(n, size, spectra_of, parts_ref, levels_ref, e_ref, True)
    lanes = []
    for side, ref in enumerate((b_up_ref, b_down_ref)):
        for ab in range(2):
            lanes.append(jnp.where(g == (n - 1 if side else 0), 1 - ab, ab))
            far_meta_ref[2 * side + ab] = ref[lanes[-1], SHOTS_DEV * fl :, :128].astype(f32)
    fill_phases([far_meta_ref[m] for m in range(4)], fl, far_ref)

    def body(i, carry):
        rows = pl.ds(pl.multiple_of(i * 16, 16), 16)
        own = (phase_ref[0, rows, :], phase_ref[1, rows, :])
        far = (far_ref[0, rows, :], far_ref[1, rows, :])
        for ab in range(2):
            for k in range(4):
                side, p = k // 2, k - 1
                if k in (1, 2):
                    b_ref, lane, phase, m, metas = (b_odd_ref if p else b_even_ref), ab, own, 2 * ab + p, meta_ref
                else:
                    b_ref, lane, phase, m, metas = (b_down_ref if side else b_up_ref), lanes[2 * side + ab], far, 2 * side + ab, far_meta_ref

                def emit(t, span, z):
                    if k in (1, 2):
                        z2_ref[ab, p, t, rows, span] = z
                    else:
                        halo2_ref[side, ab, 0, t, rows, span] = z

                def b_of(t, span):
                    at = pl.ds(pl.multiple_of(i * 16 + t * fl, 16), 16)
                    return b_ref[lane, at, span].astype(f32)

                def meta_of(t):
                    return metas[m, 3 * t : 3 * t + 1, :]

                relax(e_ref, ab, k, rows, b_of, meta_of, phase, SHOTS_DEV * m, emit)
        return carry

    lax.fori_loop(0, fl // 16, body, 0)
    add_sums(n, z2_ref, halo2_ref, parts_out, False, x_out)


def last_kernel(n, size, x_ref, parts_ref, levels_ref, table_ref, out_ref, e_ref):
    fl, q2 = x_ref.shape[3], x_ref.shape[4]

    def spectra_of(ab, rows, half):
        for w in range(3):
            yield load(x_ref, (ab, w), rows, half, q2 // 2, 8)

    shrink_windows(n, size, spectra_of, parts_ref, levels_ref, e_ref, False)
    data = e_ref[...].reshape(ROLES * SHOTS_DEV * fl, q2).astype(bf16)
    out = jnp.dot(data, table_ref[0], preferred_element_type=f32)
    out_ref[...] = out.reshape(ROLES, SHOTS_DEV, fl, q2).astype(bf16)


def unpack_kernel(in_ref, out_ref, sems):
    fl, q = in_ref.shape[2], in_ref.shape[3] // 2
    copies = []
    for role in range(ROLES):
        for part in range(2):
            source = in_ref.at[role, :, :, pl.ds(part * q, q)]
            target = out_ref.at[part, :, pl.ds(role * fl, fl), :]
            copies.append(pltpu.make_async_copy(source, target, sems.at[len(copies)]))
            copies[-1].start()
    for copy in copies:
        copy.wait()


def call(kernel, outs, in_specs, scratch=(), out_specs=None):
    return pl.pallas_call(
        kernel,
        out_shape=outs,
        in_specs=in_specs,
        out_specs=jax.tree.map(lambda _: VMEM, outs) if out_specs is None else out_specs,
        scratch_shapes=list(scratch),
        compiler_params=pltpu.CompilerParams(vmem_limit_bytes=24 * 1024 * 1024),
    )


def on_device(n, nf, blended, estimate, partner, delays, levels):
    q, fl = estimate.shape[3], estimate.shape[2] // ROLES
    shape = jax.ShapeDtypeStruct
    block = (SHOTS_DEV, fl, 2 * q)
    side = shape((2, SHOTS_DEV * fl + 16, 2 * q), bf16)
    size = 8 * nf * ROLES * fl * q
    parts_shape = shape((ROLES * nf, 16, 128), f32)
    forward, backward = receiver_tables(q, 1.0, RELAX), receiver_tables(q, -1.0, 1.0)
    before = [(i, (i - 1) % n) for i in range(n)]
    after = [(i, (i + 1) % n) for i in range(n)]

    slabs = 2 * SHOTS_DEV * (2 * q // 128)
    packed = call(
        pack_kernel,
        shape((ROLES, slabs + 1, fl, 128), bf16),
        [HBM] * 4,
        [
            pltpu.SMEM(partner.shape, jnp.int32),
            pltpu.SMEM(delays.shape, jnp.int32),
            pltpu.SemaphoreType.DMA((4 * ROLES * (q // 128),)),
            pltpu.SemaphoreType.DMA((2,)),
        ],
    )(*[pltpu.with_memory_space_constraint(x, pltpu.HBM) for x in (estimate, blended, partner, delays)])
    gathered = lax.all_to_all(packed, GROUP, 0, 0, tiled=True)
    z, meta, phase, zs, b_even, b_odd = call(
        first_kernel,
        (
            shape((2, 2, *block), f32),
            shape((ROLES, 16, 128), f32),
            shape((2, fl, 128), f32),
            shape((2, 2, *block), bf16),
            side,
            side,
        ),
        [VMEM, VMEM],
        [pltpu.VMEM((2, 2, *block), f32)] * 2,
    )(gathered, jnp.asarray(forward))
    row = n // 4
    down = lax.ppermute(zs, "g", [(i, j) for i, j in before if i % row > 0])
    up = lax.ppermute(zs, "g", [(i, j) for i, j in after if j % row > 0])
    ends = [(i, j) for i, j in before if i % row == 0] + [(i, j) for i, j in after if j % row == 0]
    cross = lax.ppermute(zs, "g", ends)
    b_down = lax.ppermute(b_even, "g", before)
    b_up = lax.ppermute(b_odd, "g", after)
    far = pltpu.VMEM((2, 2, 2, *block), f32)
    parts, near = call(
        functools.partial(wide_sums_kernel, n), (parts_shape, shape((2, 2, 2, *block), bf16)), [VMEM] * 4, [far]
    )(z, cross, up, down)
    parts = lax.all_to_all(parts, SUM_GROUP, 0, 0, tiled=True)
    x, parts = call(
        functools.partial(middle_kernel, n, size),
        (shape((2, 3, 8, fl, 2 * q), f32), parts_shape),
        [VMEM] * 3 + [SMEM] + [VMEM] * 6,
        [
            pltpu.VMEM((2, 4, *block), f32),
            pltpu.VMEM((ROLES, 16, 128), f32),
            pltpu.VMEM((2, fl, 128), f32),
            pltpu.VMEM((2, 2, *block), f32),
            pltpu.VMEM((2, 2, 1, *block), f32),
            far,
        ],
    )(z, near, parts, levels, b_even, b_odd, meta, phase, b_up, b_down)
    parts = lax.all_to_all(parts, SUM_GROUP, 0, 0, tiled=True)
    out = call(
        functools.partial(last_kernel, n, size),
        shape((ROLES, *block), bf16),
        [VMEM] * 2 + [SMEM] + [VMEM],
        [pltpu.VMEM((2, 2, *block), f32)],
    )(x, parts, levels, jnp.asarray(backward[:1]))
    out = lax.all_to_all(out, GROUP, 0, 0, tiled=True)
    return call(unpack_kernel, shape(estimate.shape, bf16), [VMEM], [pltpu.SemaphoreType.DMA((2 * ROLES,))], HBM)(out)


def solution(mesh):
    shots, nf = mesh.shape["shot"], mesh.shape["freq"]
    n = shots // 4
    fine = Mesh(mesh.devices.reshape(2, n, 2, nf), ("yh", "g", "h", "f"))
    spec = P(None, ("yh", "g", "h"), "f", None)
    return jax.shard_map(
        functools.partial(on_device, n, nf),
        mesh=fine,
        in_specs=(spec, spec, P(("yh", "g", "h")), P(), P()),
        out_specs=spec,
        check_vma=False,
    )
```

```python
import functools
import math

import jax
import jax.numpy as jnp
import numpy as np
from jax import lax
from jax.experimental import pallas as pl
from jax.experimental.pallas import tpu as pltpu
from jax.sharding import Mesh
from jax.sharding import PartitionSpec as P

NT = 1024
SHOTS_DEV = 4
ROLES = 4
RELAX = 0.5
LEVEL_SCALE = 0.25
TINY = 1e-37
ROOT8 = 1.0 / math.sqrt(8.0)
HALF_ROOT = math.sqrt(0.5)
TAPER = [math.sin(math.pi * (t + 0.5) / 8) ** 2 * ROOT8 for t in range(8)]
GROUP = ("yh", "h")
SUM_GROUP = ("yh", "h", "f")

f32 = jnp.float32
bf16 = jnp.bfloat16
VMEM = pl.BlockSpec(memory_space=pltpu.VMEM)
SMEM = pl.BlockSpec(memory_space=pltpu.SMEM)
HBM = pl.BlockSpec(memory_space=pltpu.HBM)


def receiver_tables(length, sign, gain):
    k = np.arange(length)
    angle = 2.0 * np.pi / length * ((k[:, None] * k[None, :]) % length)
    c, s = np.cos(angle) / math.sqrt(length), sign * np.sin(angle) / math.sqrt(length)
    full = (gain * np.block([[c, -s], [s, c]])).astype(np.float32)
    high = full.astype(jnp.bfloat16)
    low = (full - high.astype(np.float32)).astype(jnp.bfloat16)
    return np.stack([high, low])


def add(a, b):
    return (a[0] + b[0], a[1] + b[1])


def sub(a, b):
    return (a[0] - b[0], a[1] - b[1])


def add_turned(a, b, sign):
    return (a[0] + b[1], a[1] - b[0]) if sign > 0 else (a[0] - b[1], a[1] + b[0])


def eighth(a, sign):
    re, im = a
    if sign > 0:
        return ((re + im) * HALF_ROOT, (im - re) * HALF_ROOT)
    return ((re - im) * HALF_ROOT, (im + re) * HALF_ROOT)


def dft4(a, b, c, d, sign):
    s0, s1, s2, s3 = add(a, c), sub(a, c), add(b, d), sub(b, d)
    return [add(s0, s2), add_turned(s1, s3, sign), sub(s0, s2), add_turned(s1, s3, -sign)]


def dft8(x, sign, part="both"):
    even = dft4(x[0], x[2], x[4], x[6], sign)
    odd = dft4(x[1], x[3], x[5], x[7], sign)
    one, three = eighth(odd[1], sign), eighth(odd[3], sign)
    out = []
    if part != "second":
        out += [add(even[0], odd[0]), add(even[1], one), add_turned(even[2], odd[2], sign), add_turned(even[3], three, sign)]
    if part != "first":
        out += [sub(even[0], odd[0]), sub(even[1], one), add_turned(even[2], odd[2], -sign), add_turned(even[3], three, -sign)]
    return out


def windowed(first, second, scale):
    out = [(re * TAPER[t], im * TAPER[t]) for t, (re, im) in enumerate(first)]
    for t, (re, im) in enumerate(second):
        weight = TAPER[SHOTS_DEV + t] if scale is None else TAPER[SHOTS_DEV + t] * scale
        out.append((re * weight, im * weight))
    return out


def load(ref, at, rows, half, q, count=SHOTS_DEV):
    lo, hi = half * 128, q + half * 128
    return [(ref[(*at, t, rows, slice(lo, lo + 128))], ref[(*at, t, rows, slice(hi, hi + 128))]) for t in range(count)]


def store(ref, at, rows, half, q, block):
    for t, (re, im) in enumerate(block):
        ref[(*at, t, rows, slice(half * 128, half * 128 + 128))] = re
        ref[(*at, t, rows, slice(q + half * 128, q + half * 128 + 128))] = im


def seams(n):
    g = lax.axis_index("g")
    return jnp.where(g == 0, 0.0, 1.0), jnp.where(g == n - 1, 0.0, 1.0)


def seam_scale(marks, ab, w, wide):
    before, after = (1, 3) if wide else (0, 2)
    return marks[0] if (ab == 0 and w == before) else marks[1] if (ab == 1 and w == after) else None


def blocks_of(z_ref, halo_ref, ab, rows, half, q, wide):
    before = [load(halo_ref, (0, ab, k), rows, half, q) for k in range(2 if wide else 1)]
    own = [load(z_ref, (ab, k), rows, half, q) for k in range(2)]
    after = [load(halo_ref, (1, ab, k), rows, half, q) for k in range(2 if wide else 1)]
    return before + own + after


def add_sums(n, z_ref, halo_ref, out_ref, wide, x_ref=None):
    fl, q = z_ref.shape[3], z_ref.shape[4] // 2
    marks = seams(n)
    count = 5 if wide else 3

    def body(i, totals):
        rows = pl.ds(pl.multiple_of(i * 8, 8), 8)
        totals = list(totals)
        for ab in range(2):
            for half in range(q // 128):
                blocks = blocks_of(z_ref, halo_ref, ab, rows, half, q, wide)
                for w in range(count):
                    x = dft8(windowed(blocks[w], blocks[w + 1], seam_scale(marks, ab, w, wide)), 1)
                    if x_ref is not None:
                        store(x_ref, (ab, w), rows, half, q, x)
                    for re, im in x:
                        square = re * re + im * im
                        totals[ab * count + w] += square * lax.rsqrt(jnp.maximum(square, TINY))
        return tuple(totals)

    totals = lax.fori_loop(0, fl // 8, body, (jnp.zeros((8, 128), f32),) * (2 * count))
    row = lax.broadcasted_iota(jnp.int32, out_ref.shape[1:], 0)
    tile = jnp.zeros(out_ref.shape[1:], f32)
    for k, total in enumerate(totals):
        tile = jnp.where(row == k, jnp.sum(total, axis=0, keepdims=True), tile)
    for k in range(out_ref.shape[0]):
        out_ref[k] = tile


def shrink_windows(n, size, spectra_of, parts_ref, levels_ref, e_ref, wide):
    fl, q = e_ref.shape[3], e_ref.shape[4] // 2
    count = 5 if wide else 3
    root = ROOT8 * RELAX if wide else ROOT8
    marks = seams(n)
    tile = parts_ref[0]
    for k in range(1, parts_ref.shape[0]):
        tile = tile + parts_ref[k]
    total = jnp.sum(tile, axis=1, keepdims=True)
    lams = []
    for ab in range(2):
        for w in range(count):
            window = (2 * (ab * n + lax.axis_index("g")) + w - count // 2 + 4 * n) & (4 * n - 1)
            scale = LEVEL_SCALE / size * root * levels_ref[window].astype(f32)
            lams.append(jnp.broadcast_to(total[count * ab + w : count * ab + w + 1, :] * scale, (8, 128)))

    def body(i, carry):
        rows = pl.ds(pl.multiple_of(i * 8, 8), 8)
        for ab in range(2):
            for half in range(q // 128):
                held = None
                for w, x in enumerate(spectra_of(ab, rows, half)):
                    scale = seam_scale(marks, ab, w, wide)
                    kept = []
                    for re, im in x:
                        inverse = lax.rsqrt(jnp.maximum(re * re + im * im, TINY))
                        factor = jnp.maximum(root - lams[count * ab + w] * inverse, 0.0)
                        kept.append((re * factor, im * factor))
                    y = dft8(kept, -1, "second" if w == 0 else "first" if w == count - 1 else "both")
                    if w > 0:
                        store(e_ref, (ab, w - 1), rows, half, q, [add(c, d) for c, d in zip(held, y[:4])])
                        y = y[4:]
                    held = y if scale is None else [(re * scale, im * scale) for re, im in y]
        return carry

    lax.fori_loop(0, fl // 8, body, 0)


def pack_kernel(e_ref, b_ref, partner_ref, delays_ref, out_ref, partner_smem, delays_smem, sems, small_sems):
    fl = e_ref.shape[2] // ROLES
    columns = e_ref.shape[3] // 128
    small = [
        pltpu.make_async_copy(partner_ref, partner_smem, small_sems.at[0]),
        pltpu.make_async_copy(delays_ref, delays_smem, small_sems.at[1]),
    ]
    for copy in small:
        copy.start()
    copies = []
    for k, ref in enumerate((e_ref, b_ref)):
        for part in range(2):
            for half in range(columns):
                for role in range(ROLES):
                    source = ref.at[part, :, pl.ds(role * fl, fl), pl.ds(half * 128, 128)]
                    first = (part * columns + half) * 2 * SHOTS_DEV + k * SHOTS_DEV
                    target = out_ref.at[role, pl.ds(first, SHOTS_DEV)]
                    copies.append(pltpu.make_async_copy(source, target, sems.at[len(copies)]))
                    copies[-1].start()
    for copy in small:
        copy.wait()
    block = (lax.axis_index("yh") * lax.axis_size("g") + lax.axis_index("g")) * 2 + lax.axis_index("h")
    row = lax.broadcasted_iota(jnp.int32, (fl, 128), 0)
    meta = jnp.zeros((fl, 128), f32)
    for t in range(SHOTS_DEV):
        other = partner_smem[t]
        offset = (delays_smem[other] - delays_smem[block * SHOTS_DEV + t]) & (NT - 1)
        for i, value in enumerate((other & (SHOTS_DEV - 1), offset >> 5, offset & 31)):
            meta = jnp.where(row == 3 * t + i, value.astype(f32), meta)
    for role in range(ROLES):
        out_ref[role, 4 * SHOTS_DEV * columns] = meta.astype(bf16)
    for copy in copies:
        copy.wait()


def phases(index):
    quadrant = (index + 128) >> 8
    x = (index - (quadrant << 8)).astype(f32) * (2.0 * math.pi / NT)
    x2 = x * x
    s = x * (1 + x2 * (-1 / 6 + x2 * (1 / 120 + x2 * (-1 / 5040 + x2 * (1 / 362880)))))
    c = 1 + x2 * (-1 / 2 + x2 * (1 / 24 + x2 * (-1 / 720 + x2 * (1 / 40320))))
    swap = (quadrant & 1) == 1
    cos, sin = jnp.where(swap, s, c), jnp.where(swap, c, s)
    cos = jnp.where(((quadrant + 1) & 2) == 2, -cos, cos)
    sin = jnp.where((quadrant & 2) == 2, -sin, sin)
    return cos, sin


def fill_phases(metas, fl, phase_ref):
    lane = lax.broadcasted_iota(jnp.int32, (1, 128), 1)
    offsets = jnp.zeros((1, 128), jnp.int32)
    for m, meta in enumerate(metas):
        whole = meta.astype(jnp.int32)
        for t in range(SHOTS_DEV):
            offset = whole[3 * t + 1 : 3 * t + 2, :] * 32 + whole[3 * t + 2 : 3 * t + 3, :]
            offsets = jnp.where(lane == SHOTS_DEV * m + t, offset, offsets)
    freq = lax.axis_index("f") * (ROLES * fl) + (lax.axis_index("yh") * 2 + lax.axis_index("h")) * fl
    freq = freq + lax.broadcasted_iota(jnp.int32, (fl, 128), 0)
    cos, sin = phases((freq * offsets) & (NT - 1))
    phase_ref[0] = cos
    phase_ref[1] = sin


def relax(e_ref, ab, k, rows, b_of, meta_of, phase, column, emit):
    q = e_ref.shape[4] // 2
    slots = [jnp.broadcast_to(meta_of(t), (16, 128)) for t in range(SHOTS_DEV)]
    turns = [[jnp.broadcast_to(table[:, column + t : column + t + 1], (16, 128)) for table in phase] for t in range(SHOTS_DEV)]
    for half in range(q // 128):
        spans = (slice(half * 128, half * 128 + 128), slice(q + half * 128, q + half * 128 + 128))
        others = [[e_ref[1 - ab, k, j, rows, span] for span in spans] for j in range(SHOTS_DEV)]
        for t in range(SHOTS_DEV):
            cos, sin = turns[t]
            other = others[0]
            for j in range(1, SHOTS_DEV):
                other = [jnp.where(slots[t] == j, new, old) for old, new in zip(other, others[j])]
            shifted = (other[0] * cos + other[1] * sin, other[1] * cos - other[0] * sin)
            for span, shift in zip(spans, shifted):
                emit(t, span, (e_ref[ab, k, t, rows, span] + b_of(t, span)) - shift)


def first_kernel(in_ref, table_ref, z_ref, meta_ref, phase_ref, zs_ref, b_even_ref, b_odd_ref, e_ref, bh_ref):
    fl, q2 = in_ref.shape[2], table_ref.shape[1]
    high, low = table_ref[0], table_ref[1]
    slabs = 2 * SHOTS_DEV
    metas = []
    data = [in_ref[:, c * slabs : (c + 1) * slabs].reshape(ROLES * slabs * fl, 128) for c in range(q2 // 128)]
    data = jnp.concatenate(data, axis=1)
    both = jnp.dot(data, high, preferred_element_type=f32) + jnp.dot(data, low, preferred_element_type=f32)
    both = both.reshape(ROLES, 2, SHOTS_DEV, fl, q2)
    for src in range(ROLES):
        ab, p = src // 2, src % 2
        out = both[src]
        e_ref[ab, p] = out[0]
        bh_ref[ab, p] = out[1]
        raw = in_ref[src, slabs * (q2 // 128), :16, :]
        side = b_odd_ref if p else b_even_ref
        side[ab, : SHOTS_DEV * fl, :] = out[1].reshape(SHOTS_DEV * fl, q2).astype(bf16)
        side[ab, SHOTS_DEV * fl :, :] = jnp.concatenate([raw] * (q2 // 128), axis=1)
        metas.append(raw.astype(f32))
        meta_ref[src] = metas[-1]
    fill_phases(metas, fl, phase_ref)

    def body(i, carry):
        rows = pl.ds(pl.multiple_of(i * 16, 16), 16)
        phase = (phase_ref[0, rows, :], phase_ref[1, rows, :])
        for ab in range(2):
            for p in range(2):

                def emit(t, span, z):
                    z_ref[ab, p, t, rows, span] = z
                    zs_ref[ab, p, t, rows, span] = z.astype(bf16)

                relax(
                    e_ref,
                    ab,
                    p,
                    rows,
                    lambda t, span: bh_ref[ab, p, t, rows, span],
                    lambda t: meta_ref[2 * ab + p, 3 * t : 3 * t + 1, :],
                    phase,
                    SHOTS_DEV * (2 * ab + p),
                    emit,
                )
        return carry

    lax.fori_loop(0, fl // 16, body, 0)


def wide_sums_kernel(n, z_ref, cross_ref, up_ref, down_ref, out_ref, near_ref, halo_ref):
    g = lax.axis_index("g")
    row = n // 4
    for side, ref, at_edge, swapped in (
        (0, up_ref, g % row == 0, g == 0),
        (1, down_ref, g % row == row - 1, g == n - 1),
    ):

        @pl.when(jnp.logical_not(at_edge))
        def _(side=side, ref=ref):
            for ab in range(2):
                near_ref[side, ab] = ref[ab]
                halo_ref[side, ab] = ref[ab].astype(f32)

        @pl.when(at_edge)
        def _(side=side, swapped=swapped):
            for ab in range(2):
                block = cross_ref[jnp.where(swapped, 1 - ab, ab)]
                near_ref[side, ab] = block
                halo_ref[side, ab] = block.astype(f32)

    add_sums(n, z_ref, halo_ref, out_ref, True)


def middle_kernel(n, size, z_ref, near_ref, parts_ref, levels_ref, b_even_ref, b_odd_ref, meta_ref, phase_ref,
                  b_up_ref, b_down_ref, x_out, parts_out, e_ref, far_meta_ref, far_ref, z2_ref, halo2_ref, halo_ref):
    fl, q = z_ref.shape[3], z_ref.shape[4] // 2
    halo_ref[...] = near_ref[...].astype(f32)
    g = lax.axis_index("g")
    marks = seams(n)

    def spectra_of(ab, rows, half):
        blocks = blocks_of(z_ref, halo_ref, ab, rows, half, q, True)
        for w in range(5):
            yield dft8(windowed(blocks[w], blocks[w + 1], seam_scale(marks, ab, w, True)), 1)

    shrink_windows(n, size, spectra_of, parts_ref, levels_ref, e_ref, True)
    lanes = []
    for side, ref in enumerate((b_up_ref, b_down_ref)):
        for ab in range(2):
            lanes.append(jnp.where(g == (n - 1 if side else 0), 1 - ab, ab))
            far_meta_ref[2 * side + ab] = ref[lanes[-1], SHOTS_DEV * fl :, :128].astype(f32)
    fill_phases([far_meta_ref[m] for m in range(4)], fl, far_ref)

    def body(i, carry):
        rows = pl.ds(pl.multiple_of(i * 16, 16), 16)
        own = (phase_ref[0, rows, :], phase_ref[1, rows, :])
        far = (far_ref[0, rows, :], far_ref[1, rows, :])
        for ab in range(2):
            for k in range(4):
                side, p = k // 2, k - 1
                if k in (1, 2):
                    b_ref, lane, phase, m, metas = (b_odd_ref if p else b_even_ref), ab, own, 2 * ab + p, meta_ref
                else:
                    b_ref, lane, phase, m, metas = (b_down_ref if side else b_up_ref), lanes[2 * side + ab], far, 2 * side + ab, far_meta_ref

                def emit(t, span, z):
                    if k in (1, 2):
                        z2_ref[ab, p, t, rows, span] = z
                    else:
                        halo2_ref[side, ab, 0, t, rows, span] = z

                def b_of(t, span):
                    at = pl.ds(pl.multiple_of(i * 16 + t * fl, 16), 16)
                    return b_ref[lane, at, span].astype(f32)

                def meta_of(t):
                    return metas[m, 3 * t : 3 * t + 1, :]

                relax(e_ref, ab, k, rows, b_of, meta_of, phase, SHOTS_DEV * m, emit)
        return carry

    lax.fori_loop(0, fl // 16, body, 0)
    add_sums(n, z2_ref, halo2_ref, parts_out, False, x_out)


def last_kernel(n, size, x_ref, parts_ref, levels_ref, table_ref, out_ref, e_ref):
    fl, q2 = x_ref.shape[3], x_ref.shape[4]

    def spectra_of(ab, rows, half):
        for w in range(3):
            yield load(x_ref, (ab, w), rows, half, q2 // 2, 8)

    shrink_windows(n, size, spectra_of, parts_ref, levels_ref, e_ref, False)
    data = e_ref[...].reshape(ROLES * SHOTS_DEV * fl, q2).astype(bf16)
    out = jnp.dot(data, table_ref[0], preferred_element_type=f32)
    out_ref[...] = out.reshape(ROLES, SHOTS_DEV, fl, q2).astype(bf16)


def unpack_kernel(in_ref, out_ref, sems):
    fl, q = in_ref.shape[2], in_ref.shape[3] // 2
    copies = []
    for role in range(ROLES):
        for part in range(2):
            source = in_ref.at[role, :, :, pl.ds(part * q, q)]
            target = out_ref.at[part, :, pl.ds(role * fl, fl), :]
            copies.append(pltpu.make_async_copy(source, target, sems.at[len(copies)]))
            copies[-1].start()
    for copy in copies:
        copy.wait()


def call(kernel, outs, in_specs, scratch=(), out_specs=None):
    return pl.pallas_call(
        kernel,
        out_shape=outs,
        in_specs=in_specs,
        out_specs=jax.tree.map(lambda _: VMEM, outs) if out_specs is None else out_specs,
        scratch_shapes=list(scratch),
        compiler_params=pltpu.CompilerParams(vmem_limit_bytes=24 * 1024 * 1024),
    )


def on_device(n, nf, blended, estimate, partner, delays, levels):
    q, fl = estimate.shape[3], estimate.shape[2] // ROLES
    shape = jax.ShapeDtypeStruct
    block = (SHOTS_DEV, fl, 2 * q)
    side = shape((2, SHOTS_DEV * fl + 16, 2 * q), bf16)
    size = 8 * nf * ROLES * fl * q
    parts_shape = shape((ROLES * nf, 16, 128), f32)
    forward, backward = receiver_tables(q, 1.0, RELAX), receiver_tables(q, -1.0, 1.0)
    before = [(i, (i - 1) % n) for i in range(n)]
    after = [(i, (i + 1) % n) for i in range(n)]

    slabs = 2 * SHOTS_DEV * (2 * q // 128)
    packed = call(
        pack_kernel,
        shape((ROLES, slabs + 1, fl, 128), bf16),
        [HBM] * 4,
        [
            pltpu.SMEM(partner.shape, jnp.int32),
            pltpu.SMEM(delays.shape, jnp.int32),
            pltpu.SemaphoreType.DMA((4 * ROLES * (q // 128),)),
            pltpu.SemaphoreType.DMA((2,)),
        ],
    )(*[pltpu.with_memory_space_constraint(x, pltpu.HBM) for x in (estimate, blended, partner, delays)])
    gathered = lax.all_to_all(packed, GROUP, 0, 0, tiled=True)
    z, meta, phase, zs, b_even, b_odd = call(
        first_kernel,
        (
            shape((2, 2, *block), f32),
            shape((ROLES, 16, 128), f32),
            shape((2, fl, 128), f32),
            shape((2, 2, *block), bf16),
            side,
            side,
        ),
        [VMEM, VMEM],
        [pltpu.VMEM((2, 2, *block), f32)] * 2,
    )(gathered, jnp.asarray(forward))
    row = n // 4
    down = lax.ppermute(zs, "g", [(i, j) for i, j in before if i % row > 0])
    up = lax.ppermute(zs, "g", [(i, j) for i, j in after if j % row > 0])
    ends = [(i, j) for i, j in before if i % row == 0] + [(i, j) for i, j in after if j % row == 0]
    cross = lax.ppermute(zs, "g", ends)
    b_down = lax.ppermute(b_even, "g", before)
    b_up = lax.ppermute(b_odd, "g", after)
    far = pltpu.VMEM((2, 2, 2, *block), f32)
    parts, near = call(
        functools.partial(wide_sums_kernel, n), (parts_shape, shape((2, 2, 2, *block), bf16)), [VMEM] * 4, [far]
    )(z, cross, up, down)
    parts = lax.all_to_all(parts, SUM_GROUP, 0, 0, tiled=True)
    x, parts = call(
        functools.partial(middle_kernel, n, size),
        (shape((2, 3, 8, fl, 2 * q), f32), shape((ROLES * nf, 8, 128), f32)),
        [VMEM] * 3 + [SMEM] + [VMEM] * 6,
        [
            pltpu.VMEM((2, 4, *block), f32),
            pltpu.VMEM((ROLES, 16, 128), f32),
            pltpu.VMEM((2, fl, 128), f32),
            pltpu.VMEM((2, 2, *block), f32),
            pltpu.VMEM((2, 2, 1, *block), f32),
            far,
        ],
    )(z, near, parts, levels, b_even, b_odd, meta, phase, b_up, b_down)
    parts = lax.all_to_all(parts, SUM_GROUP, 0, 0, tiled=True)
    out = call(
        functools.partial(last_kernel, n, size),
        shape((ROLES, *block), bf16),
        [VMEM] * 2 + [SMEM] + [VMEM],
        [pltpu.VMEM((2, 2, *block), f32)],
    )(x, parts, levels, jnp.asarray(backward[:1]))
    out = lax.all_to_all(out, GROUP, 0, 0, tiled=True)
    return call(unpack_kernel, shape(estimate.shape, bf16), [VMEM], [pltpu.SemaphoreType.DMA((2 * ROLES,))], HBM)(out)


def solution(mesh):
    shots, nf = mesh.shape["shot"], mesh.shape["freq"]
    n = shots // 4
    fine = Mesh(mesh.devices.reshape(2, n, 2, nf), ("yh", "g", "h", "f"))
    spec = P(None, ("yh", "g", "h"), "f", None)
    return jax.shard_map(
        functools.partial(on_device, n, nf),
        mesh=fine,
        in_specs=(spec, spec, P(("yh", "g", "h")), P(), P()),
        out_specs=spec,
        check_vma=False,
    )
```
